32 devices in a mesh: gx: 2 (over y), gy: 4 (over z), gz: 4 (over x, core).
Axes of the slice: x: 2, y: 2, z: 4, core: 2. Of those that a mesh axis runs over, the one named last changes fastest.
Arguments:
- source_term: float32 [32, 8, 32, 512], P(None, 'gx', 'gy', 'gz'), may hold values from -16 to 16
- labels: int32 [8, 32, 512], P('gx', 'gy', 'gz'), may hold values from 0 to 5
- conductivity_table: float32 [6], replicated, may hold values from 0.05 to 1
- send_map: int32 [2, 4, 4, 256], P('gx', 'gy', 'gz'), may hold values from -1 to 4095, as said below
- owner_slots: int32 [4096], P(('gx', 'gy', 'gz')), may hold values from 0 to 255, as said below
- sensor_data: float32 [32, 128], replicated, may hold values from -6 to 6
Outputs:
- projections: float32 [3, 128, 4096], P(None, None, ('gx', 'gy', 'gz'))
- gram_blocks: float32 [6, 4096], P(None, ('gx', 'gy', 'gz'))
The draws below stay inside these ranges and needn't reach their ends.
Inputs may be any that keep to these rules, and one draw needn't show every extreme that they name: `send_map`: entries q * 32 to q * 32 + 31 of row (sx, sy, iz) hold, in their first slots, the brick-local voxels (i * 8 + j) * 128 + k of the positions that this brick sends to owner q = ix * 4 + iy of the same iz, and -1 in the others; no voxel appears twice in a row; some brick fills all 32 slots of some owner. `owner_slots`: the 128 entries of owner d = (ix * 4 + iy) * 4 + iz name, each once, exactly the slots src * 32 + slot that the bricks src = sx * 4 + sy with the same iz fill for it.
All inputs are finite; a program needn't handle non-finite values.
Results may differ from the reference program's by a relative error of at most 0.00012.
Values sent between devices are 32-bit elements; how exact they have to be, the bound alone decides.
No kernel may reach another device: no remote copies, remote signals or barrier semaphores. Data moves between devices by JAX's collectives and lax.ppermute only.
A program may use at most 64 MiB of HBM per device.

```python
import math
import jax
import jax.numpy as jnp
from jax import lax

S = 32
TIMES = 128
NLAB = 6
CX = 4
CY = 8
CZ = 128
POS_OWN = 128
CAP = 32
NX = 8
NY = 32
NZ = 512
POSITIONS = 4096
N_GX = 2
N_GY = 4
N_GZ = 4


def draw_source_term(key, part):
    noise = jnp.clip(jax.random.normal(jax.random.fold_in(key, 11), (S, NX, NY, NZ), jnp.float32), -3.0, 3.0)
    xpos = jnp.arange(NX, dtype=jnp.float32)
    ramp = (0.5 + xpos / NX)[None, :, None, None]
    field = noise * ramp
    return jnp.clip(field, -16.0, 16.0)


def draw_labels(key, part):

    def radial(count):
        offsets = 2 * jnp.arange(count, dtype=jnp.int32) - (count - 1)
        return offsets * offsets * 64 // (count * count)
    radius = radial(NX)[:, None, None] + radial(NY)[None, :, None] + radial(NZ)[None, None, :]
    shell = jnp.minimum(radius * NLAB // 193, NLAB - 1)
    jumping = jax.random.randint(jax.random.fold_in(key, 21), (NX, NY, NZ), 0, 3)
    other = jax.random.randint(jax.random.fold_in(key, 22), (NX, NY, NZ), 0, NLAB)
    return jnp.where(jumping == 0, other, shell).astype(jnp.int32)


def position_plan(key):
    peers = N_GX * N_GY
    capacity = 2 * POS_OWN // peers
    cells = CX * CY * CZ
    order_keys = jax.random.split(jax.random.fold_in(key, 31), N_GZ)
    brick_order = jax.vmap(lambda one_key: jax.random.permutation(one_key, peers))(order_keys)
    level = jax.random.randint(jax.random.fold_in(key, 32), (N_GZ, peers // 2, 1), 0, capacity + 1)
    spread = capacity // 4
    jitter = jax.random.randint(jax.random.fold_in(key, 33), (N_GZ, peers // 2, peers), -spread, spread + 1)
    first = jnp.clip(level + jitter, 0, capacity)
    first = first.at[:, 0, 0].set(capacity)
    paired = jnp.stack([first, capacity - first], axis=2).reshape(N_GZ, peers, peers)
    ranking = jnp.argsort(brick_order, axis=1)
    counts = jnp.take_along_axis(paired, ranking[:, :, None], axis=1)
    starts = jnp.cumsum(counts, axis=2) - counts
    slot_range = jnp.arange(capacity, dtype=jnp.int32)
    voxel_keys = jax.random.split(jax.random.fold_in(key, 34), N_GZ * peers)
    voxel_order = jax.vmap(lambda one_key: jax.random.permutation(one_key, cells))(voxel_keys).reshape(N_GZ, peers, cells)
    wanted = (starts[:, :, :, None] + slot_range).reshape(N_GZ, peers, peers * capacity)
    valid = (slot_range < counts[:, :, :, None]).reshape(N_GZ, peers, peers * capacity)
    picked = jnp.take_along_axis(voxel_order, jnp.clip(wanted, 0, cells - 1), axis=2)
    sent = jnp.where(valid, picked, -1)
    send_map = jnp.transpose(sent, (1, 0, 2)).reshape(N_GX, N_GY, N_GZ, peers * capacity)
    arrived = (slot_range < jnp.transpose(counts, (0, 2, 1))[:, :, :, None]).reshape(N_GZ, peers, peers * capacity)
    score_keys = jax.random.split(jax.random.fold_in(key, 35), N_GZ * peers)
    scores = jax.vmap(lambda one_key: jax.random.permutation(one_key, peers * capacity))(score_keys).reshape(N_GZ, peers, peers * capacity)
    ranked = jnp.argsort(jnp.where(arrived, scores, scores + peers * capacity), axis=2)[:, :, :POS_OWN]
    owner_slots = jnp.transpose(ranked, (1, 0, 2)).reshape(-1)
    return (send_map.astype(jnp.int32), owner_slots.astype(jnp.int32))


def draw_send_map(key, part):
    return position_plan(key)[0]


def draw_owner_slots(key, part):
    return position_plan(key)[1]


def bell_draw(rng, shape, scale, limit, kind=jnp.bfloat16):
    drawn = jax.random.normal(rng, shape, jnp.float32) * scale
    return jnp.minimum(jnp.maximum(drawn, -limit), limit).astype(kind)


def setup_inputs(seed: int = 0) -> dict:
    key_list = jax.random.split(jax.random.key(seed), 7)
    source_term = draw_source_term(jax.random.fold_in(key_list[6], 71), 0)
    labels = draw_labels(jax.random.fold_in(key_list[6], 71), 0)
    conductivity_table = jnp.clip(jnp.exp(jax.random.uniform(key_list[2], (NLAB,), jnp.float32, math.log(0.05), math.log(1.0))), 0.05, 1.0)
    send_map = draw_send_map(jax.random.fold_in(key_list[6], 71), 0)
    owner_slots = draw_owner_slots(jax.random.fold_in(key_list[6], 71), 0)
    sensor_data = bell_draw(key_list[5], (S, TIMES), 1.0, 6.0, jnp.float32)
    return {"source_term": source_term, "labels": labels, "conductivity_table": conductivity_table, "send_map": send_map, "owner_slots": owner_slots, "sensor_data": sensor_data}


mass_term = 0.25


def tissue(shifted, table):
    conductivity = jnp.zeros(shifted.shape, table.dtype)
    for tissue_level in range(table.shape[0]):
        conductivity = conductivity + jnp.where(shifted == tissue_level + 1, table[tissue_level], 0.0)
    inside = (shifted > 0).astype(table.dtype)
    return conductivity, inside


def neighbour_slices(dim_index, offset):
    selection = [slice(1, -1), slice(1, -1), slice(1, -1)]
    selection[dim_index] = slice(2, None) if offset > 0 else slice(0, -2)
    return tuple(selection)


def stencil(padded, conductivity, inside):
    leading = (slice(None),) * (padded.ndim - 3)
    middle = (slice(1, -1), slice(1, -1), slice(1, -1))
    centre = padded[leading + middle]
    own_cond = conductivity[middle]
    own_in = inside[middle]
    accumulated = mass_term * centre
    for dim_index in range(3):
        for offset in (-1, 1):
            beside_all = neighbour_slices(dim_index, offset)
            weight = 0.5 * (own_cond + conductivity[beside_all]) * own_in * inside[beside_all]
            accumulated = accumulated + weight * (centre - padded[leading + beside_all])
    return accumulated


def gram_rows(leadfield):
    entry_pairs = ((0, 0), (1, 1), (2, 2), (0, 1), (0, 2), (1, 2))
    return jnp.stack([jnp.sum(leadfield[first] * leadfield[second], axis=0) for first, second in entry_pairs])


def solve_one(source_field, conductivity, inside):
    solution = jnp.zeros_like(source_field)
    residual = source_field
    direction = source_field
    current = jnp.sum(residual * residual)
    for turn_index in range(2):
        applied = stencil(jnp.pad(direction, 1), conductivity, inside)
        step_size = current / jnp.sum(direction * applied)
        solution = solution + step_size * direction
        residual = residual - step_size * applied
        if turn_index == 0:
            following = jnp.sum(residual * residual)
            direction = residual + (following / current) * direction
            current = following
    return solution


def reference(source_term, labels, conductivity_table, send_map, owner_slots, sensor_data):
    shifted = jnp.pad(labels + 1, 1)
    conductivity, inside = tissue(shifted, conductivity_table)
    positions = jnp.arange(POSITIONS, dtype=jnp.int32)
    device = positions // POS_OWN
    owner_x = device // (N_GY * N_GZ)
    owner_y = (device // N_GZ) % N_GY
    owner_z = device % N_GZ
    owner = owner_x * N_GY + owner_y
    source_peer = owner_slots // CAP
    slot_index = owner_slots % CAP
    source_x = source_peer // N_GY
    source_y = source_peer % N_GY
    voxel = send_map[source_x, source_y, owner_z, owner * CAP + slot_index]
    cell_x = source_x * CX + voxel // (CY * CZ) + 1
    cell_y = source_y * CY + (voxel // CZ) % CY + 1
    cell_z = owner_z * CZ + voxel % CZ + 1
    cond_here = conductivity[cell_x, cell_y, cell_z]

    def one_sensor(source_field):
        solution = solve_one(source_field, conductivity, inside)
        padded = jnp.pad(solution, 1)
        along_x = cond_here * ((padded[cell_x + 1, cell_y, cell_z] - padded[cell_x - 1, cell_y, cell_z]) * 0.5)
        along_y = cond_here * ((padded[cell_x, cell_y + 1, cell_z] - padded[cell_x, cell_y - 1, cell_z]) * 0.5)
        along_z = cond_here * ((padded[cell_x, cell_y, cell_z + 1] - padded[cell_x, cell_y, cell_z - 1]) * 0.5)
        return jnp.stack([along_x, along_y, along_z])

    leadfield = jnp.transpose(lax.map(one_sensor, source_term), (1, 0, 2))
    projections = jnp.einsum("csp,st->ctp", leadfield, sensor_data, precision=lax.Precision.HIGHEST)
    return projections, gram_rows(leadfield)
```

```python
import functools

import jax
import jax.numpy as jnp
from jax import lax
from jax.experimental import pallas as pl
from jax.experimental.pallas import tpu as pltpu
from jax.sharding import PartitionSpec as P

mass_term = 0.25
lane_tile = 128
entry_pairs = ((0, 0), (1, 1), (2, 2), (0, 1), (0, 2), (1, 2))


def ring(count, step):
    return [(i, (i + step) % count) for i in range(count)]


def exchange(faces, axis):
    count = lax.axis_size(axis)
    if count == 1:
        return faces[0], faces[1]
    if count == 2:
        swapped = lax.ppermute(faces[0], axis, ring(2, 1))
        return swapped, swapped
    low, high = faces
    return lax.ppermute(high, axis, ring(count, 1)), lax.ppermute(low, axis, ring(count, -1))


def faces_per_axis(count):
    return 1 if count == 2 else 2


def lanes_equal(shape, value):
    return lax.broadcasted_iota(jnp.int32, shape, len(shape) - 1) == value


def neighbour_flags():
    flags = []
    for axis in ("gx", "gy", "gz"):
        index = lax.axis_index(axis)
        flags.append((index > 0, index < lax.axis_size(axis) - 1))
    return flags


def write_faces(dims, field, face_refs, extra=None):
    sensors, size_x, size_y, size_z = dims
    x_refs, y_refs, z_refs = face_refs

    def put(refs, axis, write):
        if len(refs) == 2:
            write(refs[0], 0)
            write(refs[1], 1)
            return
        index = lax.axis_index(axis)

        @pl.when(index == 0)
        def _():
            write(refs[0], 1)

        @pl.when(index != 0)
        def _():
            write(refs[0], 0)

    def write_x(ref, end):
        x = (size_x - 1) * end
        for y in range(size_y):
            ref[y * sensors : (y + 1) * sensors, :] = field(x * size_y + y)
        if extra is not None:
            ref[size_y * sensors : size_y * (sensors + 1), :] = extra[x]

    def write_y(ref, end):
        y = (size_y - 1) * end
        for x in range(size_x):
            ref[x * sensors : (x + 1) * sensors, :] = field(x * size_y + y)
        if extra is not None:
            for x in range(size_x):
                ref[size_x * sensors + x : size_x * sensors + x + 1, :] = extra[x][y : y + 1, :]

    def write_z(ref, end):
        z = (size_z - 1) * end
        lanes = ref.shape[1]
        packed = jnp.zeros((sensors, lanes), jnp.float32)
        for r in range(size_x * size_y):
            packed = jnp.where(lanes_equal(packed.shape, r), field(r)[:, z : z + 1], packed)
        ref[0:sensors, :] = packed
        if extra is not None:
            packed = jnp.zeros((size_y, lanes), jnp.float32)
            for x in range(size_x):
                packed = jnp.where(lanes_equal(packed.shape, x), extra[x][:, z : z + 1], packed)
            ref[sensors : sensors + size_y, :] = packed

    put(x_refs, "gx", write_x)
    put(y_refs, "gy", write_y)
    put(z_refs, "gz", write_z)


def split_refs(refs, counts):
    groups, start = [], 0
    for count in counts:
        groups.append(refs[start : start + count])
        start += count
    return groups


def pack_kernel(dims, counts, source_ref, label_ref, rows_ref, *face_refs):
    sensors, size_x, size_y, size_z = dims
    count = size_x * size_y
    for r in range(count):
        rows_ref[r * sensors : (r + 1) * sensors, :] = source_ref[pl.ds(r, sensors, stride=count), :]
    shifted = [(label_ref[x] + 1).astype(jnp.float32) for x in range(size_x)]
    field = lambda r: rows_ref[r * sensors : (r + 1) * sensors, :]
    write_faces(dims, field, split_refs(face_refs, counts), shifted)


def tissue(shifted, table_ref):
    conductivity = jnp.zeros_like(shifted)
    for level in range(table_ref.shape[0]):
        conductivity = jnp.where(shifted == level + 1, table_ref[level], conductivity)
    return conductivity, (shifted > 0).astype(jnp.float32)


def edge_weight(first, second):
    return 0.5 * (first[0] + second[0]) * first[1] * second[1]


def weights(dims, label_ref, table_ref, halo_refs, weight_ref):
    sensors, size_x, size_y, size_z = dims
    flags = neighbour_flags()
    (x_low, x_high), (y_low, y_high), (z_low, z_high) = halo_refs

    def masked(value, flag):
        return jnp.where(flag, value, 0.0)

    own = [(label_ref[x] + 1).astype(jnp.float32) for x in range(size_x)]
    own_tissue = [tissue(plane, table_ref) for plane in own]
    x_rows = slice(size_y * sensors, size_y * (sensors + 1))
    below = tissue(masked(x_low[x_rows, :], flags[0][0]), table_ref)
    above = tissue(masked(x_high[x_rows, :], flags[0][1]), table_ref)
    planes = [below] + own_tissue + [above]
    across_x = [edge_weight(planes[i], planes[i + 1]) for i in range(size_x + 1)]
    row_index = lax.broadcasted_iota(jnp.int32, (size_y, size_z), 0)
    lane_index = lax.broadcasted_iota(jnp.int32, (size_y, size_z), 1)
    for x in range(size_x):
        y_row = size_x * sensors + x
        shifted = own[x]
        y_before = jnp.where(
            row_index == 0,
            masked(y_low[y_row : y_row + 1, :], flags[1][0]),
            pltpu.roll(shifted, 1, 0),
        )
        y_after = jnp.where(
            row_index == size_y - 1,
            masked(y_high[y_row : y_row + 1, :], flags[1][1]),
            pltpu.roll(shifted, size_y - 1, 0),
        )
        z_rows = slice(sensors, sensors + size_y)
        z_before = jnp.where(
            lane_index == 0,
            masked(z_low[z_rows, x : x + 1], flags[2][0]),
            pltpu.roll(shifted, 1, 1),
        )
        z_after = jnp.where(
            lane_index == size_z - 1,
            masked(z_high[z_rows, x : x + 1], flags[2][1]),
            pltpu.roll(shifted, size_z - 1, 1),
        )
        six = [across_x[x], across_x[x + 1]]
        for beside in (y_before, y_after, z_before, z_after):
            six.append(edge_weight(own_tissue[x], tissue(beside, table_ref)))
        for k, weight in enumerate(six):
            weight_ref[k, x] = weight
        weight_ref[6, x] = mass_term + (six[0] + six[1]) + (six[2] + six[3]) + (six[4] + six[5])
        weight_ref[7, x] = 0.5 * own_tissue[x][0]


def around(dims, rows_ref, halo_refs, r, flags=None):
    sensors, size_x, size_y, size_z = dims
    (x_low, x_high), (y_low, y_high), (z_low, z_high) = halo_refs
    x, y = divmod(r, size_y)

    def keep(value, dim, end):
        return value if flags is None else jnp.where(flags[dim][end], value, 0.0)

    def row(index):
        return rows_ref[index * sensors : (index + 1) * sensors, :]

    def part(ref, index):
        return ref[index * sensors : (index + 1) * sensors, :]

    centre = row(r)
    x_before = row(r - size_y) if x > 0 else keep(part(x_low, y), 0, 0)
    x_after = row(r + size_y) if x < size_x - 1 else keep(part(x_high, y), 0, 1)
    y_before = row(r - 1) if y > 0 else keep(part(y_low, x), 1, 0)
    y_after = row(r + 1) if y < size_y - 1 else keep(part(y_high, x), 1, 1)
    lane_index = lax.broadcasted_iota(jnp.int32, centre.shape, 1)
    z_before = jnp.where(
        lane_index == 0, keep(z_low[0:sensors, r : r + 1], 2, 0), pltpu.roll(centre, 1, 1)
    )
    z_after = jnp.where(
        lane_index == size_z - 1,
        keep(z_high[0:sensors, r : r + 1], 2, 1),
        pltpu.roll(centre, size_z - 1, 1),
    )
    return centre, (x_before, x_after, y_before, y_after, z_before, z_after)


def combine(weight_ref, x, y, centre, beside):
    total = weight_ref[6, x, y : y + 1, :] * centre
    for k, value in enumerate(beside):
        total = total - weight_ref[k, x, y : y + 1, :] * value
    return total


def pair_up(refs):
    return [(refs[2 * i], refs[2 * i + 1]) for i in range(3)]


def apply_kernel(dims, counts, rows_ref, label_ref, table_ref, *refs):
    sensors, size_x, size_y, size_z = dims
    halo_refs = pair_up(refs[:6])
    weight_ref, applied_ref = refs[6:8]
    face_refs = refs[8:]
    weights(dims, label_ref, table_ref, halo_refs, weight_ref)
    for r in range(size_x * size_y):
        x, y = divmod(r, size_y)
        centre, beside = around(dims, rows_ref, halo_refs, r)
        applied_ref[r * sensors : (r + 1) * sensors, :] = combine(weight_ref, x, y, centre, beside)
    field = lambda r: applied_ref[r * sensors : (r + 1) * sensors, :]
    write_faces(dims, field, split_refs(face_refs, counts))


def halves(value):
    high = value.astype(jnp.bfloat16)
    return high, (value - high.astype(jnp.float32)).astype(jnp.bfloat16)


def select_kernel(dims, rows_ref, applied_ref, weight_ref, voxel_ref, *refs):
    sensors, size_x, size_y, size_z = dims
    source_halos = pair_up(refs[:6])
    applied_halos = pair_up(refs[6:12])
    column_ref, moment_ref, chosen_ref, high_ref, low_ref = refs[12:]
    flags = neighbour_flags()
    slots = voxel_ref.shape[0]
    sums = [jnp.zeros((sensors, size_z), jnp.float32) for _ in range(4)]
    lane_index = lax.broadcasted_iota(jnp.int32, (slots, size_z), 1)
    voxel = voxel_ref[...]
    for r in range(size_x * size_y):
        x, y = divmod(r, size_y)
        span = slice(r * size_z, (r + 1) * size_z)
        chosen_ref[:, span] = (lane_index == voxel - r * size_z).astype(jnp.float32).astype(jnp.bfloat16)
        scale = weight_ref[7, x, y : y + 1, :]
        source, source_beside = around(dims, rows_ref, source_halos, r, flags)
        applied, applied_beside = around(dims, applied_ref, applied_halos, r, flags)
        twice = combine(weight_ref, x, y, applied, applied_beside)
        for k, product in enumerate(
            (source * source, source * applied, applied * applied, applied * twice)
        ):
            sums[k] = sums[k] + product
        for part, beside in enumerate((source_beside, applied_beside)):
            for c in range(3):
                high, low = halves(scale * (beside[2 * c + 1] - beside[2 * c]))
                first = (part * 3 + c) * sensors
                high_ref[first : first + sensors, span] = high
                low_ref[first : first + sensors, span] = low
    contract = (((1,), (1,)), ((), ()))
    chosen = chosen_ref[...]
    column_ref[...] = lax.dot_general(
        chosen, high_ref[...], contract, preferred_element_type=jnp.float32
    ) + lax.dot_general(chosen, low_ref[...], contract, preferred_element_type=jnp.float32)
    stacked = jnp.concatenate(sums, axis=0)
    moment_ref[...] = lax.dot_general(
        jnp.ones((8, size_z), jnp.float32),
        stacked,
        contract,
        precision=lax.Precision.HIGHEST,
        preferred_element_type=jnp.float32,
    )


def owner_kernel(sensors, slots_each, received_ref, owned_ref, data_ref, projection_ref, gram_ref):
    total, width = received_ref.shape
    base = 6 * sensors
    extra = width - base
    moment_rows = -(-4 * sensors // extra)
    gathered = jnp.zeros((moment_rows, extra), jnp.float32)
    for source in range(total // slots_each):
        first = source * slots_each
        gathered = gathered + received_ref[first : first + moment_rows, base:width]
    moments = []
    sensor_index = lax.broadcasted_iota(jnp.int32, (sensors, extra), 0)
    lane_index = lax.broadcasted_iota(jnp.int32, (sensors, extra), 1)
    for k in range(4):
        row, offset = divmod(k * sensors, extra)
        picked = jnp.where(lane_index == sensor_index + offset, gathered[row : row + 1, :], 0.0)
        moments.append(jnp.sum(picked, axis=1, keepdims=True))
    moment_zero, moment_one, moment_two, moment_three = moments
    first_step = moment_zero / moment_one
    residue = first_step * first_step * moment_two - moment_zero
    growth = 1.0 + residue / moment_zero
    curvature = (
        growth * growth * moment_one
        - 2.0 * growth * first_step * moment_two
        + first_step * first_step * moment_three
    )
    second_step = residue / curvature
    source_coef = first_step + second_step * growth
    applied_coef = second_step * first_step
    positions = owned_ref.shape[1]
    slot_index = lax.broadcasted_iota(jnp.int32, (total, positions), 0)
    chosen = (slot_index == owned_ref[...]).astype(jnp.float32).astype(jnp.bfloat16)
    high, low = halves(received_ref[:, 0:base])
    contract = (((0,), (0,)), ((), ()))
    owned = lax.dot_general(
        high, chosen, contract, preferred_element_type=jnp.float32
    ) + lax.dot_general(low, chosen, contract, preferred_element_type=jnp.float32)
    lead = []
    for c in range(3):
        source_part = owned[c * sensors : (c + 1) * sensors, :]
        applied_part = owned[(3 + c) * sensors : (4 + c) * sensors, :]
        lead.append(source_coef * source_part - applied_coef * applied_part)
        projection_ref[c] = lax.dot_general(
            data_ref[...],
            lead[c],
            contract,
            precision=lax.Precision.HIGHEST,
            preferred_element_type=jnp.float32,
        )
    for k, (first, second) in enumerate(entry_pairs):
        gram_ref[k : k + 1, :] = jnp.sum(lead[first] * lead[second], axis=0, keepdims=True)


def in_vmem(count):
    return [pl.BlockSpec(memory_space=pltpu.VMEM)] * count


def face_shapes(dims, counts, with_labels):
    sensors, size_x, size_y, size_z = dims
    lanes = -(-size_x * size_y // lane_tile) * lane_tile
    shapes = (
        (size_y * (sensors + with_labels), size_z),
        (size_x * sensors + 8 * with_labels * -(-size_x // 8), size_z),
        (sensors + size_y * with_labels, lanes),
    )
    return [
        jax.ShapeDtypeStruct(shape, jnp.float32)
        for shape, count in zip(shapes, counts)
        for _ in range(count)
    ]


def exchange_all(faces, counts):
    halos = []
    for axis, group in zip(("gx", "gy", "gz"), split_refs(faces, counts)):
        halos.extend(exchange(group, axis))
    return halos


def per_device(source_term, labels, conductivity_table, send_map, owner_slots, sensor_data):
    dims = source_term.shape
    sensors, size_x, size_y, size_z = dims
    rows_count = size_x * size_y
    counts = [faces_per_axis(lax.axis_size(axis)) for axis in ("gx", "gy", "gz")]
    owners = lax.axis_size("gx") * lax.axis_size("gy")
    slots = send_map.size
    slots_each = slots // owners
    times = sensor_data.shape[1]
    positions = owner_slots.shape[0]

    field_shape = jax.ShapeDtypeStruct((rows_count * sensors, size_z), jnp.float32)
    packed = pl.pallas_call(
        functools.partial(pack_kernel, dims, counts),
        out_shape=[field_shape] + face_shapes(dims, counts, 1),
        in_specs=in_vmem(2),
        out_specs=in_vmem(1 + sum(counts)),
        name="pack",
    )(source_term.reshape(sensors * rows_count, size_z), labels)
    rows, faces = packed[0], packed[1:]
    source_halos = exchange_all(faces, counts)

    weight_shape = jax.ShapeDtypeStruct((8, size_x, size_y, size_z), jnp.float32)
    result = pl.pallas_call(
        functools.partial(apply_kernel, dims, counts),
        out_shape=[weight_shape, field_shape] + face_shapes(dims, counts, 0),
        in_specs=in_vmem(2) + [pl.BlockSpec(memory_space=pltpu.SMEM)] + in_vmem(6),
        out_specs=in_vmem(2 + sum(counts)),
        name="apply",
    )(rows, labels, conductivity_table, *source_halos)
    weight, applied, faces = result[0], result[1], result[2:]
    applied_halos = exchange_all(faces, counts)

    base = 6 * sensors
    columns, moment = pl.pallas_call(
        functools.partial(select_kernel, dims),
        out_shape=[
            jax.ShapeDtypeStruct((slots, base), jnp.float32),
            jax.ShapeDtypeStruct((8, 4 * sensors), jnp.float32),
        ],
        in_specs=in_vmem(16),
        out_specs=in_vmem(2),
        scratch_shapes=[
            pltpu.VMEM((slots, rows_count * size_z), jnp.bfloat16),
            pltpu.VMEM((base, rows_count * size_z), jnp.bfloat16),
            pltpu.VMEM((base, rows_count * size_z), jnp.bfloat16),
        ],
        name="choose",
    )(rows, applied, weight, send_map.reshape(slots, 1), *source_halos, *applied_halos)

    depth = lax.axis_size("gz")
    moment = moment + sum(lax.ppermute(moment, "gz", ring(depth, d)) for d in range(1, depth))
    extra = -base % lane_tile
    while slots_each * extra < 4 * sensors:
        extra += lane_tile
    spread = jnp.pad(moment[0], (0, slots_each * extra - 4 * sensors)).reshape(1, slots_each, extra)
    spread = jnp.broadcast_to(spread, (owners, slots_each, extra)).reshape(slots, extra)
    outgoing = jnp.concatenate([columns, spread], axis=1)
    received = lax.all_to_all(
        outgoing.reshape(owners, slots_each, base + extra), ("gx", "gy"), 0, 0, tiled=True
    ).reshape(slots, base + extra)
    return pl.pallas_call(
        functools.partial(owner_kernel, sensors, slots_each),
        out_shape=[
            jax.ShapeDtypeStruct((3, times, positions), jnp.float32),
            jax.ShapeDtypeStruct((6, positions), jnp.float32),
        ],
        in_specs=in_vmem(3),
        out_specs=in_vmem(2),
        name="owner",
    )(received, owner_slots.reshape(1, positions), sensor_data)


def solution(mesh):
    in_specs = (
        P(None, "gx", "gy", "gz"),
        P("gx", "gy", "gz"),
        P(),
        P("gx", "gy", "gz", None),
        P(("gx", "gy", "gz")),
        P(),
    )
    out_specs = (P(None, None, ("gx", "gy", "gz")), P(None, ("gx", "gy", "gz")))
    step = jax.shard_map(
        per_device, mesh=mesh, in_specs=in_specs, out_specs=out_specs, check_vma=False
    )
    return lambda *arguments: tuple(step(*arguments))
```

```python
import functools

import jax
import jax.numpy as jnp
from jax import lax
from jax.experimental import pallas as pl
from jax.experimental.pallas import tpu as pltpu
from jax.sharding import PartitionSpec as P

mass_term = 0.25
lane_tile = 128
vmem_grant = 16 << 20
entry_pairs = ((0, 0), (1, 1), (2, 2), (0, 1), (0, 2), (1, 2))


def ring(count, step):
    return [(i, (i + step) % count) for i in range(count)]


def exchange(faces, axis):
    count = lax.axis_size(axis)
    if count == 1:
        return faces[0], faces[1]
    if count == 2:
        swapped = lax.ppermute(faces[0], axis, ring(2, 1))
        return swapped, swapped
    low, high = faces
    return lax.ppermute(high, axis, ring(count, 1)), lax.ppermute(low, axis, ring(count, -1))


def faces_per_axis(count):
    return 1 if count == 2 else 2


def lanes_equal(shape, value):
    return lax.broadcasted_iota(jnp.int32, shape, len(shape) - 1) == value


def neighbour_flags():
    flags = []
    for axis in ("gx", "gy", "gz"):
        index = lax.axis_index(axis)
        flags.append((index > 0, index < lax.axis_size(axis) - 1))
    return flags


def write_faces(dims, field, face_refs, extra=None):
    sensors, size_x, size_y, size_z = dims
    x_refs, y_refs, z_refs = face_refs

    def put(refs, axis, write):
        if len(refs) == 2:
            write(refs[0], 0)
            write(refs[1], 1)
            return
        index = lax.axis_index(axis)

        @pl.when(index == 0)
        def _():
            write(refs[0], 1)

        @pl.when(index != 0)
        def _():
            write(refs[0], 0)

    def write_x(ref, end):
        x = (size_x - 1) * end
        for y in range(size_y):
            ref[y * sensors : (y + 1) * sensors, :] = field(x * size_y + y)
        if extra is not None:
            ref[size_y * sensors : size_y * (sensors + 1), :] = extra[x]

    def write_y(ref, end):
        y = (size_y - 1) * end
        for x in range(size_x):
            ref[x * sensors : (x + 1) * sensors, :] = field(x * size_y + y)
        if extra is not None:
            for x in range(size_x):
                ref[size_x * sensors + x : size_x * sensors + x + 1, :] = extra[x][y : y + 1, :]

    def write_z(ref, end):
        z = (size_z - 1) * end
        lanes = ref.shape[1]
        packed = jnp.zeros((sensors, lanes), jnp.float32)
        for r in range(size_x * size_y):
            packed = jnp.where(lanes_equal(packed.shape, r), field(r)[:, z : z + 1], packed)
        ref[0:sensors, :] = packed
        if extra is not None:
            packed = jnp.zeros((size_y, lanes), jnp.float32)
            for x in range(size_x):
                packed = jnp.where(lanes_equal(packed.shape, x), extra[x][:, z : z + 1], packed)
            ref[sensors : sensors + size_y, :] = packed

    put(x_refs, "gx", write_x)
    put(y_refs, "gy", write_y)
    put(z_refs, "gz", write_z)


def split_refs(refs, counts):
    groups, start = [], 0
    for count in counts:
        groups.append(refs[start : start + count])
        start += count
    return groups


def pack_kernel(dims, counts, source_ref, label_ref, rows_ref, *face_refs):
    sensors, size_x, size_y, size_z = dims
    count = size_x * size_y
    for r in range(count):
        rows_ref[r * sensors : (r + 1) * sensors, :] = source_ref[pl.ds(r, sensors, stride=count), :]
    shifted = [(label_ref[x] + 1).astype(jnp.float32) for x in range(size_x)]
    field = lambda r: rows_ref[r * sensors : (r + 1) * sensors, :]
    write_faces(dims, field, split_refs(face_refs, counts), shifted)


def tissue(shifted, table_ref):
    conductivity = jnp.zeros_like(shifted)
    for level in range(table_ref.shape[0]):
        conductivity = jnp.where(shifted == level + 1, table_ref[level], conductivity)
    return conductivity, (shifted > 0).astype(jnp.float32)


def edge_weight(first, second):
    return 0.5 * (first[0] + second[0]) * first[1] * second[1]


def weights(dims, label_ref, table_ref, halo_refs, weight_ref):
    sensors, size_x, size_y, size_z = dims
    flags = neighbour_flags()
    (x_low, x_high), (y_low, y_high), (z_low, z_high) = halo_refs

    def masked(value, flag):
        return jnp.where(flag, value, 0.0)

    own = [(label_ref[x] + 1).astype(jnp.float32) for x in range(size_x)]
    own_tissue = [tissue(plane, table_ref) for plane in own]
    x_rows = slice(size_y * sensors, size_y * (sensors + 1))
    below = tissue(masked(x_low[x_rows, :], flags[0][0]), table_ref)
    above = tissue(masked(x_high[x_rows, :], flags[0][1]), table_ref)
    planes = [below] + own_tissue + [above]
    across_x = [edge_weight(planes[i], planes[i + 1]) for i in range(size_x + 1)]
    row_index = lax.broadcasted_iota(jnp.int32, (size_y, size_z), 0)
    lane_index = lax.broadcasted_iota(jnp.int32, (size_y, size_z), 1)
    for x in range(size_x):
        y_row = size_x * sensors + x
        shifted = own[x]
        y_before = jnp.where(
            row_index == 0,
            masked(y_low[y_row : y_row + 1, :], flags[1][0]),
            pltpu.roll(shifted, 1, 0),
        )
        y_after = jnp.where(
            row_index == size_y - 1,
            masked(y_high[y_row : y_row + 1, :], flags[1][1]),
            pltpu.roll(shifted, size_y - 1, 0),
        )
        z_rows = slice(sensors, sensors + size_y)
        z_before = jnp.where(
            lane_index == 0,
            masked(z_low[z_rows, x : x + 1], flags[2][0]),
            pltpu.roll(shifted, 1, 1),
        )
        z_after = jnp.where(
            lane_index == size_z - 1,
            masked(z_high[z_rows, x : x + 1], flags[2][1]),
            pltpu.roll(shifted, size_z - 1, 1),
        )
        six = [across_x[x], across_x[x + 1]]
        for beside in (y_before, y_after, z_before, z_after):
            six.append(edge_weight(own_tissue[x], tissue(beside, table_ref)))
        for k, weight in enumerate(six):
            weight_ref[k, x] = weight
        weight_ref[6, x] = mass_term + (six[0] + six[1]) + (six[2] + six[3]) + (six[4] + six[5])
        weight_ref[7, x] = 0.5 * own_tissue[x][0]


def around(dims, rows_ref, halo_refs, r, flags=None):
    sensors, size_x, size_y, size_z = dims
    (x_low, x_high), (y_low, y_high), (z_low, z_high) = halo_refs
    x, y = divmod(r, size_y)

    def keep(value, dim, end):
        return value if flags is None else jnp.where(flags[dim][end], value, 0.0)

    def row(index):
        return rows_ref[index * sensors : (index + 1) * sensors, :]

    def part(ref, index):
        return ref[index * sensors : (index + 1) * sensors, :]

    centre = row(r)
    x_before = row(r - size_y) if x > 0 else keep(part(x_low, y), 0, 0)
    x_after = row(r + size_y) if x < size_x - 1 else keep(part(x_high, y), 0, 1)
    y_before = row(r - 1) if y > 0 else keep(part(y_low, x), 1, 0)
    y_after = row(r + 1) if y < size_y - 1 else keep(part(y_high, x), 1, 1)
    lane_index = lax.broadcasted_iota(jnp.int32, centre.shape, 1)
    z_before = jnp.where(
        lane_index == 0, keep(z_low[0:sensors, r : r + 1], 2, 0), pltpu.roll(centre, 1, 1)
    )
    z_after = jnp.where(
        lane_index == size_z - 1,
        keep(z_high[0:sensors, r : r + 1], 2, 1),
        pltpu.roll(centre, size_z - 1, 1),
    )
    return centre, (x_before, x_after, y_before, y_after, z_before, z_after)


def combine(weight_ref, x, y, centre, beside):
    total = weight_ref[6, x, y : y + 1, :] * centre
    for k, value in enumerate(beside):
        total = total - weight_ref[k, x, y : y + 1, :] * value
    return total


def pair_up(refs):
    return [(refs[2 * i], refs[2 * i + 1]) for i in range(3)]


def apply_kernel(dims, counts, rows_ref, label_ref, table_ref, *refs):
    sensors, size_x, size_y, size_z = dims
    halo_refs = pair_up(refs[:6])
    weight_ref, applied_ref = refs[6:8]
    face_refs = refs[8:]
    weights(dims, label_ref, table_ref, halo_refs, weight_ref)
    for r in range(size_x * size_y):
        x, y = divmod(r, size_y)
        centre, beside = around(dims, rows_ref, halo_refs, r)
        applied_ref[r * sensors : (r + 1) * sensors, :] = combine(weight_ref, x, y, centre, beside)
    field = lambda r: applied_ref[r * sensors : (r + 1) * sensors, :]
    write_faces(dims, field, split_refs(face_refs, counts))


def halves(value):
    high = value.astype(jnp.bfloat16)
    return high, (value - high.astype(jnp.float32)).astype(jnp.bfloat16)


def select_kernel(dims, rows_ref, applied_ref, weight_ref, voxel_ref, *refs):
    sensors, size_x, size_y, size_z = dims
    source_halos = pair_up(refs[:6])
    applied_halos = pair_up(refs[6:12])
    column_ref, moment_ref, chosen_ref, high_ref, low_ref = refs[12:]
    flags = neighbour_flags()
    slots = voxel_ref.shape[0]
    sums = [jnp.zeros((sensors, size_z), jnp.float32) for _ in range(4)]
    lane_index = lax.broadcasted_iota(jnp.int32, (slots, size_z), 1)
    voxel = voxel_ref[...]
    for r in range(size_x * size_y):
        x, y = divmod(r, size_y)
        span = slice(r * size_z, (r + 1) * size_z)
        chosen_ref[:, span] = (lane_index == voxel - r * size_z).astype(jnp.float32).astype(jnp.bfloat16)
        scale = weight_ref[7, x, y : y + 1, :]
        source, source_beside = around(dims, rows_ref, source_halos, r, flags)
        applied, applied_beside = around(dims, applied_ref, applied_halos, r, flags)
        twice = combine(weight_ref, x, y, applied, applied_beside)
        for k, product in enumerate(
            (source * source, source * applied, applied * applied, applied * twice)
        ):
            sums[k] = sums[k] + product
        for part, beside in enumerate((source_beside, applied_beside)):
            for c in range(3):
                high, low = halves(scale * (beside[2 * c + 1] - beside[2 * c]))
                first = (part * 3 + c) * sensors
                high_ref[first : first + sensors, span] = high
                low_ref[first : first + sensors, span] = low
    contract = (((1,), (1,)), ((), ()))
    chosen = chosen_ref[...]
    column_ref[...] = lax.dot_general(
        chosen, high_ref[...], contract, preferred_element_type=jnp.float32
    ) + lax.dot_general(chosen, low_ref[...], contract, preferred_element_type=jnp.float32)
    stacked = jnp.concatenate(sums, axis=0)
    moment_ref[...] = lax.dot_general(
        jnp.ones((8, size_z), jnp.float32),
        stacked,
        contract,
        precision=lax.Precision.HIGHEST,
        preferred_element_type=jnp.float32,
    )


def owner_kernel(sensors, slots_each, received_ref, owned_ref, data_ref, projection_ref, gram_ref):
    total, width = received_ref.shape
    base = 6 * sensors
    extra = width - base
    moment_rows = -(-4 * sensors // extra)
    gathered = jnp.zeros((moment_rows, extra), jnp.float32)
    for source in range(total // slots_each):
        first = source * slots_each
        gathered = gathered + received_ref[first : first + moment_rows, base:width]
    moments = []
    sensor_index = lax.broadcasted_iota(jnp.int32, (sensors, extra), 0)
    lane_index = lax.broadcasted_iota(jnp.int32, (sensors, extra), 1)
    for k in range(4):
        row, offset = divmod(k * sensors, extra)
        picked = jnp.where(lane_index == sensor_index + offset, gathered[row : row + 1, :], 0.0)
        moments.append(jnp.sum(picked, axis=1, keepdims=True))
    moment_zero, moment_one, moment_two, moment_three = moments
    first_step = moment_zero / moment_one
    residue = first_step * first_step * moment_two - moment_zero
    growth = 1.0 + residue / moment_zero
    curvature = (
        growth * growth * moment_one
        - 2.0 * growth * first_step * moment_two
        + first_step * first_step * moment_three
    )
    second_step = residue / curvature
    source_coef = first_step + second_step * growth
    applied_coef = second_step * first_step
    positions = owned_ref.shape[1]
    slot_index = lax.broadcasted_iota(jnp.int32, (total, positions), 0)
    chosen = (slot_index == owned_ref[...]).astype(jnp.float32).astype(jnp.bfloat16)
    high, low = halves(received_ref[:, 0:base])
    contract = (((0,), (0,)), ((), ()))
    owned = lax.dot_general(
        high, chosen, contract, preferred_element_type=jnp.float32
    ) + lax.dot_general(low, chosen, contract, preferred_element_type=jnp.float32)
    lead = []
    for c in range(3):
        source_part = owned[c * sensors : (c + 1) * sensors, :]
        applied_part = owned[(3 + c) * sensors : (4 + c) * sensors, :]
        lead.append(source_coef * source_part - applied_coef * applied_part)
        projection_ref[c] = lax.dot_general(
            data_ref[...],
            lead[c],
            contract,
            precision=lax.Precision.HIGHEST,
            preferred_element_type=jnp.float32,
        )
    for k, (first, second) in enumerate(entry_pairs):
        gram_ref[k : k + 1, :] = jnp.sum(lead[first] * lead[second], axis=0, keepdims=True)


def call(body, **arguments):
    return pl.pallas_call(
        body, compiler_params=pltpu.CompilerParams(vmem_limit_bytes=vmem_grant), **arguments
    )


def in_vmem(count):
    return [pl.BlockSpec(memory_space=pltpu.VMEM)] * count


def face_shapes(dims, counts, with_labels):
    sensors, size_x, size_y, size_z = dims
    lanes = -(-size_x * size_y // lane_tile) * lane_tile
    shapes = (
        (size_y * (sensors + with_labels), size_z),
        (size_x * sensors + 8 * with_labels * -(-size_x // 8), size_z),
        (sensors + size_y * with_labels, lanes),
    )
    return [
        jax.ShapeDtypeStruct(shape, jnp.float32)
        for shape, count in zip(shapes, counts)
        for _ in range(count)
    ]


def exchange_all(faces, counts):
    halos = []
    for axis, group in zip(("gx", "gy", "gz"), split_refs(faces, counts)):
        halos.extend(exchange(group, axis))
    return halos


def per_device(source_term, labels, conductivity_table, send_map, owner_slots, sensor_data):
    dims = source_term.shape
    sensors, size_x, size_y, size_z = dims
    rows_count = size_x * size_y
    counts = [faces_per_axis(lax.axis_size(axis)) for axis in ("gx", "gy", "gz")]
    owners = lax.axis_size("gx") * lax.axis_size("gy")
    slots = send_map.size
    slots_each = slots // owners
    times = sensor_data.shape[1]
    positions = owner_slots.shape[0]

    field_shape = jax.ShapeDtypeStruct((rows_count * sensors, size_z), jnp.float32)
    packed = call(
        functools.partial(pack_kernel, dims, counts),
        out_shape=[field_shape] + face_shapes(dims, counts, 1),
        in_specs=in_vmem(2),
        out_specs=in_vmem(1 + sum(counts)),
        name="pack",
    )(source_term.reshape(sensors * rows_count, size_z), labels)
    rows, faces = packed[0], packed[1:]
    source_halos = exchange_all(faces, counts)

    weight_shape = jax.ShapeDtypeStruct((8, size_x, size_y, size_z), jnp.float32)
    result = call(
        functools.partial(apply_kernel, dims, counts),
        out_shape=[weight_shape, field_shape] + face_shapes(dims, counts, 0),
        in_specs=in_vmem(2) + [pl.BlockSpec(memory_space=pltpu.SMEM)] + in_vmem(6),
        out_specs=in_vmem(2 + sum(counts)),
        name="apply",
    )(rows, labels, conductivity_table, *source_halos)
    weight, applied, faces = result[0], result[1], result[2:]
    applied_halos = exchange_all(faces, counts)

    base = 6 * sensors
    columns, moment = call(
        functools.partial(select_kernel, dims),
        out_shape=[
            jax.ShapeDtypeStruct((slots, base), jnp.float32),
            jax.ShapeDtypeStruct((8, 4 * sensors), jnp.float32),
        ],
        in_specs=in_vmem(16),
        out_specs=in_vmem(2),
        scratch_shapes=[
            pltpu.VMEM((slots, rows_count * size_z), jnp.bfloat16),
            pltpu.VMEM((base, rows_count * size_z), jnp.bfloat16),
            pltpu.VMEM((base, rows_count * size_z), jnp.bfloat16),
        ],
        name="choose",
    )(rows, applied, weight, send_map.reshape(slots, 1), *source_halos, *applied_halos)

    depth = lax.axis_size("gz")
    moment = moment + sum(lax.ppermute(moment, "gz", ring(depth, d)) for d in range(1, depth))
    extra = -base % lane_tile
    while slots_each * extra < 4 * sensors:
        extra += lane_tile
    spread = jnp.pad(moment[0], (0, slots_each * extra - 4 * sensors)).reshape(1, slots_each, extra)
    spread = jnp.broadcast_to(spread, (owners, slots_each, extra)).reshape(slots, extra)
    outgoing = jnp.concatenate([columns, spread], axis=1)
    received = lax.all_to_all(
        outgoing.reshape(owners, slots_each, base + extra), ("gx", "gy"), 0, 0, tiled=True
    ).reshape(slots, base + extra)
    return call(
        functools.partial(owner_kernel, sensors, slots_each),
        out_shape=[
            jax.ShapeDtypeStruct((3, times, positions), jnp.float32),
            jax.ShapeDtypeStruct((6, positions), jnp.float32),
        ],
        in_specs=in_vmem(3),
        out_specs=in_vmem(2),
        name="owner",
    )(received, owner_slots.reshape(1, positions), sensor_data)


def solution(mesh):
    in_specs = (
        P(None, "gx", "gy", "gz"),
        P("gx", "gy", "gz"),
        P(),
        P("gx", "gy", "gz", None),
        P(("gx", "gy", "gz")),
        P(),
    )
    out_specs = (P(None, None, ("gx", "gy", "gz")), P(None, ("gx", "gy", "gz")))
    step = jax.shard_map(
        per_device, mesh=mesh, in_specs=in_specs, out_specs=out_specs, check_vma=False
    )
    return lambda *arguments: tuple(step(*arguments))
```

```python
import functools

import jax
import jax.numpy as jnp
from jax import lax
from jax.experimental import pallas as pl
from jax.experimental.pallas import tpu as pltpu
from jax.sharding import PartitionSpec as P

mass_term = 0.25
lane_tile = 128
vmem_grant = 16 << 20
last_with_last = (((1,), (1,)), ((), ()))
entry_pairs = ((0, 0), (1, 1), (2, 2), (0, 1), (0, 2), (1, 2))


def ring(count, step):
    return [(i, (i + step) % count) for i in range(count)]


def exchange(faces, axis):
    count = lax.axis_size(axis)
    if count == 1:
        return faces[0], faces[1]
    if count == 2:
        swapped = lax.ppermute(faces[0], axis, ring(2, 1))
        return swapped, swapped
    low, high = faces
    return lax.ppermute(high, axis, ring(count, 1)), lax.ppermute(low, axis, ring(count, -1))


def faces_per_axis(count):
    return 1 if count == 2 else 2


def lanes_equal(shape, value):
    return lax.broadcasted_iota(jnp.int32, shape, len(shape) - 1) == value


def neighbour_flags():
    flags = []
    for axis in ("gx", "gy", "gz"):
        index = lax.axis_index(axis)
        flags.append((index > 0, index < lax.axis_size(axis) - 1))
    return flags


def write_faces(dims, field, face_refs, extra=None):
    sensors, size_x, size_y, size_z = dims
    x_refs, y_refs, z_refs = face_refs

    def put(refs, axis, write):
        if len(refs) == 2:
            write(refs[0], 0)
            write(refs[1], 1)
            return
        index = lax.axis_index(axis)

        @pl.when(index == 0)
        def _():
            write(refs[0], 1)

        @pl.when(index != 0)
        def _():
            write(refs[0], 0)

    def write_x(ref, end):
        x = (size_x - 1) * end
        for y in range(size_y):
            ref[y * sensors : (y + 1) * sensors, :] = field(x * size_y + y)
        if extra is not None:
            ref[size_y * sensors : size_y * (sensors + 1), :] = extra[x]

    def write_y(ref, end):
        y = (size_y - 1) * end
        for x in range(size_x):
            ref[x * sensors : (x + 1) * sensors, :] = field(x * size_y + y)
        if extra is not None:
            for x in range(size_x):
                ref[size_x * sensors + x : size_x * sensors + x + 1, :] = extra[x][y : y + 1, :]

    def write_z(ref, end):
        z = (size_z - 1) * end
        lanes = ref.shape[1]
        packed = jnp.zeros((sensors, lanes), jnp.float32)
        for r in range(size_x * size_y):
            packed = jnp.where(lanes_equal(packed.shape, r), field(r)[:, z : z + 1], packed)
        ref[0:sensors, :] = packed
        if extra is not None:
            packed = jnp.zeros((size_y, lanes), jnp.float32)
            for x in range(size_x):
                packed = jnp.where(lanes_equal(packed.shape, x), extra[x][:, z : z + 1], packed)
            ref[sensors : sensors + size_y, :] = packed

    put(x_refs, "gx", write_x)
    put(y_refs, "gy", write_y)
    put(z_refs, "gz", write_z)


def split_refs(refs, counts):
    groups, start = [], 0
    for count in counts:
        groups.append(refs[start : start + count])
        start += count
    return groups


def pack_kernel(dims, counts, source_ref, label_ref, rows_ref, shifted_ref, *refs):
    sensors, size_x, size_y, size_z = dims
    face_refs, (staged_ref, label_vmem, semaphores) = refs[:-3], refs[-3:]
    copies = [
        pltpu.make_async_copy(source_ref.at[:, x], staged_ref.at[x], semaphores.at[x])
        for x in range(size_x)
    ]
    copies.append(pltpu.make_async_copy(label_ref, label_vmem, semaphores.at[size_x]))
    for copy in copies:
        copy.start()
    flat = staged_ref.reshape(size_x, sensors * size_y, size_z)
    for x in range(size_x):
        copies[x].wait()
        for y in range(size_y):
            r = x * size_y + y
            rows_ref[r * sensors : (r + 1) * sensors, :] = flat[x, pl.ds(y, sensors, stride=size_y), :]
    copies[size_x].wait()
    shifted = [(label_vmem[x] + 1).astype(jnp.float32) for x in range(size_x)]
    for x in range(size_x):
        shifted_ref[x] = shifted[x]
    field = lambda r: rows_ref[r * sensors : (r + 1) * sensors, :]
    write_faces(dims, field, split_refs(face_refs, counts), shifted)


def prepare_kernel(
    size_z,
    voxel_hbm,
    owned_hbm,
    data_hbm,
    table_hbm,
    chosen_ref,
    owned_chosen_ref,
    held_ref,
    table_ref,
    voxel_ref,
    owned_ref,
    level_ref,
    semaphores,
):
    moves = (
        (voxel_hbm, voxel_ref),
        (owned_hbm, owned_ref),
        (data_hbm, held_ref),
        (table_hbm, level_ref),
    )
    copies = [pltpu.make_async_copy(*move, semaphores.at[k]) for k, move in enumerate(moves)]
    for copy in copies:
        copy.start()
    for copy in copies:
        copy.wait()
    for level in range(level_ref.shape[0]):
        table_ref[level] = jnp.full(table_ref.shape[1:], level_ref[level], jnp.float32)
    slots, voxels = chosen_ref.shape
    square = (slots, slots)
    diagonal = lanes_equal(square, lax.broadcasted_iota(jnp.int32, square, 0))
    voxel = jnp.where(diagonal, voxel_ref[...].astype(jnp.float32), 0.0)
    voxel = jnp.sum(voxel, axis=1, keepdims=True).astype(jnp.int32)
    voxel = jnp.broadcast_to(voxel, (slots, size_z))
    lane_index = lax.broadcasted_iota(jnp.int32, (slots, size_z), 1)
    for first in range(0, voxels, size_z):
        chosen_ref[:, first : first + size_z] = one_hot(lane_index == voxel - first)
    slot_index = lax.broadcasted_iota(jnp.int32, owned_chosen_ref.shape, 0)
    owned_chosen_ref[...] = one_hot(slot_index == owned_ref[...])


def one_hot(condition):
    return condition.astype(jnp.float32).astype(jnp.bfloat16)


def tissue(shifted, table_ref):
    conductivity = jnp.zeros_like(shifted)
    for level in range(table_ref.shape[0]):
        conductivity = jnp.where(shifted == level + 1, table_ref[level], conductivity)
    return conductivity, (shifted > 0).astype(jnp.float32)


def edge_weight(first, second):
    return 0.5 * (first[0] + second[0]) * first[1] * second[1]


def weights(dims, shifted_ref, table_ref, halo_refs, weight_ref):
    sensors, size_x, size_y, size_z = dims
    flags = neighbour_flags()
    (x_low, x_high), (y_low, y_high), (z_low, z_high) = halo_refs

    def masked(value, flag):
        return jnp.where(flag, value, 0.0)

    own = [shifted_ref[x] for x in range(size_x)]
    own_tissue = [tissue(plane, table_ref) for plane in own]
    x_rows = slice(size_y * sensors, size_y * (sensors + 1))
    below = tissue(masked(x_low[x_rows, :], flags[0][0]), table_ref)
    above = tissue(masked(x_high[x_rows, :], flags[0][1]), table_ref)
    planes = [below] + own_tissue + [above]
    across_x = [edge_weight(planes[i], planes[i + 1]) for i in range(size_x + 1)]
    row_index = lax.broadcasted_iota(jnp.int32, (size_y, size_z), 0)
    lane_index = lax.broadcasted_iota(jnp.int32, (size_y, size_z), 1)
    for x in range(size_x):
        y_row = size_x * sensors + x
        shifted = own[x]
        y_before = jnp.where(
            row_index == 0,
            masked(y_low[y_row : y_row + 1, :], flags[1][0]),
            pltpu.roll(shifted, 1, 0),
        )
        y_after = jnp.where(
            row_index == size_y - 1,
            masked(y_high[y_row : y_row + 1, :], flags[1][1]),
            pltpu.roll(shifted, size_y - 1, 0),
        )
        z_rows = slice(sensors, sensors + size_y)
        z_before = jnp.where(
            lane_index == 0,
            masked(z_low[z_rows, x : x + 1], flags[2][0]),
            pltpu.roll(shifted, 1, 1),
        )
        z_after = jnp.where(
            lane_index == size_z - 1,
            masked(z_high[z_rows, x : x + 1], flags[2][1]),
            pltpu.roll(shifted, size_z - 1, 1),
        )
        six = [across_x[x], across_x[x + 1]]
        for beside in (y_before, y_after, z_before, z_after):
            six.append(edge_weight(own_tissue[x], tissue(beside, table_ref)))
        for k, weight in enumerate(six):
            weight_ref[k, x] = weight
        weight_ref[6, x] = mass_term + (six[0] + six[1]) + (six[2] + six[3]) + (six[4] + six[5])
        weight_ref[7, x] = 0.5 * own_tissue[x][0]


def around(dims, rows_ref, halo_refs, r, flags=None):
    sensors, size_x, size_y, size_z = dims
    (x_low, x_high), (y_low, y_high), (z_low, z_high) = halo_refs
    x, y = divmod(r, size_y)

    def keep(value, dim, end):
        return value if flags is None else jnp.where(flags[dim][end], value, 0.0)

    def row(index):
        return rows_ref[index * sensors : (index + 1) * sensors, :]

    def part(ref, index):
        return ref[index * sensors : (index + 1) * sensors, :]

    centre = row(r)
    x_before = row(r - size_y) if x > 0 else keep(part(x_low, y), 0, 0)
    x_after = row(r + size_y) if x < size_x - 1 else keep(part(x_high, y), 0, 1)
    y_before = row(r - 1) if y > 0 else keep(part(y_low, x), 1, 0)
    y_after = row(r + 1) if y < size_y - 1 else keep(part(y_high, x), 1, 1)
    lane_index = lax.broadcasted_iota(jnp.int32, centre.shape, 1)
    z_before = jnp.where(
        lane_index == 0, keep(z_low[0:sensors, r : r + 1], 2, 0), pltpu.roll(centre, 1, 1)
    )
    z_after = jnp.where(
        lane_index == size_z - 1,
        keep(z_high[0:sensors, r : r + 1], 2, 1),
        pltpu.roll(centre, size_z - 1, 1),
    )
    return centre, (x_before, x_after, y_before, y_after, z_before, z_after)


def combine(weight_ref, x, y, centre, beside):
    total = weight_ref[6, x, y : y + 1, :] * centre
    for k, value in enumerate(beside):
        total = total - weight_ref[k, x, y : y + 1, :] * value
    return total


def pair_up(refs):
    return [(refs[2 * i], refs[2 * i + 1]) for i in range(3)]


def apply_kernel(dims, counts, rows_ref, shifted_ref, table_ref, *refs):
    sensors, size_x, size_y, size_z = dims
    halo_refs = pair_up(refs[:6])
    weight_ref, applied_ref = refs[6:8]
    face_refs = refs[8:]
    weights(dims, shifted_ref, table_ref, halo_refs, weight_ref)
    for r in range(size_x * size_y):
        x, y = divmod(r, size_y)
        centre, beside = around(dims, rows_ref, halo_refs, r)
        applied_ref[r * sensors : (r + 1) * sensors, :] = combine(weight_ref, x, y, centre, beside)
    field = lambda r: applied_ref[r * sensors : (r + 1) * sensors, :]
    write_faces(dims, field, split_refs(face_refs, counts))


def halves(value):
    high = value.astype(jnp.bfloat16)
    return high, (value - high.astype(jnp.float32)).astype(jnp.bfloat16)


def local_twice(dims, rows_ref, weight_ref, r):
    sensors, size_x, size_y, size_z = dims
    x, y = divmod(r, size_y)

    def row(index):
        return rows_ref[index * sensors : (index + 1) * sensors, :]

    def weight(k):
        return weight_ref[k, x, y : y + 1, :]

    centre = row(r)
    lane_index = lax.broadcasted_iota(jnp.int32, centre.shape, 1)
    total = weight(6) * centre
    if x > 0:
        total = total - weight(0) * row(r - size_y)
    if x < size_x - 1:
        total = total - weight(1) * row(r + size_y)
    if y > 0:
        total = total - weight(2) * row(r - 1)
    if y < size_y - 1:
        total = total - weight(3) * row(r + 1)
    before = jnp.where(lane_index == 0, 0.0, pltpu.roll(centre, 1, 1))
    after = jnp.where(lane_index == size_z - 1, 0.0, pltpu.roll(centre, size_z - 1, 1))
    return total - weight(4) * before - weight(5) * after


def select_columns(dims, rows_ref, weight_ref, halo_refs, chosen_ref, high_ref, low_ref):
    sensors, size_x, size_y, size_z = dims
    flags = neighbour_flags()
    for r in range(size_x * size_y):
        x, y = divmod(r, size_y)
        span = slice(r * size_z, (r + 1) * size_z)
        scale = weight_ref[7, x, y : y + 1, :]
        _, beside = around(dims, rows_ref, halo_refs, r, flags)
        for c in range(3):
            high, low = halves(scale * (beside[2 * c + 1] - beside[2 * c]))
            high_ref[c * sensors : (c + 1) * sensors, span] = high
            low_ref[c * sensors : (c + 1) * sensors, span] = low
    chosen = chosen_ref[...]
    return lax.dot_general(
        chosen, high_ref[...], last_with_last, preferred_element_type=jnp.float32
    ) + lax.dot_general(chosen, low_ref[...], last_with_last, preferred_element_type=jnp.float32)


def source_kernel(dims, rows_ref, applied_ref, weight_ref, chosen_ref, *refs):
    sensors, size_x, size_y, size_z = dims
    halo_refs = pair_up(refs[:6])
    column_ref, sum_ref, high_ref, low_ref = refs[6:]
    sums = [jnp.zeros((sensors, size_z), jnp.float32) for _ in range(4)]
    for r in range(size_x * size_y):
        source = rows_ref[r * sensors : (r + 1) * sensors, :]
        applied = applied_ref[r * sensors : (r + 1) * sensors, :]
        twice = local_twice(dims, applied_ref, weight_ref, r)
        for k, product in enumerate(
            (source * source, source * applied, applied * applied, applied * twice)
        ):
            sums[k] = sums[k] + product
    for k in range(4):
        sum_ref[k * sensors : (k + 1) * sensors, :] = sums[k]
    column_ref[...] = select_columns(
        dims, rows_ref, weight_ref, halo_refs, chosen_ref, high_ref, low_ref
    )


def moment_kernel(dims, applied_ref, weight_ref, sum_ref, *refs):
    sensors, size_x, size_y, size_z = dims
    (x_low, x_high), (y_low, y_high), (z_low, z_high) = pair_up(refs[:6])
    moment_ref = refs[6]

    def part(ref, index):
        return ref[index * sensors : (index + 1) * sensors, :]

    def crossing(k, r, beside):
        x, y = divmod(r, size_y)
        return weight_ref[k, x, y : y + 1, :] * part(applied_ref, r) * beside

    zero = jnp.zeros((sensors, size_z), jnp.float32)
    outward, below, above = zero, zero, zero
    for y in range(size_y):
        outward = outward + crossing(0, y, part(x_low, y))
        outward = outward + crossing(1, (size_x - 1) * size_y + y, part(x_high, y))
    for x in range(size_x):
        outward = outward + crossing(2, x * size_y, part(y_low, x))
        outward = outward + crossing(3, x * size_y + size_y - 1, part(y_high, x))
    for r in range(size_x * size_y):
        below = below + crossing(4, r, z_low[0:sensors, r : r + 1])
        above = above + crossing(5, r, z_high[0:sensors, r : r + 1])
    lane_index = lax.broadcasted_iota(jnp.int32, zero.shape, 1)
    outward = outward + jnp.where(lane_index == 0, below, 0.0)
    outward = outward + jnp.where(lane_index == size_z - 1, above, 0.0)
    last = part(sum_ref, 3) - outward
    moment_ref[...] = lax.dot_general(
        jnp.ones((8, size_z), jnp.float32),
        jnp.concatenate([sum_ref[0 : 3 * sensors, :], last], axis=0),
        last_with_last,
        precision=lax.Precision.HIGHEST,
        preferred_element_type=jnp.float32,
    )


def applied_kernel(dims, applied_ref, weight_ref, chosen_ref, source_column_ref, *refs):
    sensors = dims[0]
    column_ref, high_ref, low_ref = refs[6:]
    half = column_ref.shape[1] // 2
    column_ref[...] = jnp.zeros_like(column_ref)
    column_ref[:, 0 : 3 * sensors] = source_column_ref[...]
    column_ref[:, half : half + 3 * sensors] = select_columns(
        dims, applied_ref, weight_ref, pair_up(refs[:6]), chosen_ref, high_ref, low_ref
    )


def owner_kernel(sensors, slots_each, received_ref, chosen_ref, data_ref, projection_ref, gram_ref):
    total, width = received_ref.shape
    half = width // 2
    gathered = [jnp.zeros((2, sensors), jnp.float32) for _ in range(2)]
    for first in range(0, total, slots_each):
        for k in range(2):
            start = k * half + 3 * sensors
            gathered[k] = gathered[k] + received_ref[first : first + 2, start : start + sensors]
    moments = []
    sensor_index = lax.broadcasted_iota(jnp.int32, (sensors, sensors), 0)
    lane_index = lax.broadcasted_iota(jnp.int32, (sensors, sensors), 1)
    for k in range(4):
        row = gathered[k % 2][k // 2 : k // 2 + 1, :]
        picked = jnp.where(lane_index == sensor_index, row, 0.0)
        moments.append(jnp.sum(picked, axis=1, keepdims=True))
    moment_zero, moment_one, moment_two, moment_three = moments
    first_step = moment_zero / moment_one
    residue = first_step * first_step * moment_two - moment_zero
    growth = 1.0 + residue / moment_zero
    curvature = (
        growth * growth * moment_one
        - 2.0 * growth * first_step * moment_two
        + first_step * first_step * moment_three
    )
    second_step = residue / curvature
    source_coef = first_step + second_step * growth
    applied_coef = second_step * first_step
    chosen = chosen_ref[...]
    contract = (((0,), (0,)), ((), ()))
    owned = []
    for start in (0, half):
        high, low = halves(received_ref[:, start : start + half])
        owned.append(
            lax.dot_general(high, chosen, contract, preferred_element_type=jnp.float32)
            + lax.dot_general(low, chosen, contract, preferred_element_type=jnp.float32)
        )
    lead = []
    for c in range(3):
        source_part, applied_part = (part[c * sensors : (c + 1) * sensors, :] for part in owned)
        lead.append(source_coef * source_part - applied_coef * applied_part)
        projection_ref[c] = lax.dot_general(
            data_ref[...],
            lead[c],
            contract,
            precision=lax.Precision.HIGHEST,
            preferred_element_type=jnp.float32,
        )
    for k, (first, second) in enumerate(entry_pairs):
        gram_ref[k : k + 1, :] = jnp.sum(lead[first] * lead[second], axis=0, keepdims=True)


def call(body, **arguments):
    return pl.pallas_call(
        body, compiler_params=pltpu.CompilerParams(vmem_limit_bytes=vmem_grant), **arguments
    )


def in_hbm(count):
    return [pl.BlockSpec(memory_space=pltpu.HBM)] * count


def held_in_hbm(*arrays):
    return [pltpu.with_memory_space_constraint(a, pltpu.HBM) for a in arrays]


def in_vmem(count):
    return [pl.BlockSpec(memory_space=pltpu.VMEM)] * count


def face_shapes(dims, counts, with_labels):
    sensors, size_x, size_y, size_z = dims
    lanes = -(-size_x * size_y // lane_tile) * lane_tile
    shapes = (
        (size_y * (sensors + with_labels), size_z),
        (size_x * sensors + 8 * with_labels * -(-size_x // 8), size_z),
        (sensors + size_y * with_labels, lanes),
    )
    return [
        jax.ShapeDtypeStruct(shape, jnp.float32)
        for shape, count in zip(shapes, counts)
        for _ in range(count)
    ]


def exchange_all(faces, counts):
    halos = []
    for axis, group in zip(("gx", "gy", "gz"), split_refs(faces, counts)):
        halos.extend(exchange(group, axis))
    return halos


def per_device(source_term, labels, conductivity_table, send_map, owner_slots, sensor_data):
    dims = source_term.shape
    sensors, size_x, size_y, size_z = dims
    rows_count = size_x * size_y
    counts = [faces_per_axis(lax.axis_size(axis)) for axis in ("gx", "gy", "gz")]
    owners = lax.axis_size("gx") * lax.axis_size("gy")
    slots = send_map.size
    slots_each = slots // owners
    times = sensor_data.shape[1]
    positions = owner_slots.shape[0]

    voxels = rows_count * size_z

    def array(shape, dtype=jnp.float32):
        return jax.ShapeDtypeStruct(shape, dtype)

    def halves_scratch(rows):
        return [pltpu.VMEM((rows, voxels), jnp.bfloat16)] * 2

    field_shape = array((rows_count * sensors, size_z))
    packed = call(
        functools.partial(pack_kernel, dims, counts),
        out_shape=[field_shape, array(labels.shape)] + face_shapes(dims, counts, 1),
        in_specs=in_hbm(2),
        out_specs=in_vmem(2 + sum(counts)),
        scratch_shapes=[
            pltpu.VMEM((size_x, sensors, size_y, size_z), jnp.float32),
            pltpu.VMEM((size_x, size_y, size_z), jnp.int32),
            pltpu.SemaphoreType.DMA((size_x + 1,)),
        ],
        name="pack",
    )(*held_in_hbm(source_term, labels))
    rows, shifted, faces = packed[0], packed[1], packed[2:]
    source_halos = exchange_all(faces, counts)
    levels = conductivity_table.shape[0]
    chosen, owned_chosen, data, table = call(
        functools.partial(prepare_kernel, size_z),
        out_shape=[
            array((slots, voxels), jnp.bfloat16),
            array((slots, positions), jnp.bfloat16),
            array(sensor_data.shape),
            array((levels, size_y, size_z)),
        ],
        in_specs=in_hbm(4),
        out_specs=in_vmem(4),
        scratch_shapes=[
            pltpu.VMEM((1, slots), jnp.int32),
            pltpu.VMEM((1, positions), jnp.int32),
            pltpu.SMEM((levels,), jnp.float32),
            pltpu.SemaphoreType.DMA((4,)),
        ],
        name="prepare",
    )(
        *held_in_hbm(
            send_map.reshape(1, slots),
            owner_slots.reshape(1, positions),
            sensor_data,
            conductivity_table,
        )
    )

    result = call(
        functools.partial(apply_kernel, dims, counts),
        out_shape=[array((8, size_x, size_y, size_z)), field_shape] + face_shapes(dims, counts, 0),
        in_specs=in_vmem(9),
        out_specs=in_vmem(2 + sum(counts)),
        name="apply",
    )(rows, shifted, table, *source_halos)
    weight, applied, faces = result[0], result[1], result[2:]
    applied_halos = exchange_all(faces, counts)

    source_columns, sums = call(
        functools.partial(source_kernel, dims),
        out_shape=[array((slots, 3 * sensors)), array((4 * sensors, size_z))],
        in_specs=in_vmem(10),
        out_specs=in_vmem(2),
        scratch_shapes=halves_scratch(3 * sensors),
        name="source_columns",
    )(rows, applied, weight, chosen, *source_halos)
    moment = call(
        functools.partial(moment_kernel, dims),
        out_shape=array((8, 4 * sensors)),
        in_specs=in_vmem(9),
        out_specs=in_vmem(1)[0],
        name="moments",
    )(applied, weight, sums, *applied_halos)
    depth = lax.axis_size("gz")
    moment = moment + sum(lax.ppermute(moment, "gz", ring(depth, d)) for d in range(1, depth))

    half = -(-4 * sensors // lane_tile) * lane_tile
    columns = call(
        functools.partial(applied_kernel, dims),
        out_shape=array((slots, 2 * half)),
        in_specs=in_vmem(10),
        out_specs=in_vmem(1)[0],
        scratch_shapes=halves_scratch(3 * sensors),
        name="applied_columns",
    )(applied, weight, chosen, source_columns, *applied_halos)
    stamp = jnp.pad(
        moment[0].reshape(1, 2, 2, sensors),
        ((0, 0), (0, slots_each - 2), (0, 0), (3 * sensors, half - 4 * sensors)),
    ).reshape(1, slots_each, 2 * half)
    outgoing = columns.reshape(owners, slots_each, 2 * half) + stamp
    received = lax.all_to_all(outgoing, ("gx", "gy"), 0, 0, tiled=True).reshape(slots, 2 * half)
    return call(
        functools.partial(owner_kernel, sensors, slots_each),
        out_shape=[array((3, times, positions)), array((6, positions))],
        in_specs=in_vmem(3),
        out_specs=in_vmem(2),
        name="owner",
    )(received, owned_chosen, data)


def solution(mesh):
    in_specs = (
        P(None, "gx", "gy", "gz"),
        P("gx", "gy", "gz"),
        P(),
        P("gx", "gy", "gz", None),
        P(("gx", "gy", "gz")),
        P(),
    )
    out_specs = (P(None, None, ("gx", "gy", "gz")), P(None, ("gx", "gy", "gz")))
    step = jax.shard_map(
        per_device, mesh=mesh, in_specs=in_specs, out_specs=out_specs, check_vma=False
    )
    return lambda *arguments: tuple(step(*arguments))
```

```python
import functools

import jax
import jax.numpy as jnp
from jax import lax
from jax.experimental import pallas as pl
from jax.experimental.pallas import tpu as pltpu
from jax.sharding import PartitionSpec as P

mass_term = 0.25
lane_tile = 128
vmem_grant = 16 << 20
last_with_last = (((1,), (1,)), ((), ()))
entry_pairs = ((0, 0), (1, 1), (2, 2), (0, 1), (0, 2), (1, 2))


def ring(count, step):
    return [(i, (i + step) % count) for i in range(count)]


def exchange(faces, axis):
    count = lax.axis_size(axis)
    if count == 1:
        return faces[0], faces[1]
    if count == 2:
        swapped = lax.ppermute(faces[0], axis, ring(2, 1))
        return swapped, swapped
    low, high = faces
    return lax.ppermute(high, axis, ring(count, 1)), lax.ppermute(low, axis, ring(count, -1))


def faces_per_axis(count):
    return 1 if count == 2 else 2


def lanes_equal(shape, value):
    return lax.broadcasted_iota(jnp.int32, shape, len(shape) - 1) == value


def neighbour_flags():
    flags = []
    for axis in ("gx", "gy", "gz"):
        index = lax.axis_index(axis)
        flags.append((index > 0, index < lax.axis_size(axis) - 1))
    return flags


def write_faces(dims, field, face_refs, extra=None):
    sensors, size_x, size_y, size_z = dims
    x_refs, y_refs, z_refs = face_refs

    def put(refs, axis, write):
        if len(refs) == 2:
            write(refs[0], 0)
            write(refs[1], 1)
            return
        index = lax.axis_index(axis)

        @pl.when(index == 0)
        def _():
            write(refs[0], 1)

        @pl.when(index != 0)
        def _():
            write(refs[0], 0)

    def write_x(ref, end):
        x = (size_x - 1) * end
        for y in range(size_y):
            ref[y * sensors : (y + 1) * sensors, :] = field(x * size_y + y)
        if extra is not None:
            ref[size_y * sensors : size_y * (sensors + 1), :] = extra[x]

    def write_y(ref, end):
        y = (size_y - 1) * end
        for x in range(size_x):
            ref[x * sensors : (x + 1) * sensors, :] = field(x * size_y + y)
        if extra is not None:
            for x in range(size_x):
                ref[size_x * sensors + x : size_x * sensors + x + 1, :] = extra[x][y : y + 1, :]

    def write_z(ref, end):
        z = (size_z - 1) * end
        lanes = ref.shape[1]
        packed = jnp.zeros((sensors, lanes), jnp.float32)
        for r in range(size_x * size_y):
            packed = jnp.where(lanes_equal(packed.shape, r), field(r)[:, z : z + 1], packed)
        ref[0:sensors, :] = packed
        if extra is not None:
            packed = jnp.zeros((size_y, lanes), jnp.float32)
            for x in range(size_x):
                packed = jnp.where(lanes_equal(packed.shape, x), extra[x][:, z : z + 1], packed)
            ref[sensors : sensors + size_y, :] = packed

    put(x_refs, "gx", write_x)
    put(y_refs, "gy", write_y)
    put(z_refs, "gz", write_z)


def split_refs(refs, counts):
    groups, start = [], 0
    for count in counts:
        groups.append(refs[start : start + count])
        start += count
    return groups


def pack_kernel(dims, counts, source_ref, label_ref, rows_ref, shifted_ref, *refs):
    sensors, size_x, size_y, size_z = dims
    face_refs, (staged_ref, label_vmem, semaphores) = refs[:-3], refs[-3:]
    copies = [
        pltpu.make_async_copy(source_ref.at[:, x], staged_ref.at[x], semaphores.at[x])
        for x in range(size_x)
    ]
    copies.append(pltpu.make_async_copy(label_ref, label_vmem, semaphores.at[size_x]))
    for copy in copies:
        copy.start()
    flat = staged_ref.reshape(size_x, sensors * size_y, size_z)
    for x in range(size_x):
        copies[x].wait()
        for y in range(size_y):
            r = x * size_y + y
            rows_ref[r * sensors : (r + 1) * sensors, :] = flat[x, pl.ds(y, sensors, stride=size_y), :]
    copies[size_x].wait()
    shifted = [(label_vmem[x] + 1).astype(jnp.float32) for x in range(size_x)]
    for x in range(size_x):
        shifted_ref[x] = shifted[x]
    field = lambda r: rows_ref[r * sensors : (r + 1) * sensors, :]
    write_faces(dims, field, split_refs(face_refs, counts), shifted)


def prepare_kernel(
    size_z,
    folding,
    voxel_hbm,
    owned_hbm,
    data_hbm,
    table_hbm,
    chosen_ref,
    owned_chosen_ref,
    held_ref,
    table_ref,
    voxel_ref,
    owned_ref,
    level_ref,
    semaphores,
):
    moves = (
        (voxel_hbm, voxel_ref),
        (owned_hbm, owned_ref),
        (data_hbm, held_ref),
        (table_hbm, level_ref),
    )
    copies = [pltpu.make_async_copy(*move, semaphores.at[k]) for k, move in enumerate(moves)]
    for copy in copies:
        copy.start()
    for copy in copies:
        copy.wait()
    for level in range(level_ref.shape[0]):
        table_ref[level] = jnp.full(table_ref.shape[1:], level_ref[level], jnp.float32)
    slots, voxels = chosen_ref.shape
    square = (slots, slots)
    diagonal = lanes_equal(square, lax.broadcasted_iota(jnp.int32, square, 0))
    voxel = jnp.where(diagonal, voxel_ref[...].astype(jnp.float32), 0.0)
    voxel = jnp.sum(voxel, axis=1, keepdims=True).astype(jnp.int32)
    voxel = jnp.broadcast_to(voxel, (slots, size_z))
    lane_index = lax.broadcasted_iota(jnp.int32, (slots, size_z), 1)
    for first in range(0, voxels, size_z):
        chosen_ref[:, first : first + size_z] = one_hot(lane_index == voxel - first)
    row_index = lax.broadcasted_iota(jnp.int32, (slots, owned_ref.shape[1]), 0)
    owned_chosen_ref[0:slots, :] = one_hot(row_index == owned_ref[...])
    slots_each, fold = folding
    if fold:
        part = slots_each // fold
        row_index = lax.broadcasted_iota(jnp.int32, (slots // fold, owned_ref.shape[1]), 0)
        slot_index = row_index // part * slots_each + row_index % part
        for k in range(fold):
            first = slots + k * (slots // fold)
            owned_chosen_ref[first : first + slots // fold, :] = one_hot(
                slot_index + k * part == owned_ref[...]
            )


def one_hot(condition):
    return condition.astype(jnp.float32).astype(jnp.bfloat16)


def tissue(shifted, table_ref):
    conductivity = jnp.zeros_like(shifted)
    for level in range(table_ref.shape[0]):
        conductivity = jnp.where(shifted == level + 1, table_ref[level], conductivity)
    return conductivity, (shifted > 0).astype(jnp.float32)


def edge_weight(first, second):
    return 0.5 * (first[0] + second[0]) * first[1] * second[1]


def weights(dims, shifted_ref, table_ref, halo_refs, weight_ref):
    sensors, size_x, size_y, size_z = dims
    flags = neighbour_flags()
    (x_low, x_high), (y_low, y_high), (z_low, z_high) = halo_refs

    def masked(value, flag):
        return jnp.where(flag, value, 0.0)

    own = [shifted_ref[x] for x in range(size_x)]
    own_tissue = [tissue(plane, table_ref) for plane in own]
    x_rows = slice(size_y * sensors, size_y * (sensors + 1))
    below = tissue(masked(x_low[x_rows, :], flags[0][0]), table_ref)
    above = tissue(masked(x_high[x_rows, :], flags[0][1]), table_ref)
    planes = [below] + own_tissue + [above]
    across_x = [edge_weight(planes[i], planes[i + 1]) for i in range(size_x + 1)]
    row_index = lax.broadcasted_iota(jnp.int32, (size_y, size_z), 0)
    lane_index = lax.broadcasted_iota(jnp.int32, (size_y, size_z), 1)
    for x in range(size_x):
        y_row = size_x * sensors + x
        shifted = own[x]
        y_before = jnp.where(
            row_index == 0,
            masked(y_low[y_row : y_row + 1, :], flags[1][0]),
            pltpu.roll(shifted, 1, 0),
        )
        y_after = jnp.where(
            row_index == size_y - 1,
            masked(y_high[y_row : y_row + 1, :], flags[1][1]),
            pltpu.roll(shifted, size_y - 1, 0),
        )
        z_rows = slice(sensors, sensors + size_y)
        z_before = jnp.where(
            lane_index == 0,
            masked(z_low[z_rows, x : x + 1], flags[2][0]),
            pltpu.roll(shifted, 1, 1),
        )
        z_after = jnp.where(
            lane_index == size_z - 1,
            masked(z_high[z_rows, x : x + 1], flags[2][1]),
            pltpu.roll(shifted, size_z - 1, 1),
        )
        six = [across_x[x], across_x[x + 1]]
        for beside in (y_before, y_after, z_before, z_after):
            six.append(edge_weight(own_tissue[x], tissue(beside, table_ref)))
        for k, weight in enumerate(six):
            weight_ref[k, x] = weight
        weight_ref[6, x] = mass_term + (six[0] + six[1]) + (six[2] + six[3]) + (six[4] + six[5])
        weight_ref[7, x] = 0.5 * own_tissue[x][0]


def around(dims, rows_ref, halo_refs, r, flags=None):
    sensors, size_x, size_y, size_z = dims
    (x_low, x_high), (y_low, y_high), (z_low, z_high) = halo_refs
    x, y = divmod(r, size_y)

    def keep(value, dim, end):
        return value if flags is None else jnp.where(flags[dim][end], value, 0.0)

    def row(index):
        return rows_ref[index * sensors : (index + 1) * sensors, :]

    def part(ref, index):
        return ref[index * sensors : (index + 1) * sensors, :]

    centre = row(r)
    x_before = row(r - size_y) if x > 0 else keep(part(x_low, y), 0, 0)
    x_after = row(r + size_y) if x < size_x - 1 else keep(part(x_high, y), 0, 1)
    y_before = row(r - 1) if y > 0 else keep(part(y_low, x), 1, 0)
    y_after = row(r + 1) if y < size_y - 1 else keep(part(y_high, x), 1, 1)
    lane_index = lax.broadcasted_iota(jnp.int32, centre.shape, 1)
    z_before = jnp.where(
        lane_index == 0, keep(z_low[0:sensors, r : r + 1], 2, 0), pltpu.roll(centre, 1, 1)
    )
    z_after = jnp.where(
        lane_index == size_z - 1,
        keep(z_high[0:sensors, r : r + 1], 2, 1),
        pltpu.roll(centre, size_z - 1, 1),
    )
    return centre, (x_before, x_after, y_before, y_after, z_before, z_after)


def combine(weight_ref, x, y, centre, beside):
    total = weight_ref[6, x, y : y + 1, :] * centre
    for k, value in enumerate(beside):
        total = total - weight_ref[k, x, y : y + 1, :] * value
    return total


def pair_up(refs):
    return [(refs[2 * i], refs[2 * i + 1]) for i in range(3)]


def apply_kernel(dims, counts, rows_ref, shifted_ref, table_ref, *refs):
    sensors, size_x, size_y, size_z = dims
    halo_refs = pair_up(refs[:6])
    weight_ref, applied_ref = refs[6:8]
    face_refs = refs[8:]
    weights(dims, shifted_ref, table_ref, halo_refs, weight_ref)
    for r in range(size_x * size_y):
        x, y = divmod(r, size_y)
        centre, beside = around(dims, rows_ref, halo_refs, r)
        applied_ref[r * sensors : (r + 1) * sensors, :] = combine(weight_ref, x, y, centre, beside)
    field = lambda r: applied_ref[r * sensors : (r + 1) * sensors, :]
    write_faces(dims, field, split_refs(face_refs, counts))


def halves(value):
    high = value.astype(jnp.bfloat16)
    return high, (value - high.astype(jnp.float32)).astype(jnp.bfloat16)


def local_twice(dims, rows_ref, weight_ref, r):
    sensors, size_x, size_y, size_z = dims
    x, y = divmod(r, size_y)

    def row(index):
        return rows_ref[index * sensors : (index + 1) * sensors, :]

    def weight(k):
        return weight_ref[k, x, y : y + 1, :]

    centre = row(r)
    lane_index = lax.broadcasted_iota(jnp.int32, centre.shape, 1)
    total = weight(6) * centre
    if x > 0:
        total = total - weight(0) * row(r - size_y)
    if x < size_x - 1:
        total = total - weight(1) * row(r + size_y)
    if y > 0:
        total = total - weight(2) * row(r - 1)
    if y < size_y - 1:
        total = total - weight(3) * row(r + 1)
    before = jnp.where(lane_index == 0, 0.0, pltpu.roll(centre, 1, 1))
    after = jnp.where(lane_index == size_z - 1, 0.0, pltpu.roll(centre, size_z - 1, 1))
    return total - weight(4) * before - weight(5) * after


def select_columns(dims, rows_ref, weight_ref, halo_refs, chosen_ref, high_ref, low_ref):
    sensors, size_x, size_y, size_z = dims
    flags = neighbour_flags()
    for r in range(size_x * size_y):
        x, y = divmod(r, size_y)
        span = slice(r * size_z, (r + 1) * size_z)
        scale = weight_ref[7, x, y : y + 1, :]
        _, beside = around(dims, rows_ref, halo_refs, r, flags)
        for c in range(3):
            high, low = halves(scale * (beside[2 * c + 1] - beside[2 * c]))
            high_ref[c * sensors : (c + 1) * sensors, span] = high
            low_ref[c * sensors : (c + 1) * sensors, span] = low
    chosen = chosen_ref[...]
    return lax.dot_general(
        chosen, high_ref[...], last_with_last, preferred_element_type=jnp.float32
    ) + lax.dot_general(chosen, low_ref[...], last_with_last, preferred_element_type=jnp.float32)


def source_kernel(dims, rows_ref, applied_ref, weight_ref, chosen_ref, *refs):
    sensors, size_x, size_y, size_z = dims
    halo_refs = pair_up(refs[:6])
    column_ref, sum_ref, high_ref, low_ref = refs[6:]
    sums = [jnp.zeros((sensors, size_z), jnp.float32) for _ in range(4)]
    for r in range(size_x * size_y):
        source = rows_ref[r * sensors : (r + 1) * sensors, :]
        applied = applied_ref[r * sensors : (r + 1) * sensors, :]
        twice = local_twice(dims, applied_ref, weight_ref, r)
        for k, product in enumerate(
            (source * source, source * applied, applied * applied, applied * twice)
        ):
            sums[k] = sums[k] + product
    for k in range(4):
        sum_ref[k * sensors : (k + 1) * sensors, :] = sums[k]
    column_ref[...] = select_columns(
        dims, rows_ref, weight_ref, halo_refs, chosen_ref, high_ref, low_ref
    )


def moment_kernel(dims, applied_ref, weight_ref, sum_ref, *refs):
    sensors, size_x, size_y, size_z = dims
    (x_low, x_high), (y_low, y_high), (z_low, z_high) = pair_up(refs[:6])
    moment_ref = refs[6]

    def part(ref, index):
        return ref[index * sensors : (index + 1) * sensors, :]

    def crossing(k, r, beside):
        x, y = divmod(r, size_y)
        return weight_ref[k, x, y : y + 1, :] * part(applied_ref, r) * beside

    zero = jnp.zeros((sensors, size_z), jnp.float32)
    outward, below, above = zero, zero, zero
    for y in range(size_y):
        outward = outward + crossing(0, y, part(x_low, y))
        outward = outward + crossing(1, (size_x - 1) * size_y + y, part(x_high, y))
    for x in range(size_x):
        outward = outward + crossing(2, x * size_y, part(y_low, x))
        outward = outward + crossing(3, x * size_y + size_y - 1, part(y_high, x))
    for r in range(size_x * size_y):
        below = below + crossing(4, r, z_low[0:sensors, r : r + 1])
        above = above + crossing(5, r, z_high[0:sensors, r : r + 1])
    lane_index = lax.broadcasted_iota(jnp.int32, zero.shape, 1)
    outward = outward + jnp.where(lane_index == 0, below, 0.0)
    outward = outward + jnp.where(lane_index == size_z - 1, above, 0.0)
    last = part(sum_ref, 3) - outward
    moment_ref[...] = lax.dot_general(
        jnp.ones((8, size_z), jnp.float32),
        jnp.concatenate([sum_ref[0 : 3 * sensors, :], last], axis=0),
        last_with_last,
        precision=lax.Precision.HIGHEST,
        preferred_element_type=jnp.float32,
    )


def payload_rows(sensors, slots_each):
    whole, rest = divmod(6 * sensors, lane_tile)
    fold = lane_tile // rest if rest else 0
    assert not fold or (fold * rest == lane_tile and slots_each % fold == 0)
    rows = whole * slots_each + (slots_each // fold if fold else 0)
    return whole, rest, fold, rows, -(-4 * sensors // lane_tile)


def applied_kernel(dims, slots_each, applied_ref, weight_ref, chosen_ref, source_column_ref, *refs):
    sensors = dims[0]
    column_ref, high_ref, low_ref = refs[6:]
    applied_columns = select_columns(
        dims, applied_ref, weight_ref, pair_up(refs[:6]), chosen_ref, high_ref, low_ref
    )
    columns = jnp.concatenate([source_column_ref[...], applied_columns], axis=1)
    whole, rest, fold, rows, moment_rows = payload_rows(sensors, slots_each)
    for owner in range(columns.shape[0] // slots_each):
        mine = slice(owner * slots_each, (owner + 1) * slots_each)
        at = owner * (rows + moment_rows)
        for tile in range(whole):
            column_ref[at : at + slots_each, :] = columns[mine, tile * lane_tile : (tile + 1) * lane_tile]
            at += slots_each
        if fold:
            part = slots_each // fold
            others = columns[mine, whole * lane_tile :]
            column_ref[at : at + part, :] = jnp.concatenate(
                [others[k * part : (k + 1) * part, :] for k in range(fold)], axis=1
            )
            at += part
        column_ref[at : at + moment_rows, :] = jnp.zeros((moment_rows, lane_tile), jnp.float32)


def owner_kernel(sensors, slots_each, received_ref, chosen_ref, data_ref, projection_ref, gram_ref):
    whole, rest, fold, rows, moment_rows = payload_rows(sensors, slots_each)
    each = rows + moment_rows
    sources = received_ref.shape[0] // each
    slots = sources * slots_each

    def collected(start, count):
        return jnp.concatenate(
            [received_ref[k * each + start : k * each + start + count, :] for k in range(sources)],
            axis=0,
        )

    gathered = jnp.zeros((moment_rows, lane_tile), jnp.float32)
    for k in range(sources):
        gathered = gathered + received_ref[k * each + rows : (k + 1) * each, :]
    moments = []
    sensor_index = lax.broadcasted_iota(jnp.int32, (sensors, lane_tile), 0)
    lane_index = lax.broadcasted_iota(jnp.int32, (sensors, lane_tile), 1)
    for k in range(4):
        total = jnp.zeros((sensors, 1), jnp.float32)
        for row in range(moment_rows):
            here = lane_index + row * lane_tile == sensor_index + k * sensors
            picked = jnp.where(here, gathered[row : row + 1, :], 0.0)
            total = total + jnp.sum(picked, axis=1, keepdims=True)
        moments.append(total)
    moment_zero, moment_one, moment_two, moment_three = moments
    first_step = moment_zero / moment_one
    residue = first_step * first_step * moment_two - moment_zero
    growth = 1.0 + residue / moment_zero
    curvature = (
        growth * growth * moment_one
        - 2.0 * growth * first_step * moment_two
        + first_step * first_step * moment_three
    )
    second_step = residue / curvature
    source_coef = first_step + second_step * growth
    applied_coef = second_step * first_step
    contract = (((0,), (0,)), ((), ()))

    def selected(values, first):
        chosen = chosen_ref[first : first + values.shape[0], :]
        high, low = halves(values)
        return lax.dot_general(
            high, chosen, contract, preferred_element_type=jnp.float32
        ) + lax.dot_general(low, chosen, contract, preferred_element_type=jnp.float32)

    owned = [
        selected(collected(tile * slots_each, slots_each), 0) for tile in range(whole)
    ]
    if fold:
        folded = collected(whole * slots_each, slots_each // fold)
        others = jnp.zeros((rest, chosen_ref.shape[1]), jnp.float32)
        for k in range(fold):
            found = selected(folded, slots + k * (slots // fold))
            others = others + found[k * rest : (k + 1) * rest, :]
        owned.append(others)
    owned = jnp.concatenate(owned, axis=0)
    lead = []
    for c in range(3):
        source_part = owned[c * sensors : (c + 1) * sensors, :]
        applied_part = owned[(3 + c) * sensors : (4 + c) * sensors, :]
        lead.append(source_coef * source_part - applied_coef * applied_part)
        projection_ref[c] = lax.dot_general(
            data_ref[...],
            lead[c],
            contract,
            precision=lax.Precision.HIGHEST,
            preferred_element_type=jnp.float32,
        )
    for k, (first, second) in enumerate(entry_pairs):
        gram_ref[k : k + 1, :] = jnp.sum(lead[first] * lead[second], axis=0, keepdims=True)


def call(body, **arguments):
    return pl.pallas_call(
        body, compiler_params=pltpu.CompilerParams(vmem_limit_bytes=vmem_grant), **arguments
    )


def in_hbm(count):
    return [pl.BlockSpec(memory_space=pltpu.HBM)] * count


def held_in_hbm(*arrays):
    return [pltpu.with_memory_space_constraint(a, pltpu.HBM) for a in arrays]


def in_vmem(count):
    return [pl.BlockSpec(memory_space=pltpu.VMEM)] * count


def face_shapes(dims, counts, with_labels):
    sensors, size_x, size_y, size_z = dims
    lanes = -(-size_x * size_y // lane_tile) * lane_tile
    shapes = (
        (size_y * (sensors + with_labels), size_z),
        (size_x * sensors + 8 * with_labels * -(-size_x // 8), size_z),
        (sensors + size_y * with_labels, lanes),
    )
    return [
        jax.ShapeDtypeStruct(shape, jnp.float32)
        for shape, count in zip(shapes, counts)
        for _ in range(count)
    ]


def exchange_all(faces, counts):
    halos = []
    for axis, group in zip(("gx", "gy", "gz"), split_refs(faces, counts)):
        halos.extend(exchange(group, axis))
    return halos


def per_device(source_term, labels, conductivity_table, send_map, owner_slots, sensor_data):
    dims = source_term.shape
    sensors, size_x, size_y, size_z = dims
    rows_count = size_x * size_y
    counts = [faces_per_axis(lax.axis_size(axis)) for axis in ("gx", "gy", "gz")]
    owners = lax.axis_size("gx") * lax.axis_size("gy")
    slots = send_map.size
    slots_each = slots // owners
    _, _, fold, payload, moment_rows = payload_rows(sensors, slots_each)
    times = sensor_data.shape[1]
    positions = owner_slots.shape[0]

    voxels = rows_count * size_z

    def array(shape, dtype=jnp.float32):
        return jax.ShapeDtypeStruct(shape, dtype)

    def halves_scratch(rows):
        return [pltpu.VMEM((rows, voxels), jnp.bfloat16)] * 2

    field_shape = array((rows_count * sensors, size_z))
    packed = call(
        functools.partial(pack_kernel, dims, counts),
        out_shape=[field_shape, array(labels.shape)] + face_shapes(dims, counts, 1),
        in_specs=in_hbm(2),
        out_specs=in_vmem(2 + sum(counts)),
        scratch_shapes=[
            pltpu.VMEM((size_x, sensors, size_y, size_z), jnp.float32),
            pltpu.VMEM((size_x, size_y, size_z), jnp.int32),
            pltpu.SemaphoreType.DMA((size_x + 1,)),
        ],
        name="pack",
    )(*held_in_hbm(source_term, labels))
    rows, shifted, faces = packed[0], packed[1], packed[2:]
    source_halos = exchange_all(faces, counts)
    levels = conductivity_table.shape[0]
    chosen, owned_chosen, data, table = call(
        functools.partial(prepare_kernel, size_z, (slots_each, fold)),
        out_shape=[
            array((slots, voxels), jnp.bfloat16),
            array((slots * (2 if fold else 1), positions), jnp.bfloat16),
            array(sensor_data.shape),
            array((levels, size_y, size_z)),
        ],
        in_specs=in_hbm(4),
        out_specs=in_vmem(4),
        scratch_shapes=[
            pltpu.VMEM((1, slots), jnp.int32),
            pltpu.VMEM((1, positions), jnp.int32),
            pltpu.SMEM((levels,), jnp.float32),
            pltpu.SemaphoreType.DMA((4,)),
        ],
        name="prepare",
    )(
        *held_in_hbm(
            send_map.reshape(1, slots),
            owner_slots.reshape(1, positions),
            sensor_data,
            conductivity_table,
        )
    )

    result = call(
        functools.partial(apply_kernel, dims, counts),
        out_shape=[array((8, size_x, size_y, size_z)), field_shape] + face_shapes(dims, counts, 0),
        in_specs=in_vmem(9),
        out_specs=in_vmem(2 + sum(counts)),
        name="apply",
    )(rows, shifted, table, *source_halos)
    weight, applied, faces = result[0], result[1], result[2:]
    applied_halos = exchange_all(faces, counts)

    source_columns, sums = call(
        functools.partial(source_kernel, dims),
        out_shape=[array((slots, 3 * sensors)), array((4 * sensors, size_z))],
        in_specs=in_vmem(10),
        out_specs=in_vmem(2),
        scratch_shapes=halves_scratch(3 * sensors),
        name="source_columns",
    )(rows, applied, weight, chosen, *source_halos)
    moment = call(
        functools.partial(moment_kernel, dims),
        out_shape=array((8, 4 * sensors)),
        in_specs=in_vmem(9),
        out_specs=in_vmem(1)[0],
        name="moments",
    )(applied, weight, sums, *applied_halos)
    depth = lax.axis_size("gz")
    moment = moment + sum(lax.ppermute(moment, "gz", ring(depth, d)) for d in range(depth - 1, 0, -1))

    each = payload + moment_rows
    columns = call(
        functools.partial(applied_kernel, dims, slots_each),
        out_shape=array((owners * each, lane_tile)),
        in_specs=in_vmem(10),
        out_specs=in_vmem(1)[0],
        scratch_shapes=halves_scratch(3 * sensors),
        name="applied_columns",
    )(applied, weight, chosen, source_columns, *applied_halos)
    place = lax.broadcasted_iota(jnp.int32, columns.shape, 0) % each
    stamp = jnp.pad(moment[0], (0, moment_rows * lane_tile - 4 * sensors)).reshape(-1, lane_tile)
    for row in range(moment_rows):
        columns = jnp.where(place == payload + row, stamp[row : row + 1], columns)
    received = lax.all_to_all(
        columns.reshape(owners, 1, each * lane_tile), ("gx", "gy"), 0, 0, tiled=True
    ).reshape(columns.shape)
    return call(
        functools.partial(owner_kernel, sensors, slots_each),
        out_shape=[array((3, times, positions)), array((6, positions))],
        in_specs=in_vmem(3),
        out_specs=in_vmem(2),
        name="owner",
    )(received, owned_chosen, data)


def solution(mesh):
    in_specs = (
        P(None, "gx", "gy", "gz"),
        P("gx", "gy", "gz"),
        P(),
        P("gx", "gy", "gz", None),
        P(("gx", "gy", "gz")),
        P(),
    )
    out_specs = (P(None, None, ("gx", "gy", "gz")), P(None, ("gx", "gy", "gz")))
    step = jax.shard_map(
        per_device, mesh=mesh, in_specs=in_specs, out_specs=out_specs, check_vma=False
    )
    return lambda *arguments: tuple(step(*arguments))
```

```python
import functools

import jax
import jax.numpy as jnp
from jax import lax
from jax.experimental import pallas as pl
from jax.experimental.pallas import tpu as pltpu
from jax.sharding import PartitionSpec as P

mass_term = 0.25
lane_tile = 128
axes = ("gx", "gy", "gz")
vmem_grant = 16 << 20
last_with_last = (((1,), (1,)), ((), ()))
entry_pairs = ((0, 0), (1, 1), (2, 2), (0, 1), (0, 2), (1, 2))


def swap(value, axis, odd):
    count, beside = lax.axis_size(axis), lax.axis_size("gz")
    partner = {}
    for first in range(odd, count - 1, 2):
        partner[first], partner[first + 1] = first + 1, first
    alone = [i for i in range(count) if i not in partner]
    if alone and axis != "gz" and beside % 2 == 0:
        table = [
            (i * beside + k, partner[i] * beside + k if i in partner else i * beside + (k ^ 1))
            for i in range(count)
            for k in range(beside)
        ]
        return lax.ppermute(value, (axis, "gz"), table)
    for source, target in zip(alone, alone[::-1]):
        partner[source] = target
    return lax.ppermute(value, axis, sorted(partner.items()))


def sum_over(value, axis):
    count = lax.axis_size(axis)
    if count & (count - 1) == 0:
        tables = [[(i, i ^ d) for i in range(count)] for d in range(count - 1, 0, -1)]
    else:
        tables = [[(i, (i + d) % count) for i in range(count)] for d in range(count - 1, 0, -1)]
    return value + sum(lax.ppermute(value, axis, table) for table in tables)


def face_counts():
    return [1 if lax.axis_size(axis) <= 2 else 2 for axis in axes]


def exchange_all(faces, counts):
    halos = []
    for axis, group in zip(axes, split_refs(faces, counts)):
        if lax.axis_size(axis) > 1:
            group = [swap(face, axis, odd) for odd, face in enumerate(group)]
        halos.extend(group)
    return halos


def sort_halos(halo_refs, held_refs, counts):
    sorted_refs, held_refs = [], list(held_refs)
    for axis, group in zip(axes, split_refs(halo_refs, counts)):
        if len(group) == 1:
            sorted_refs.append((group[0], group[0]))
            continue
        even = lax.axis_index(axis) % 2 == 0
        below, above = held_refs.pop(0), held_refs.pop(0)
        first, second = group[0][...], group[1][...]
        below[...] = jnp.where(even, second, first)
        above[...] = jnp.where(even, first, second)
        sorted_refs.append((below, above))
    return sorted_refs


def held_halos(faces, counts):
    return [
        pltpu.VMEM(face.shape, face.dtype)
        for group in split_refs(faces, counts)
        for face in (group if len(group) == 2 else [])
    ]


def lanes_equal(shape, value):
    return lax.broadcasted_iota(jnp.int32, shape, len(shape) - 1) == value


def neighbour_flags():
    flags = []
    for axis in axes:
        index = lax.axis_index(axis)
        flags.append((index > 0, index < lax.axis_size(axis) - 1))
    return flags


def write_faces(dims, rows_ref, face_refs, extra=None):
    sensors, size_x, size_y, size_z = dims
    x_refs, y_refs, z_refs = face_refs

    def field(r):
        return rows_ref[pl.ds(pl.multiple_of(r * sensors, sensors), sensors), :]

    def high_end(axis, number):
        return lax.axis_index(axis) % 2 == number

    for number, ref in enumerate(x_refs):
        high = high_end("gx", number)
        x = jnp.where(high, size_x - 1, 0)
        for y in range(size_y):
            ref[y * sensors : (y + 1) * sensors, :] = field(x * size_y + y)
        if extra is not None:
            ref[size_y * sensors : size_y * (sensors + 1), :] = jnp.where(high, extra[-1], extra[0])

    for number, ref in enumerate(y_refs):
        high = high_end("gy", number)
        y = jnp.where(high, size_y - 1, 0)
        for x in range(size_x):
            ref[x * sensors : (x + 1) * sensors, :] = field(x * size_y + y)
            if extra is not None:
                row = size_x * sensors + x
                ref[row : row + 1, :] = jnp.where(high, extra[x][size_y - 1 :, :], extra[x][0:1, :])

    lanes = z_refs[0].shape[1]
    ends = []
    for z in (0, size_z - 1):
        packed = jnp.zeros((sensors, lanes), jnp.float32)
        for r in range(size_x * size_y):
            row = rows_ref[r * sensors : (r + 1) * sensors, :]
            packed = jnp.where(lanes_equal(packed.shape, r), row[:, z : z + 1], packed)
        if extra is not None:
            labels = jnp.zeros((size_y, lanes), jnp.float32)
            for x in range(size_x):
                labels = jnp.where(lanes_equal(labels.shape, x), extra[x][:, z : z + 1], labels)
            packed = jnp.concatenate([packed, labels], axis=0)
        ends.append(packed)
    for number, ref in enumerate(z_refs):
        ref[...] = jnp.where(high_end("gz", number), ends[1], ends[0])


def split_refs(refs, counts):
    groups, start = [], 0
    for count in counts:
        groups.append(refs[start : start + count])
        start += count
    return groups


def pack_kernel(dims, counts, source_ref, label_ref, rows_ref, shifted_ref, *refs):
    sensors, size_x, size_y, size_z = dims
    face_refs, (staged_ref, label_vmem, semaphores) = refs[:-3], refs[-3:]
    copies = [
        pltpu.make_async_copy(source_ref.at[:, x], staged_ref.at[x], semaphores.at[x])
        for x in range(size_x)
    ]
    copies.append(pltpu.make_async_copy(label_ref, label_vmem, semaphores.at[size_x]))
    for copy in copies:
        copy.start()
    flat = staged_ref.reshape(size_x, sensors * size_y, size_z)
    for x in range(size_x):
        copies[x].wait()
        for y in range(size_y):
            r = x * size_y + y
            rows_ref[r * sensors : (r + 1) * sensors, :] = flat[x, pl.ds(y, sensors, stride=size_y), :]
    copies[size_x].wait()
    shifted = [(label_vmem[x] + 1).astype(jnp.float32) for x in range(size_x)]
    for x in range(size_x):
        shifted_ref[x] = shifted[x]
    write_faces(dims, rows_ref, split_refs(face_refs, counts), shifted)


def prepare_kernel(
    size_z,
    folding,
    voxel_hbm,
    owned_hbm,
    data_hbm,
    table_hbm,
    chosen_ref,
    owned_chosen_ref,
    held_ref,
    table_ref,
    voxel_ref,
    owned_ref,
    level_ref,
    semaphores,
):
    moves = (
        (voxel_hbm, voxel_ref),
        (owned_hbm, owned_ref),
        (data_hbm, held_ref),
        (table_hbm, level_ref),
    )
    copies = [pltpu.make_async_copy(*move, semaphores.at[k]) for k, move in enumerate(moves)]
    for copy in copies:
        copy.start()
    for copy in copies:
        copy.wait()
    for level in range(level_ref.shape[0]):
        table_ref[level] = jnp.full(table_ref.shape[1:], level_ref[level], jnp.float32)
    slots, voxels = chosen_ref.shape
    square = (slots, slots)
    diagonal = lanes_equal(square, lax.broadcasted_iota(jnp.int32, square, 0))
    voxel = jnp.where(diagonal, voxel_ref[...].astype(jnp.float32), 0.0)
    voxel = jnp.sum(voxel, axis=1, keepdims=True).astype(jnp.int32)
    voxel = jnp.broadcast_to(voxel, (slots, size_z))
    lane_index = lax.broadcasted_iota(jnp.int32, (slots, size_z), 1)
    for first in range(0, voxels, size_z):
        chosen_ref[:, first : first + size_z] = one_hot(lane_index == voxel - first)
    row_index = lax.broadcasted_iota(jnp.int32, (slots, owned_ref.shape[1]), 0)
    owned_chosen_ref[0:slots, :] = one_hot(row_index == owned_ref[...])
    slots_each, fold = folding
    if fold:
        part = slots_each // fold
        row_index = lax.broadcasted_iota(jnp.int32, (slots // fold, owned_ref.shape[1]), 0)
        slot_index = row_index // part * slots_each + row_index % part
        for k in range(fold):
            first = slots + k * (slots // fold)
            owned_chosen_ref[first : first + slots // fold, :] = one_hot(
                slot_index + k * part == owned_ref[...]
            )


def one_hot(condition):
    return condition.astype(jnp.float32).astype(jnp.bfloat16)


def tissue(shifted, table_ref):
    conductivity = jnp.zeros_like(shifted)
    for level in range(table_ref.shape[0]):
        conductivity = jnp.where(shifted == level + 1, table_ref[level], conductivity)
    return conductivity, (shifted > 0).astype(jnp.float32)


def edge_weight(first, second):
    return 0.5 * (first[0] + second[0]) * first[1] * second[1]


def weights(dims, shifted_ref, table_ref, halo_refs, weight_ref):
    sensors, size_x, size_y, size_z = dims
    flags = neighbour_flags()
    (x_low, x_high), (y_low, y_high), (z_low, z_high) = halo_refs

    def masked(value, flag):
        return jnp.where(flag, value, 0.0)

    own = [shifted_ref[x] for x in range(size_x)]
    own_tissue = [tissue(plane, table_ref) for plane in own]
    x_rows = slice(size_y * sensors, size_y * (sensors + 1))
    below = tissue(masked(x_low[x_rows, :], flags[0][0]), table_ref)
    above = tissue(masked(x_high[x_rows, :], flags[0][1]), table_ref)
    planes = [below] + own_tissue + [above]
    across_x = [edge_weight(planes[i], planes[i + 1]) for i in range(size_x + 1)]
    row_index = lax.broadcasted_iota(jnp.int32, (size_y, size_z), 0)
    lane_index = lax.broadcasted_iota(jnp.int32, (size_y, size_z), 1)
    for x in range(size_x):
        y_row = size_x * sensors + x
        shifted = own[x]
        y_before = jnp.where(
            row_index == 0,
            masked(y_low[y_row : y_row + 1, :], flags[1][0]),
            pltpu.roll(shifted, 1, 0),
        )
        y_after = jnp.where(
            row_index == size_y - 1,
            masked(y_high[y_row : y_row + 1, :], flags[1][1]),
            pltpu.roll(shifted, size_y - 1, 0),
        )
        z_rows = slice(sensors, sensors + size_y)
        z_before = jnp.where(
            lane_index == 0,
            masked(z_low[z_rows, x : x + 1], flags[2][0]),
            pltpu.roll(shifted, 1, 1),
        )
        z_after = jnp.where(
            lane_index == size_z - 1,
            masked(z_high[z_rows, x : x + 1], flags[2][1]),
            pltpu.roll(shifted, size_z - 1, 1),
        )
        six = [across_x[x], across_x[x + 1]]
        for beside in (y_before, y_after, z_before, z_after):
            six.append(edge_weight(own_tissue[x], tissue(beside, table_ref)))
        for k, weight in enumerate(six):
            weight_ref[k, x] = weight
        weight_ref[6, x] = mass_term + (six[0] + six[1]) + (six[2] + six[3]) + (six[4] + six[5])
        weight_ref[7, x] = 0.5 * own_tissue[x][0]


def around(dims, rows_ref, halo_refs, r, flags=None):
    sensors, size_x, size_y, size_z = dims
    (x_low, x_high), (y_low, y_high), (z_low, z_high) = halo_refs
    x, y = divmod(r, size_y)

    def keep(value, dim, end):
        return value if flags is None else jnp.where(flags[dim][end], value, 0.0)

    def row(index):
        return rows_ref[index * sensors : (index + 1) * sensors, :]

    def part(ref, index):
        return ref[index * sensors : (index + 1) * sensors, :]

    centre = row(r)
    x_before = row(r - size_y) if x > 0 else keep(part(x_low, y), 0, 0)
    x_after = row(r + size_y) if x < size_x - 1 else keep(part(x_high, y), 0, 1)
    y_before = row(r - 1) if y > 0 else keep(part(y_low, x), 1, 0)
    y_after = row(r + 1) if y < size_y - 1 else keep(part(y_high, x), 1, 1)
    lane_index = lax.broadcasted_iota(jnp.int32, centre.shape, 1)
    z_before = jnp.where(
        lane_index == 0, keep(z_low[0:sensors, r : r + 1], 2, 0), pltpu.roll(centre, 1, 1)
    )
    z_after = jnp.where(
        lane_index == size_z - 1,
        keep(z_high[0:sensors, r : r + 1], 2, 1),
        pltpu.roll(centre, size_z - 1, 1),
    )
    return centre, (x_before, x_after, y_before, y_after, z_before, z_after)


def combine(weight_ref, x, y, centre, beside):
    total = weight_ref[6, x, y : y + 1, :] * centre
    for k, value in enumerate(beside):
        total = total - weight_ref[k, x, y : y + 1, :] * value
    return total


def apply_kernel(dims, counts, rows_ref, shifted_ref, table_ref, *refs):
    sensors, size_x, size_y, size_z = dims
    messages = sum(counts)
    halo_refs = sort_halos(refs[:messages], refs[2 * messages + 2 :], counts)
    weight_ref, applied_ref = refs[messages : messages + 2]
    face_refs = refs[messages + 2 : 2 * messages + 2]
    weights(dims, shifted_ref, table_ref, halo_refs, weight_ref)
    for r in range(size_x * size_y):
        x, y = divmod(r, size_y)
        centre, beside = around(dims, rows_ref, halo_refs, r)
        applied_ref[r * sensors : (r + 1) * sensors, :] = combine(weight_ref, x, y, centre, beside)
    write_faces(dims, applied_ref, split_refs(face_refs, counts))


def halves(value):
    high = value.astype(jnp.bfloat16)
    return high, (value - high.astype(jnp.float32)).astype(jnp.bfloat16)


def local_twice(dims, rows_ref, weight_ref, r):
    sensors, size_x, size_y, size_z = dims
    x, y = divmod(r, size_y)

    def row(index):
        return rows_ref[index * sensors : (index + 1) * sensors, :]

    def weight(k):
        return weight_ref[k, x, y : y + 1, :]

    centre = row(r)
    lane_index = lax.broadcasted_iota(jnp.int32, centre.shape, 1)
    total = weight(6) * centre
    if x > 0:
        total = total - weight(0) * row(r - size_y)
    if x < size_x - 1:
        total = total - weight(1) * row(r + size_y)
    if y > 0:
        total = total - weight(2) * row(r - 1)
    if y < size_y - 1:
        total = total - weight(3) * row(r + 1)
    before = jnp.where(lane_index == 0, 0.0, pltpu.roll(centre, 1, 1))
    after = jnp.where(lane_index == size_z - 1, 0.0, pltpu.roll(centre, size_z - 1, 1))
    return total - weight(4) * before - weight(5) * after


def select_columns(dims, rows_ref, weight_ref, halo_refs, chosen_ref, high_ref, low_ref):
    sensors, size_x, size_y, size_z = dims
    flags = neighbour_flags()
    for r in range(size_x * size_y):
        x, y = divmod(r, size_y)
        span = slice(r * size_z, (r + 1) * size_z)
        scale = weight_ref[7, x, y : y + 1, :]
        _, beside = around(dims, rows_ref, halo_refs, r, flags)
        for c in range(3):
            high, low = halves(scale * (beside[2 * c + 1] - beside[2 * c]))
            high_ref[c * sensors : (c + 1) * sensors, span] = high
            low_ref[c * sensors : (c + 1) * sensors, span] = low
    chosen = chosen_ref[...]
    return lax.dot_general(
        chosen, high_ref[...], last_with_last, preferred_element_type=jnp.float32
    ) + lax.dot_general(chosen, low_ref[...], last_with_last, preferred_element_type=jnp.float32)


def source_kernel(dims, counts, rows_ref, applied_ref, weight_ref, chosen_ref, *refs):
    sensors, size_x, size_y, size_z = dims
    messages = sum(counts)
    column_ref, sum_ref, high_ref, low_ref = refs[messages : messages + 4]
    halo_refs = sort_halos(refs[:messages], refs[messages + 4 :], counts)
    sums = [jnp.zeros((sensors, size_z), jnp.float32) for _ in range(4)]
    for r in range(size_x * size_y):
        source = rows_ref[r * sensors : (r + 1) * sensors, :]
        applied = applied_ref[r * sensors : (r + 1) * sensors, :]
        twice = local_twice(dims, applied_ref, weight_ref, r)
        for k, product in enumerate(
            (source * source, source * applied, applied * applied, applied * twice)
        ):
            sums[k] = sums[k] + product
    for k in range(4):
        sum_ref[k * sensors : (k + 1) * sensors, :] = sums[k]
    column_ref[...] = select_columns(
        dims, rows_ref, weight_ref, halo_refs, chosen_ref, high_ref, low_ref
    )


def moment_kernel(dims, counts, applied_ref, weight_ref, sum_ref, *refs):
    sensors, size_x, size_y, size_z = dims
    messages = sum(counts)
    moment_ref = refs[messages]
    halo_refs = sort_halos(refs[:messages], refs[messages + 1 :], counts)
    (x_low, x_high), (y_low, y_high), (z_low, z_high) = halo_refs

    def part(ref, index):
        return ref[index * sensors : (index + 1) * sensors, :]

    def crossing(k, r, beside):
        x, y = divmod(r, size_y)
        return weight_ref[k, x, y : y + 1, :] * part(applied_ref, r) * beside

    zero = jnp.zeros((sensors, size_z), jnp.float32)
    outward, below, above = zero, zero, zero
    for y in range(size_y):
        outward = outward + crossing(0, y, part(x_low, y))
        outward = outward + crossing(1, (size_x - 1) * size_y + y, part(x_high, y))
    for x in range(size_x):
        outward = outward + crossing(2, x * size_y, part(y_low, x))
        outward = outward + crossing(3, x * size_y + size_y - 1, part(y_high, x))
    for r in range(size_x * size_y):
        below = below + crossing(4, r, z_low[0:sensors, r : r + 1])
        above = above + crossing(5, r, z_high[0:sensors, r : r + 1])
    lane_index = lax.broadcasted_iota(jnp.int32, zero.shape, 1)
    outward = outward + jnp.where(lane_index == 0, below, 0.0)
    outward = outward + jnp.where(lane_index == size_z - 1, above, 0.0)
    last = part(sum_ref, 3) - outward
    moment_ref[...] = lax.dot_general(
        jnp.ones((8, size_z), jnp.float32),
        jnp.concatenate([sum_ref[0 : 3 * sensors, :], last], axis=0),
        last_with_last,
        precision=lax.Precision.HIGHEST,
        preferred_element_type=jnp.float32,
    )


def payload_rows(sensors, slots_each):
    whole, rest = divmod(6 * sensors, lane_tile)
    fold = lane_tile // rest if rest else 0
    assert not fold or (fold * rest == lane_tile and slots_each % fold == 0)
    rows = whole * slots_each + (slots_each // fold if fold else 0)
    return whole, rest, fold, rows, -(-4 * sensors // lane_tile)


def applied_kernel(
    dims, counts, slots_each, applied_ref, weight_ref, chosen_ref, source_column_ref, *refs
):
    sensors, messages = dims[0], sum(counts)
    column_ref, high_ref, low_ref = refs[messages : messages + 3]
    halo_refs = sort_halos(refs[:messages], refs[messages + 3 :], counts)
    applied_columns = select_columns(
        dims, applied_ref, weight_ref, halo_refs, chosen_ref, high_ref, low_ref
    )
    columns = jnp.concatenate([source_column_ref[...], applied_columns], axis=1)
    whole, rest, fold, rows, moment_rows = payload_rows(sensors, slots_each)
    for owner in range(columns.shape[0] // slots_each):
        mine = slice(owner * slots_each, (owner + 1) * slots_each)
        at = owner * (rows + moment_rows)
        for tile in range(whole):
            column_ref[at : at + slots_each, :] = columns[mine, tile * lane_tile : (tile + 1) * lane_tile]
            at += slots_each
        if fold:
            part = slots_each // fold
            others = columns[mine, whole * lane_tile :]
            column_ref[at : at + part, :] = jnp.concatenate(
                [others[k * part : (k + 1) * part, :] for k in range(fold)], axis=1
            )
            at += part
        column_ref[at : at + moment_rows, :] = jnp.zeros((moment_rows, lane_tile), jnp.float32)


def owner_kernel(sensors, slots_each, received_ref, chosen_ref, data_ref, projection_ref, gram_ref):
    whole, rest, fold, rows, moment_rows = payload_rows(sensors, slots_each)
    each = rows + moment_rows
    sources = received_ref.shape[0] // each
    slots = sources * slots_each

    def collected(start, count):
        return jnp.concatenate(
            [received_ref[k * each + start : k * each + start + count, :] for k in range(sources)],
            axis=0,
        )

    gathered = jnp.zeros((moment_rows, lane_tile), jnp.float32)
    for k in range(sources):
        gathered = gathered + received_ref[k * each + rows : (k + 1) * each, :]
    moments = []
    sensor_index = lax.broadcasted_iota(jnp.int32, (sensors, lane_tile), 0)
    lane_index = lax.broadcasted_iota(jnp.int32, (sensors, lane_tile), 1)
    for k in range(4):
        total = jnp.zeros((sensors, 1), jnp.float32)
        for row in range(moment_rows):
            here = lane_index + row * lane_tile == sensor_index + k * sensors
            picked = jnp.where(here, gathered[row : row + 1, :], 0.0)
            total = total + jnp.sum(picked, axis=1, keepdims=True)
        moments.append(total)
    moment_zero, moment_one, moment_two, moment_three = moments
    first_step = moment_zero / moment_one
    residue = first_step * first_step * moment_two - moment_zero
    growth = 1.0 + residue / moment_zero
    curvature = (
        growth * growth * moment_one
        - 2.0 * growth * first_step * moment_two
        + first_step * first_step * moment_three
    )
    second_step = residue / curvature
    source_coef = first_step + second_step * growth
    applied_coef = second_step * first_step
    contract = (((0,), (0,)), ((), ()))

    def selected(values, first):
        chosen = chosen_ref[first : first + values.shape[0], :]
        high, low = halves(values)
        return lax.dot_general(
            high, chosen, contract, preferred_element_type=jnp.float32
        ) + lax.dot_general(low, chosen, contract, preferred_element_type=jnp.float32)

    owned = [
        selected(collected(tile * slots_each, slots_each), 0) for tile in range(whole)
    ]
    if fold:
        folded = collected(whole * slots_each, slots_each // fold)
        others = jnp.zeros((rest, chosen_ref.shape[1]), jnp.float32)
        for k in range(fold):
            found = selected(folded, slots + k * (slots // fold))
            others = others + found[k * rest : (k + 1) * rest, :]
        owned.append(others)
    owned = jnp.concatenate(owned, axis=0)
    lead = []
    for c in range(3):
        source_part = owned[c * sensors : (c + 1) * sensors, :]
        applied_part = owned[(3 + c) * sensors : (4 + c) * sensors, :]
        lead.append(source_coef * source_part - applied_coef * applied_part)
        projection_ref[c] = lax.dot_general(
            data_ref[...],
            lead[c],
            contract,
            precision=lax.Precision.HIGHEST,
            preferred_element_type=jnp.float32,
        )
    for k, (first, second) in enumerate(entry_pairs):
        gram_ref[k : k + 1, :] = jnp.sum(lead[first] * lead[second], axis=0, keepdims=True)


def call(body, **arguments):
    return pl.pallas_call(
        body, compiler_params=pltpu.CompilerParams(vmem_limit_bytes=vmem_grant), **arguments
    )


def in_hbm(count):
    return [pl.BlockSpec(memory_space=pltpu.HBM)] * count


def held_in_hbm(*arrays):
    return [pltpu.with_memory_space_constraint(a, pltpu.HBM) for a in arrays]


def in_vmem(count):
    return [pl.BlockSpec(memory_space=pltpu.VMEM)] * count


def face_shapes(dims, counts, with_labels):
    sensors, size_x, size_y, size_z = dims
    lanes = -(-size_x * size_y // lane_tile) * lane_tile
    shapes = (
        (size_y * (sensors + with_labels), size_z),
        (size_x * sensors + 8 * with_labels * -(-size_x // 8), size_z),
        (sensors + size_y * with_labels, lanes),
    )
    return [
        jax.ShapeDtypeStruct(shape, jnp.float32)
        for shape, count in zip(shapes, counts)
        for _ in range(count)
    ]


def per_device(source_term, labels, conductivity_table, send_map, owner_slots, sensor_data):
    dims = source_term.shape
    sensors, size_x, size_y, size_z = dims
    rows_count = size_x * size_y
    counts = face_counts()
    messages = sum(counts)
    owners = lax.axis_size("gx") * lax.axis_size("gy")
    slots = send_map.size
    slots_each = slots // owners
    _, _, fold, payload, moment_rows = payload_rows(sensors, slots_each)
    times = sensor_data.shape[1]
    positions = owner_slots.shape[0]

    voxels = rows_count * size_z

    def array(shape, dtype=jnp.float32):
        return jax.ShapeDtypeStruct(shape, dtype)

    def halves_scratch(rows):
        return [pltpu.VMEM((rows, voxels), jnp.bfloat16)] * 2

    field_shape = array((rows_count * sensors, size_z))
    packed = call(
        functools.partial(pack_kernel, dims, counts),
        out_shape=[field_shape, array(labels.shape)] + face_shapes(dims, counts, 1),
        in_specs=in_hbm(2),
        out_specs=in_vmem(2 + messages),
        scratch_shapes=[
            pltpu.VMEM((size_x, sensors, size_y, size_z), jnp.float32),
            pltpu.VMEM((size_x, size_y, size_z), jnp.int32),
            pltpu.SemaphoreType.DMA((size_x + 1,)),
        ],
        name="pack",
    )(*held_in_hbm(source_term, labels))
    rows, shifted, faces = packed[0], packed[1], packed[2:]
    source_halos = exchange_all(faces, counts)
    levels = conductivity_table.shape[0]
    chosen, owned_chosen, data, table = call(
        functools.partial(prepare_kernel, size_z, (slots_each, fold)),
        out_shape=[
            array((slots, voxels), jnp.bfloat16),
            array((slots * (2 if fold else 1), positions), jnp.bfloat16),
            array(sensor_data.shape),
            array((levels, size_y, size_z)),
        ],
        in_specs=in_hbm(4),
        out_specs=in_vmem(4),
        scratch_shapes=[
            pltpu.VMEM((1, slots), jnp.int32),
            pltpu.VMEM((1, positions), jnp.int32),
            pltpu.SMEM((levels,), jnp.float32),
            pltpu.SemaphoreType.DMA((4,)),
        ],
        name="prepare",
    )(
        *held_in_hbm(
            send_map.reshape(1, slots),
            owner_slots.reshape(1, positions),
            sensor_data,
            conductivity_table,
        )
    )

    result = call(
        functools.partial(apply_kernel, dims, counts),
        out_shape=[array((8, size_x, size_y, size_z)), field_shape] + face_shapes(dims, counts, 0),
        in_specs=in_vmem(3 + messages),
        out_specs=in_vmem(2 + messages),
        scratch_shapes=held_halos(source_halos, counts),
        name="apply",
    )(rows, shifted, table, *source_halos)
    weight, applied, faces = result[0], result[1], result[2:]
    applied_halos = exchange_all(faces, counts)

    source_columns, sums = call(
        functools.partial(source_kernel, dims, counts),
        out_shape=[array((slots, 3 * sensors)), array((4 * sensors, size_z))],
        in_specs=in_vmem(4 + messages),
        out_specs=in_vmem(2),
        scratch_shapes=halves_scratch(3 * sensors) + held_halos(source_halos, counts),
        name="source_columns",
    )(rows, applied, weight, chosen, *source_halos)
    moment = call(
        functools.partial(moment_kernel, dims, counts),
        out_shape=array((8, 4 * sensors)),
        in_specs=in_vmem(3 + messages),
        out_specs=in_vmem(1)[0],
        scratch_shapes=held_halos(applied_halos, counts),
        name="moments",
    )(applied, weight, sums, *applied_halos)
    moment = sum_over(moment, "gz")

    each = payload + moment_rows
    columns = call(
        functools.partial(applied_kernel, dims, counts, slots_each),
        out_shape=array((owners * each, lane_tile)),
        in_specs=in_vmem(4 + messages),
        out_specs=in_vmem(1)[0],
        scratch_shapes=halves_scratch(3 * sensors) + held_halos(applied_halos, counts),
        name="applied_columns",
    )(applied, weight, chosen, source_columns, *applied_halos)
    place = lax.broadcasted_iota(jnp.int32, columns.shape, 0) % each
    stamp = jnp.pad(moment[0], (0, moment_rows * lane_tile - 4 * sensors)).reshape(-1, lane_tile)
    for row in range(moment_rows):
        columns = jnp.where(place == payload + row, stamp[row : row + 1], columns)
    received = lax.all_to_all(
        columns.reshape(owners, 1, each * lane_tile), ("gx", "gy"), 0, 0, tiled=True
    ).reshape(columns.shape)
    return call(
        functools.partial(owner_kernel, sensors, slots_each),
        out_shape=[array((3, times, positions)), array((6, positions))],
        in_specs=in_vmem(3),
        out_specs=in_vmem(2),
        name="owner",
    )(received, owned_chosen, data)


def solution(mesh):
    in_specs = (
        P(None, "gx", "gy", "gz"),
        P("gx", "gy", "gz"),
        P(),
        P("gx", "gy", "gz", None),
        P(("gx", "gy", "gz")),
        P(),
    )
    out_specs = (P(None, None, ("gx", "gy", "gz")), P(None, ("gx", "gy", "gz")))
    step = jax.shard_map(
        per_device, mesh=mesh, in_specs=in_specs, out_specs=out_specs, check_vma=False
    )
    return lambda *arguments: tuple(step(*arguments))
```

```python
import functools

import jax
import jax.numpy as jnp
from jax import lax
from jax.experimental import pallas as pl
from jax.experimental.pallas import tpu as pltpu
from jax.sharding import PartitionSpec as P

mass_term = 0.25
lane_tile = 128
axes = ("gx", "gy", "gz")
vmem_grant = 16 << 20
last_with_last = (((1,), (1,)), ((), ()))
entry_pairs = ((0, 0), (1, 1), (2, 2), (0, 1), (0, 2), (1, 2))


def swap(value, axis, odd):
    count, beside = lax.axis_size(axis), lax.axis_size("gz")
    partner = {}
    for first in range(odd, count - 1, 2):
        partner[first], partner[first + 1] = first + 1, first
    alone = [i for i in range(count) if i not in partner]
    if alone and axis != "gz" and beside % 2 == 0:
        table = [
            (i * beside + k, partner[i] * beside + k if i in partner else i * beside + (k ^ 1))
            for i in range(count)
            for k in range(beside)
        ]
        return lax.ppermute(value, (axis, "gz"), table)
    for source, target in zip(alone, alone[::-1]):
        partner[source] = target
    return lax.ppermute(value, axis, sorted(partner.items()))


def sum_over(value, axis):
    count = lax.axis_size(axis)
    if count & (count - 1) == 0:
        tables = [[(i, i ^ d) for i in range(count)] for d in range(count - 1, 0, -1)]
    else:
        tables = [[(i, (i + d) % count) for i in range(count)] for d in range(count - 1, 0, -1)]
    return value + sum(lax.ppermute(value, axis, table) for table in tables)


def face_counts():
    return [1 if lax.axis_size(axis) <= 2 else 2 for axis in axes]


def exchange_all(faces, counts):
    halos = []
    for axis, group in zip(axes, split_refs(faces, counts)):
        if lax.axis_size(axis) > 1:
            group = [swap(face, axis, odd) for odd, face in enumerate(group)]
        halos.extend(group)
    return halos


def sort_halos(halo_refs, held_refs, counts):
    sorted_refs, held_refs = [], list(held_refs)
    for axis, group in zip(axes, split_refs(halo_refs, counts)):
        if len(group) == 1:
            sorted_refs.append((group[0], group[0]))
            continue
        even = lax.axis_index(axis) % 2 == 0
        below, above = held_refs.pop(0), held_refs.pop(0)
        first, second = group[0][...], group[1][...]
        below[...] = jnp.where(even, second, first)
        above[...] = jnp.where(even, first, second)
        sorted_refs.append((below, above))
    return sorted_refs


def held_halos(faces, counts):
    return [
        pltpu.VMEM(face.shape, face.dtype)
        for group in split_refs(faces, counts)
        for face in (group if len(group) == 2 else [])
    ]


def lanes_equal(shape, value):
    return lax.broadcasted_iota(jnp.int32, shape, len(shape) - 1) == value


def neighbour_flags():
    flags = []
    for axis in axes:
        index = lax.axis_index(axis)
        flags.append((index > 0, index < lax.axis_size(axis) - 1))
    return flags


def write_faces(dims, rows_ref, face_refs, z_ends, extra=None):
    sensors, size_x, size_y, size_z = dims
    x_refs, y_refs, z_refs = face_refs

    def field(r):
        return rows_ref[pl.ds(pl.multiple_of(r * sensors, sensors), sensors), :]

    def high_end(axis, number):
        return lax.axis_index(axis) % 2 == number

    for number, ref in enumerate(x_refs):
        high = high_end("gx", number)
        x = jnp.where(high, size_x - 1, 0)
        for y in range(size_y):
            ref[y * sensors : (y + 1) * sensors, :] = field(x * size_y + y)
        if extra is not None:
            ref[size_y * sensors : size_y * (sensors + 1), :] = jnp.where(high, extra[-1], extra[0])

    for number, ref in enumerate(y_refs):
        high = high_end("gy", number)
        y = jnp.where(high, size_y - 1, 0)
        for x in range(size_x):
            ref[x * sensors : (x + 1) * sensors, :] = field(x * size_y + y)
            if extra is not None:
                row = size_x * sensors + x
                ref[row : row + 1, :] = jnp.where(high, extra[x][size_y - 1 :, :], extra[x][0:1, :])

    ends = z_ends
    if extra is not None:
        ends = []
        for z, packed in zip((0, size_z - 1), z_ends):
            labels = jnp.zeros((size_y, packed.shape[1]), jnp.float32)
            for x in range(size_x):
                labels = jnp.where(lanes_equal(labels.shape, x), extra[x][:, z : z + 1], labels)
            ends.append(jnp.concatenate([packed, labels], axis=0))
    for number, ref in enumerate(z_refs):
        ref[...] = jnp.where(high_end("gz", number), ends[1], ends[0])


def pack_ends(dims, rows_ref, lanes):
    sensors, size_x, size_y, size_z = dims
    ends = []
    for z in (0, size_z - 1):
        packed = jnp.zeros((sensors, lanes), jnp.float32)
        for r in range(size_x * size_y):
            row = rows_ref[r * sensors : (r + 1) * sensors, :]
            packed = jnp.where(lanes_equal(packed.shape, r), row[:, z : z + 1], packed)
        ends.append(packed)
    return ends


def split_refs(refs, counts):
    groups, start = [], 0
    for count in counts:
        groups.append(refs[start : start + count])
        start += count
    return groups


def pack_kernel(dims, counts, source_ref, label_ref, *refs):
    sensors, size_x, size_y, size_z = dims
    small_hbm, refs = refs[:4], refs[4:]
    (rows_ref, shifted_ref, table_ref), small_refs = refs[:3], refs[3:6]
    face_refs = refs[6 : 6 + sum(counts)]
    staged_ref, label_vmem, level_ref, semaphores = refs[6 + sum(counts) :]
    copies = [
        pltpu.make_async_copy(source_ref.at[:, x], staged_ref.at[x], semaphores.at[x])
        for x in range(size_x)
    ]
    moves = [(label_ref, label_vmem), *zip(small_hbm, (*small_refs, level_ref))]
    for k, move in enumerate(moves):
        copies.append(pltpu.make_async_copy(*move, semaphores.at[size_x + k]))
    for copy in copies[size_x:] + copies[:size_x]:
        copy.start()
    for copy in copies[size_x:]:
        copy.wait()
    for level in range(level_ref.shape[0]):
        table_ref[level] = jnp.full(table_ref.shape[1:], level_ref[level], jnp.float32)
    shifted = [(label_vmem[x] + 1).astype(jnp.float32) for x in range(size_x)]
    for x in range(size_x):
        shifted_ref[x] = shifted[x]
    flat = staged_ref.reshape(size_x, sensors * size_y, size_z)
    for x in range(size_x):
        copies[x].wait()
        for y in range(size_y):
            r = x * size_y + y
            rows_ref[r * sensors : (r + 1) * sensors, :] = flat[x, pl.ds(y, sensors, stride=size_y), :]
    face_refs = split_refs(face_refs, counts)
    z_ends = pack_ends(dims, rows_ref, face_refs[2][0].shape[1])
    write_faces(dims, rows_ref, face_refs, z_ends, shifted)


def prepare_kernel(
    size_z, folding, voxel_ref, owned_ref, level_ref, chosen_ref, owned_chosen_ref, table_ref
):
    table_ref[...] = level_ref[...]
    slots, voxels = chosen_ref.shape
    square = (slots, slots)
    diagonal = lanes_equal(square, lax.broadcasted_iota(jnp.int32, square, 0))
    voxel = jnp.where(diagonal, voxel_ref[...].astype(jnp.float32), 0.0)
    voxel = jnp.sum(voxel, axis=1, keepdims=True).astype(jnp.int32)
    voxel = jnp.broadcast_to(voxel, (slots, size_z))
    row = voxel // size_z
    lane_index = lax.broadcasted_iota(jnp.int32, (slots, size_z), 1)
    lane = one_hot(lane_index == voxel - row * size_z)
    row = row.astype(jnp.float32).astype(jnp.bfloat16)
    none = jnp.zeros_like(lane)
    for r in range(voxels // size_z):
        chosen_ref[:, r * size_z : (r + 1) * size_z] = jnp.where(row == r, lane, none)
    row_index = lax.broadcasted_iota(jnp.int32, (slots, owned_ref.shape[1]), 0)
    owned_chosen_ref[0:slots, :] = one_hot(row_index == owned_ref[...])
    slots_each, fold = folding
    if fold:
        part = slots_each // fold
        row_index = lax.broadcasted_iota(jnp.int32, (slots // fold, owned_ref.shape[1]), 0)
        slot_index = row_index // part * slots_each + row_index % part
        for k in range(fold):
            first = slots + k * (slots // fold)
            owned_chosen_ref[first : first + slots // fold, :] = one_hot(
                slot_index + k * part == owned_ref[...]
            )


def one_hot(condition):
    return condition.astype(jnp.float32).astype(jnp.bfloat16)


def tissue(shifted, table_ref):
    conductivity = jnp.zeros_like(shifted)
    for level in range(table_ref.shape[0]):
        conductivity = jnp.where(shifted == level + 1, table_ref[level], conductivity)
    return conductivity, (shifted > 0).astype(jnp.float32)


def edge_weight(first, second):
    return 0.5 * (first[0] + second[0]) * first[1] * second[1]


def weights(dims, shifted_ref, table_ref, halo_refs, weight_ref):
    sensors, size_x, size_y, size_z = dims
    flags = neighbour_flags()
    (x_low, x_high), (y_low, y_high), (z_low, z_high) = halo_refs

    def masked(value, flag):
        return jnp.where(flag, value, 0.0)

    own = [shifted_ref[x] for x in range(size_x)]
    own_tissue = [tissue(plane, table_ref) for plane in own]
    x_rows = slice(size_y * sensors, size_y * (sensors + 1))
    below = tissue(masked(x_low[x_rows, :], flags[0][0]), table_ref)
    above = tissue(masked(x_high[x_rows, :], flags[0][1]), table_ref)
    planes = [below] + own_tissue + [above]
    across_x = [edge_weight(planes[i], planes[i + 1]) for i in range(size_x + 1)]
    row_index = lax.broadcasted_iota(jnp.int32, (size_y, size_z), 0)
    lane_index = lax.broadcasted_iota(jnp.int32, (size_y, size_z), 1)
    for x in range(size_x):
        y_row = size_x * sensors + x
        shifted = own[x]
        y_before = jnp.where(
            row_index == 0,
            masked(y_low[y_row : y_row + 1, :], flags[1][0]),
            pltpu.roll(shifted, 1, 0),
        )
        y_after = jnp.where(
            row_index == size_y - 1,
            masked(y_high[y_row : y_row + 1, :], flags[1][1]),
            pltpu.roll(shifted, size_y - 1, 0),
        )
        z_rows = slice(sensors, sensors + size_y)
        z_before = jnp.where(
            lane_index == 0,
            masked(z_low[z_rows, x : x + 1], flags[2][0]),
            pltpu.roll(shifted, 1, 1),
        )
        z_after = jnp.where(
            lane_index == size_z - 1,
            masked(z_high[z_rows, x : x + 1], flags[2][1]),
            pltpu.roll(shifted, size_z - 1, 1),
        )
        six = [across_x[x], across_x[x + 1]]
        for beside in (y_before, y_after, z_before, z_after):
            six.append(edge_weight(own_tissue[x], tissue(beside, table_ref)))
        for k, weight in enumerate(six):
            weight_ref[k, x] = weight
        weight_ref[6, x] = mass_term + (six[0] + six[1]) + (six[2] + six[3]) + (six[4] + six[5])
        weight_ref[7, x] = 0.5 * own_tissue[x][0]


def around(dims, rows_ref, halo_refs, r, flags=None):
    sensors, size_x, size_y, size_z = dims
    (x_low, x_high), (y_low, y_high), (z_low, z_high) = halo_refs
    x, y = divmod(r, size_y)

    def keep(value, dim, end):
        return value if flags is None else jnp.where(flags[dim][end], value, 0.0)

    def row(index):
        return rows_ref[index * sensors : (index + 1) * sensors, :]

    def part(ref, index):
        return ref[index * sensors : (index + 1) * sensors, :]

    centre = row(r)
    x_before = row(r - size_y) if x > 0 else keep(part(x_low, y), 0, 0)
    x_after = row(r + size_y) if x < size_x - 1 else keep(part(x_high, y), 0, 1)
    y_before = row(r - 1) if y > 0 else keep(part(y_low, x), 1, 0)
    y_after = row(r + 1) if y < size_y - 1 else keep(part(y_high, x), 1, 1)
    lane_index = lax.broadcasted_iota(jnp.int32, centre.shape, 1)
    z_before = jnp.where(
        lane_index == 0, keep(z_low[0:sensors, r : r + 1], 2, 0), pltpu.roll(centre, 1, 1)
    )
    z_after = jnp.where(
        lane_index == size_z - 1,
        keep(z_high[0:sensors, r : r + 1], 2, 1),
        pltpu.roll(centre, size_z - 1, 1),
    )
    return centre, (x_before, x_after, y_before, y_after, z_before, z_after)


def combine(weight_ref, x, y, centre, beside):
    total = weight_ref[6, x, y : y + 1, :] * centre
    for k, value in enumerate(beside):
        total = total - weight_ref[k, x, y : y + 1, :] * value
    return total


def apply_kernel(dims, counts, rows_ref, shifted_ref, table_ref, *refs):
    sensors, size_x, size_y, size_z = dims
    messages = sum(counts)
    halo_refs = sort_halos(refs[:messages], refs[2 * messages + 3 :], counts)
    weight_ref, end_ref, applied_ref = refs[messages : messages + 3]
    face_refs = split_refs(refs[messages + 3 : 2 * messages + 3], counts)
    weights(dims, shifted_ref, table_ref, halo_refs, weight_ref)
    for r in range(size_x * size_y):
        x, y = divmod(r, size_y)
        centre, beside = around(dims, rows_ref, halo_refs, r)
        applied_ref[r * sensors : (r + 1) * sensors, :] = combine(weight_ref, x, y, centre, beside)
    z_ends = pack_ends(dims, applied_ref, end_ref.shape[2])
    write_faces(dims, applied_ref, face_refs, z_ends)
    for end, (k, z) in enumerate(((4, 0), (5, size_z - 1))):
        packed = jnp.zeros((size_y, end_ref.shape[2]), jnp.float32)
        row_index = lax.broadcasted_iota(jnp.int32, packed.shape, 0)
        for x in range(size_x):
            here = lanes_equal(packed.shape, row_index + x * size_y)
            packed = jnp.where(here, weight_ref[k, x][:, z : z + 1], packed)
        end_ref[end] = jnp.sum(packed, axis=0, keepdims=True) * z_ends[end]


def halves(value):
    high = value.astype(jnp.bfloat16)
    return high, (value - high.astype(jnp.float32)).astype(jnp.bfloat16)


def local_twice(dims, rows_ref, weight_ref, r):
    sensors, size_x, size_y, size_z = dims
    x, y = divmod(r, size_y)

    def row(index):
        return rows_ref[index * sensors : (index + 1) * sensors, :]

    def weight(k):
        return weight_ref[k, x, y : y + 1, :]

    centre = row(r)
    lane_index = lax.broadcasted_iota(jnp.int32, centre.shape, 1)
    total = weight(6) * centre
    if x > 0:
        total = total - weight(0) * row(r - size_y)
    if x < size_x - 1:
        total = total - weight(1) * row(r + size_y)
    if y > 0:
        total = total - weight(2) * row(r - 1)
    if y < size_y - 1:
        total = total - weight(3) * row(r + 1)
    before = jnp.where(lane_index == 0, 0.0, pltpu.roll(centre, 1, 1))
    after = jnp.where(lane_index == size_z - 1, 0.0, pltpu.roll(centre, size_z - 1, 1))
    return total - weight(4) * before - weight(5) * after


def select_columns(dims, rows_ref, weight_ref, halo_refs, chosen_ref, parts_ref):
    sensors, size_x, size_y, size_z = dims
    flags = neighbour_flags()
    width = 3 * sensors
    for r in range(size_x * size_y):
        x, y = divmod(r, size_y)
        span = slice(r * size_z, (r + 1) * size_z)
        scale = weight_ref[7, x, y : y + 1, :]
        _, beside = around(dims, rows_ref, halo_refs, r, flags)
        for c in range(3):
            high, low = halves(scale * (beside[2 * c + 1] - beside[2 * c]))
            parts_ref[c * sensors : (c + 1) * sensors, span] = high
            parts_ref[width + c * sensors : width + (c + 1) * sensors, span] = low
    found = lax.dot_general(
        chosen_ref[...], parts_ref[...], last_with_last, preferred_element_type=jnp.float32
    )
    return found[:, :width] + found[:, width:]


def source_kernel(dims, counts, rows_ref, applied_ref, weight_ref, chosen_ref, *refs):
    sensors, size_x, size_y, size_z = dims
    messages = sum(counts)
    column_ref, sum_ref, parts_ref = refs[messages : messages + 3]
    halo_refs = sort_halos(refs[:messages], refs[messages + 3 :], counts)
    sums = [jnp.zeros((sensors, size_z), jnp.float32) for _ in range(4)]
    for r in range(size_x * size_y):
        source = rows_ref[r * sensors : (r + 1) * sensors, :]
        applied = applied_ref[r * sensors : (r + 1) * sensors, :]
        twice = local_twice(dims, applied_ref, weight_ref, r)
        for k, product in enumerate(
            (source * source, source * applied, applied * applied, applied * twice)
        ):
            sums[k] = sums[k] + product
    for k in range(4):
        sum_ref[k * sensors : (k + 1) * sensors, :] = sums[k]
    column_ref[...] = select_columns(
        dims, rows_ref, weight_ref, halo_refs, chosen_ref, parts_ref
    )


def moment_kernel(dims, counts, applied_ref, weight_ref, sum_ref, end_ref, *refs):
    sensors, size_x, size_y, size_z = dims
    messages = sum(counts)
    moment_ref = refs[messages]
    halo_refs = sort_halos(refs[:messages], refs[messages + 1 :], counts)
    (x_low, x_high), (y_low, y_high), (z_low, z_high) = halo_refs

    def part(ref, index):
        return ref[index * sensors : (index + 1) * sensors, :]

    def crossing(k, r, beside):
        x, y = divmod(r, size_y)
        return weight_ref[k, x, y : y + 1, :] * part(applied_ref, r) * beside

    outward = jnp.zeros((sensors, size_z), jnp.float32)
    for y in range(size_y):
        outward = outward + crossing(0, y, part(x_low, y))
        outward = outward + crossing(1, (size_x - 1) * size_y + y, part(x_high, y))
    for x in range(size_x):
        outward = outward + crossing(2, x * size_y, part(y_low, x))
        outward = outward + crossing(3, x * size_y + size_y - 1, part(y_high, x))
    crossed = end_ref[0] * z_low[0:sensors, :] + end_ref[1] * z_high[0:sensors, :]
    for first in range(0, crossed.shape[1], size_z):
        piece = crossed[:, first : first + size_z]
        spare = size_z - piece.shape[1]
        if spare:
            piece = jnp.concatenate([piece, jnp.zeros((sensors, spare), jnp.float32)], axis=1)
        outward = outward + piece
    last = part(sum_ref, 3) - outward
    moment_ref[...] = lax.dot_general(
        jnp.ones((8, size_z), jnp.float32),
        jnp.concatenate([sum_ref[0 : 3 * sensors, :], last], axis=0),
        last_with_last,
        precision=lax.Precision.HIGHEST,
        preferred_element_type=jnp.float32,
    )


def payload_rows(sensors, slots_each):
    whole, rest = divmod(6 * sensors, lane_tile)
    fold = lane_tile // rest if rest else 0
    assert not fold or (fold * rest == lane_tile and slots_each % fold == 0)
    rows = whole * slots_each + (slots_each // fold if fold else 0)
    return whole, rest, fold, rows, -(-4 * sensors // lane_tile)


def applied_kernel(
    dims, counts, slots_each, applied_ref, weight_ref, chosen_ref, source_column_ref, *refs
):
    sensors, messages = dims[0], sum(counts)
    column_ref, parts_ref = refs[messages : messages + 2]
    halo_refs = sort_halos(refs[:messages], refs[messages + 2 :], counts)
    applied_columns = select_columns(
        dims, applied_ref, weight_ref, halo_refs, chosen_ref, parts_ref
    )
    columns = jnp.concatenate([source_column_ref[...], applied_columns], axis=1)
    whole, rest, fold, rows, moment_rows = payload_rows(sensors, slots_each)
    for owner in range(columns.shape[0] // slots_each):
        mine = slice(owner * slots_each, (owner + 1) * slots_each)
        at = owner * (rows + moment_rows)
        for tile in range(whole):
            column_ref[at : at + slots_each, :] = columns[mine, tile * lane_tile : (tile + 1) * lane_tile]
            at += slots_each
        if fold:
            part = slots_each // fold
            others = columns[mine, whole * lane_tile :]
            column_ref[at : at + part, :] = jnp.concatenate(
                [others[k * part : (k + 1) * part, :] for k in range(fold)], axis=1
            )
            at += part
        column_ref[at : at + moment_rows, :] = jnp.zeros((moment_rows, lane_tile), jnp.float32)


def owner_kernel(sensors, slots_each, received_ref, chosen_ref, data_ref, projection_ref, gram_ref):
    whole, rest, fold, rows, moment_rows = payload_rows(sensors, slots_each)
    each = rows + moment_rows
    sources = received_ref.shape[0] // each
    slots = sources * slots_each

    def collected(start, count):
        return jnp.concatenate(
            [received_ref[k * each + start : k * each + start + count, :] for k in range(sources)],
            axis=0,
        )

    gathered = jnp.zeros((moment_rows, lane_tile), jnp.float32)
    for k in range(sources):
        gathered = gathered + received_ref[k * each + rows : (k + 1) * each, :]
    moments = []
    sensor_index = lax.broadcasted_iota(jnp.int32, (sensors, lane_tile), 0)
    lane_index = lax.broadcasted_iota(jnp.int32, (sensors, lane_tile), 1)
    for k in range(4):
        total = jnp.zeros((sensors, 1), jnp.float32)
        for row in range(moment_rows):
            here = lane_index + row * lane_tile == sensor_index + k * sensors
            picked = jnp.where(here, gathered[row : row + 1, :], 0.0)
            total = total + jnp.sum(picked, axis=1, keepdims=True)
        moments.append(total)
    moment_zero, moment_one, moment_two, moment_three = moments
    first_step = moment_zero / moment_one
    residue = first_step * first_step * moment_two - moment_zero
    growth = 1.0 + residue / moment_zero
    curvature = (
        growth * growth * moment_one
        - 2.0 * growth * first_step * moment_two
        + first_step * first_step * moment_three
    )
    second_step = residue / curvature
    source_coef = first_step + second_step * growth
    applied_coef = second_step * first_step
    contract = (((0,), (0,)), ((), ()))

    def selected(values, first):
        chosen = chosen_ref[first : first + values.shape[0], :]
        high, low = halves(values)
        return lax.dot_general(
            high, chosen, contract, preferred_element_type=jnp.float32
        ) + lax.dot_general(low, chosen, contract, preferred_element_type=jnp.float32)

    owned = [
        selected(collected(tile * slots_each, slots_each), 0) for tile in range(whole)
    ]
    if fold:
        folded = collected(whole * slots_each, slots_each // fold)
        others = jnp.zeros((rest, chosen_ref.shape[1]), jnp.float32)
        for k in range(fold):
            found = selected(folded, slots + k * (slots // fold))
            others = others + found[k * rest : (k + 1) * rest, :]
        owned.append(others)
    owned = jnp.concatenate(owned, axis=0)
    lead = []
    for c in range(3):
        source_part = owned[c * sensors : (c + 1) * sensors, :]
        applied_part = owned[(3 + c) * sensors : (4 + c) * sensors, :]
        lead.append(source_coef * source_part - applied_coef * applied_part)
        projection_ref[c] = lax.dot_general(
            data_ref[...],
            lead[c],
            contract,
            precision=lax.Precision.HIGHEST,
            preferred_element_type=jnp.float32,
        )
    for k, (first, second) in enumerate(entry_pairs):
        gram_ref[k : k + 1, :] = jnp.sum(lead[first] * lead[second], axis=0, keepdims=True)


def call(body, **arguments):
    return pl.pallas_call(
        body, compiler_params=pltpu.CompilerParams(vmem_limit_bytes=vmem_grant), **arguments
    )


def in_hbm(count):
    return [pl.BlockSpec(memory_space=pltpu.HBM)] * count


def held_in_hbm(*arrays):
    return [pltpu.with_memory_space_constraint(a, pltpu.HBM) for a in arrays]


def in_vmem(count):
    return [pl.BlockSpec(memory_space=pltpu.VMEM)] * count


def face_shapes(dims, counts, with_labels):
    sensors, size_x, size_y, size_z = dims
    lanes = -(-size_x * size_y // lane_tile) * lane_tile
    shapes = (
        (size_y * (sensors + with_labels), size_z),
        (size_x * sensors + 8 * with_labels * -(-size_x // 8), size_z),
        (sensors + size_y * with_labels, lanes),
    )
    return [
        jax.ShapeDtypeStruct(shape, jnp.float32)
        for shape, count in zip(shapes, counts)
        for _ in range(count)
    ]


def per_device(source_term, labels, conductivity_table, send_map, owner_slots, sensor_data):
    dims = source_term.shape
    sensors, size_x, size_y, size_z = dims
    rows_count = size_x * size_y
    counts = face_counts()
    messages = sum(counts)
    owners = lax.axis_size("gx") * lax.axis_size("gy")
    slots = send_map.size
    slots_each = slots // owners
    _, _, fold, payload, moment_rows = payload_rows(sensors, slots_each)
    times = sensor_data.shape[1]
    positions = owner_slots.shape[0]

    voxels = rows_count * size_z

    def array(shape, dtype=jnp.float32):
        return jax.ShapeDtypeStruct(shape, dtype)

    parts = [pltpu.VMEM((6 * sensors, voxels), jnp.bfloat16)]
    field_shape = array((rows_count * sensors, size_z))
    levels = conductivity_table.shape[0]
    small = (
        send_map.reshape(1, slots),
        owner_slots.reshape(1, positions),
        sensor_data,
        conductivity_table,
    )
    packed = call(
        functools.partial(pack_kernel, dims, counts),
        out_shape=[field_shape, array(labels.shape), array((levels, size_y, size_z))]
        + [array(value.shape, value.dtype) for value in small[:3]]
        + face_shapes(dims, counts, 1),
        in_specs=in_hbm(6),
        out_specs=in_vmem(6 + messages),
        scratch_shapes=[
            pltpu.VMEM((size_x, sensors, size_y, size_z), jnp.float32),
            pltpu.VMEM((size_x, size_y, size_z), jnp.int32),
            pltpu.SMEM((levels,), jnp.float32),
            pltpu.SemaphoreType.DMA((size_x + 5,)),
        ],
        name="pack",
    )(*held_in_hbm(source_term, labels, *small))
    rows, shifted, table, voxel, owned, data, *faces = packed
    source_halos = exchange_all(faces, counts)
    chosen, owned_chosen, table = call(
        functools.partial(prepare_kernel, size_z, (slots_each, fold)),
        out_shape=[
            array((slots, voxels), jnp.bfloat16),
            array((slots * (2 if fold else 1), positions), jnp.bfloat16),
            array(table.shape),
        ],
        in_specs=in_vmem(3),
        out_specs=in_vmem(3),
        name="prepare",
    )(voxel, owned, table)

    faces_out = face_shapes(dims, counts, 0)
    end_shape = (2, *faces_out[-1].shape)
    result = call(
        functools.partial(apply_kernel, dims, counts),
        out_shape=[array((8, size_x, size_y, size_z)), array(end_shape), field_shape] + faces_out,
        in_specs=in_vmem(3 + messages),
        out_specs=in_vmem(3 + messages),
        scratch_shapes=held_halos(source_halos, counts),
        name="apply",
    )(rows, shifted, table, *source_halos)
    weight, ends, applied, faces = *result[:3], result[3:]
    applied_halos = exchange_all(faces, counts)

    source_columns, sums = call(
        functools.partial(source_kernel, dims, counts),
        out_shape=[array((slots, 3 * sensors)), array((4 * sensors, size_z))],
        in_specs=in_vmem(4 + messages),
        out_specs=in_vmem(2),
        scratch_shapes=parts + held_halos(source_halos, counts),
        name="source_columns",
    )(rows, applied, weight, chosen, *source_halos)
    moment = call(
        functools.partial(moment_kernel, dims, counts),
        out_shape=array((8, 4 * sensors)),
        in_specs=in_vmem(4 + messages),
        out_specs=in_vmem(1)[0],
        scratch_shapes=held_halos(applied_halos, counts),
        name="moments",
    )(applied, weight, sums, ends, *applied_halos)
    moment = sum_over(moment, "gz")

    each = payload + moment_rows
    columns = call(
        functools.partial(applied_kernel, dims, counts, slots_each),
        out_shape=array((owners * each, lane_tile)),
        in_specs=in_vmem(4 + messages),
        out_specs=in_vmem(1)[0],
        scratch_shapes=parts + held_halos(applied_halos, counts),
        name="applied_columns",
    )(applied, weight, chosen, source_columns, *applied_halos)
    place = lax.broadcasted_iota(jnp.int32, columns.shape, 0) % each
    stamp = jnp.pad(moment[0], (0, moment_rows * lane_tile - 4 * sensors)).reshape(-1, lane_tile)
    for row in range(moment_rows):
        columns = jnp.where(place == payload + row, stamp[row : row + 1], columns)
    received = lax.all_to_all(
        columns.reshape(owners, 1, each * lane_tile), ("gx", "gy"), 0, 0, tiled=True
    ).reshape(columns.shape)
    return call(
        functools.partial(owner_kernel, sensors, slots_each),
        out_shape=[array((3, times, positions)), array((6, positions))],
        in_specs=in_vmem(3),
        out_specs=in_vmem(2),
        name="owner",
    )(received, owned_chosen, data)


def solution(mesh):
    in_specs = (
        P(None, "gx", "gy", "gz"),
        P("gx", "gy", "gz"),
        P(),
        P("gx", "gy", "gz", None),
        P(("gx", "gy", "gz")),
        P(),
    )
    out_specs = (P(None, None, ("gx", "gy", "gz")), P(None, ("gx", "gy", "gz")))
    step = jax.shard_map(
        per_device, mesh=mesh, in_specs=in_specs, out_specs=out_specs, check_vma=False
    )
    return lambda *arguments: tuple(step(*arguments))
```

```python
import functools

import jax
import jax.numpy as jnp
from jax import lax
from jax.experimental import pallas as pl
from jax.experimental.pallas import tpu as pltpu
from jax.sharding import PartitionSpec as P

mass_term = 0.25
lane_tile = 128
axes = ("gx", "gy", "gz")
vmem_grant = 16 << 20
last_with_last = (((1,), (1,)), ((), ()))
entry_pairs = ((0, 0), (1, 1), (2, 2), (0, 1), (0, 2), (1, 2))


def swap(value, axis, odd):
    count, beside = lax.axis_size(axis), lax.axis_size("gz")
    partner = {}
    for first in range(odd, count - 1, 2):
        partner[first], partner[first + 1] = first + 1, first
    alone = [i for i in range(count) if i not in partner]
    if alone and axis != "gz" and beside % 2 == 0:
        table = [
            (i * beside + k, partner[i] * beside + k if i in partner else i * beside + (k ^ 1))
            for i in range(count)
            for k in range(beside)
        ]
        return lax.ppermute(value, (axis, "gz"), table)
    for source, target in zip(alone, alone[::-1]):
        partner[source] = target
    return lax.ppermute(value, axis, sorted(partner.items()))


def sum_over(value, axis):
    count = lax.axis_size(axis)
    if count & (count - 1) == 0:
        tables = [[(i, i ^ d) for i in range(count)] for d in range(count - 1, 0, -1)]
    else:
        tables = [[(i, (i + d) % count) for i in range(count)] for d in range(count - 1, 0, -1)]
    return value + sum(lax.ppermute(value, axis, table) for table in tables)


def face_counts():
    return [1 if lax.axis_size(axis) <= 2 else 2 for axis in axes]


def exchange_all(groups):
    halos = []
    for axis, group in zip(axes, groups):
        if lax.axis_size(axis) > 1:
            group = [swap(face, axis, odd) for odd, face in enumerate(group)]
        halos.extend(group)
    return halos


def sort_halos(halo_refs, held_refs, counts):
    sorted_refs, held_refs = [], list(held_refs)
    for axis, group in zip(axes, split_refs(halo_refs, counts[:2])):
        if len(group) == 1:
            sorted_refs.append((group[0], group[0]))
            continue
        even = lax.axis_index(axis) % 2 == 0
        below, above = held_refs.pop(0), held_refs.pop(0)
        first, second = group[0][...], group[1][...]
        below[...] = jnp.where(even, second, first)
        above[...] = jnp.where(even, first, second)
        sorted_refs.append((below, above))
    return sorted_refs


def sort_ends(z_refs):
    below = above = z_refs[0][...]
    if len(z_refs) == 2:
        even = lax.axis_index("gz") % 2 == 0
        below, above = (
            jnp.where(even, z_refs[1 - k][...], z_refs[k][...]) for k in range(2)
        )
    half = below.shape[1] // 2
    lane_index = lax.broadcasted_iota(jnp.int32, below.shape, 1)
    return pltpu.roll(jnp.where(lane_index < half, above, below), half, 1)


def held_halos(faces, counts):
    return [
        pltpu.VMEM(face.shape, face.dtype)
        for group in split_refs(faces, counts[:2])
        for face in (group if len(group) == 2 else [])
    ]


def lanes_equal(shape, value):
    return lax.broadcasted_iota(jnp.int32, shape, len(shape) - 1) == value


def neighbour_flags():
    flags = []
    for axis in axes:
        index = lax.axis_index(axis)
        flags.append((index > 0, index < lax.axis_size(axis) - 1))
    return flags


def write_faces(dims, rows_ref, face_refs, labels=None, beyond=None):
    sensors, size_x, size_y, size_z = dims
    x_refs, y_refs = face_refs

    def field(r):
        return rows_ref[pl.ds(pl.multiple_of(r * sensors, sensors), sensors), :]

    def high_end(axis, number):
        return lax.axis_index(axis) % 2 == number

    for number, ref in enumerate(x_refs):
        high = high_end("gx", number)
        x = jnp.where(high, size_x - 1, 0)
        for y in range(size_y):
            ref[y * sensors : (y + 1) * sensors, :] = field(x * size_y + y)
        if labels is not None:
            ref[size_y * sensors :, :] = jnp.where(high, labels[-1], labels[0])
        else:
            ref[size_y * sensors :, :] = beyond

    for number, ref in enumerate(y_refs):
        high = high_end("gy", number)
        y = jnp.where(high, size_y - 1, 0)
        for x in range(size_x):
            ref[x * sensors : (x + 1) * sensors, :] = field(x * size_y + y)
            if labels is not None:
                row = size_x * sensors + x
                ref[row : row + 1, :] = jnp.where(high, labels[x][size_y - 1 :, :], labels[x][0:1, :])
        if labels is None:
            ref[size_x * sensors :, :] = beyond


def put_lanes(packed, row, source, target, count):
    lanes = packed.shape[1]
    moved = pltpu.roll(row, (target - source) % lanes, 1)
    lane_index = lax.broadcasted_iota(jnp.int32, packed.shape, 1)
    return jnp.where((lane_index >= target) & (lane_index < target + count), moved, packed)


def pack_lines(dims, values, depth, low_shift):
    size_x, size_y, size_z = dims[1:]
    half = size_z // 2
    packed = jnp.zeros((size_y, size_z), jnp.float32)
    row_index = lax.broadcasted_iota(jnp.int32, packed.shape, 0)
    for x in range(size_x):
        line = 2 * (x * size_y + row_index)
        for p in range(depth):
            low, high = values[x]
            end = size_z - depth + p
            packed = jnp.where(lanes_equal(packed.shape, line + low_shift + p), low[:, p : p + 1], packed)
            packed = jnp.where(lanes_equal(packed.shape, line + half + p), high[:, end : end + 1], packed)
    return jnp.broadcast_to(jnp.sum(packed, axis=0, keepdims=True), (8, size_z))


def pack_rows(dims, rows_ref, depth, low_shift):
    sensors, size_x, size_y, size_z = dims
    half = size_z // 2
    assert 2 * size_x * size_y <= half
    packed = jnp.zeros((sensors, size_z), jnp.float32)
    for r in range(size_x * size_y):
        row = rows_ref[r * sensors : (r + 1) * sensors, :]
        packed = put_lanes(packed, row, 0, 2 * r + low_shift, depth)
        packed = put_lanes(packed, row, size_z - depth, half + 2 * r, depth)
    return packed


def split_refs(refs, counts):
    groups, start = [], 0
    for count in counts:
        groups.append(refs[start : start + count])
        start += count
    return groups


def pack_kernel(dims, counts, source_ref, label_ref, *refs):
    sensors, size_x, size_y, size_z = dims
    small_hbm, refs = refs[:4], refs[4:]
    (rows_ref, shifted_ref, table_ref), small_refs = refs[:3], refs[3:6]
    own_ref, refs = refs[6], refs[7:]
    face_refs = split_refs(refs[: sum(counts[:2])], counts[:2])
    staged_ref, label_vmem, level_ref, semaphores = refs[sum(counts[:2]) :]
    copies = [
        pltpu.make_async_copy(source_ref.at[:, x], staged_ref.at[x], semaphores.at[x])
        for x in range(size_x)
    ]
    moves = [(label_ref, label_vmem), *zip(small_hbm, (*small_refs, level_ref))]
    for k, move in enumerate(moves):
        copies.append(pltpu.make_async_copy(*move, semaphores.at[size_x + k]))
    for copy in copies[size_x:] + copies[:size_x]:
        copy.start()
    for copy in copies[size_x:]:
        copy.wait()
    for level in range(level_ref.shape[0]):
        table_ref[level] = jnp.full(table_ref.shape[1:], level_ref[level], jnp.float32)
    shifted = [(label_vmem[x] + 1).astype(jnp.float32) for x in range(size_x)]
    for x in range(size_x):
        shifted_ref[x] = shifted[x]
    flat = staged_ref.reshape(size_x, sensors * size_y, size_z)
    for x in range(size_x):
        copies[x].wait()
        for y in range(size_y):
            r = x * size_y + y
            rows_ref[r * sensors : (r + 1) * sensors, :] = flat[x, pl.ds(y, sensors, stride=size_y), :]
    write_faces(dims, rows_ref, face_refs, labels=shifted)
    own_ref[0:sensors, :] = pack_rows(dims, rows_ref, 2, 0)
    own_ref[sensors:, :] = pack_lines(dims, [(plane, plane) for plane in shifted], 2, 0)


def prepare_kernel(
    size_z, folding, voxel_ref, owned_ref, level_ref, chosen_ref, owned_chosen_ref, table_ref
):
    table_ref[...] = level_ref[...]
    slots, voxels = chosen_ref.shape
    square = (slots, slots)
    diagonal = lanes_equal(square, lax.broadcasted_iota(jnp.int32, square, 0))
    voxel = jnp.where(diagonal, voxel_ref[...].astype(jnp.float32), 0.0)
    voxel = jnp.sum(voxel, axis=1, keepdims=True).astype(jnp.int32)
    voxel = jnp.broadcast_to(voxel, (slots, size_z))
    row = voxel // size_z
    lane_index = lax.broadcasted_iota(jnp.int32, (slots, size_z), 1)
    lane = one_hot(lane_index == voxel - row * size_z)
    row = row.astype(jnp.float32).astype(jnp.bfloat16)
    none = jnp.zeros_like(lane)
    for r in range(voxels // size_z):
        chosen_ref[:, r * size_z : (r + 1) * size_z] = jnp.where(row == r, lane, none)
    row_index = lax.broadcasted_iota(jnp.int32, (slots, owned_ref.shape[1]), 0)
    owned_chosen_ref[0:slots, :] = one_hot(row_index == owned_ref[...])
    slots_each, fold = folding
    if fold:
        part = slots_each // fold
        row_index = lax.broadcasted_iota(jnp.int32, (slots // fold, owned_ref.shape[1]), 0)
        slot_index = row_index // part * slots_each + row_index % part
        for k in range(fold):
            first = slots + k * (slots // fold)
            owned_chosen_ref[first : first + slots // fold, :] = one_hot(
                slot_index + k * part == owned_ref[...]
            )


def one_hot(condition):
    return condition.astype(jnp.float32).astype(jnp.bfloat16)


def tissue(shifted, table_ref):
    conductivity = jnp.zeros_like(shifted)
    for level in range(table_ref.shape[0]):
        value = table_ref[level] if shifted.shape == table_ref.shape[1:] else table_ref[level, 0:1, 0:1]
        conductivity = jnp.where(shifted == level + 1, value, conductivity)
    return conductivity, (shifted > 0).astype(jnp.float32)


def edge_weight(first, second):
    return 0.5 * (first[0] + second[0]) * first[1] * second[1]


def weights(dims, shifted_ref, table_ref, halo_refs, z_ref, weight_ref):
    sensors, size_x, size_y, size_z = dims
    flags = neighbour_flags()
    (x_low, x_high), (y_low, y_high) = halo_refs
    beyond = z_ref[sensors : sensors + 1, :]
    half = size_z // 2

    def beyond_end(x, first, flag):
        line = 2 * (x * size_y + row_index) + first
        picked = jnp.where(lanes_equal(row_index.shape, line), beyond, 0.0)
        return masked(jnp.sum(picked, axis=1, keepdims=True), flag)

    def masked(value, flag):
        return jnp.where(flag, value, 0.0)

    own = [shifted_ref[x] for x in range(size_x)]
    own_tissue = [tissue(plane, table_ref) for plane in own]
    x_rows = slice(size_y * sensors, size_y * (sensors + 1))
    below = tissue(masked(x_low[x_rows, :], flags[0][0]), table_ref)
    above = tissue(masked(x_high[x_rows, :], flags[0][1]), table_ref)
    planes = [below] + own_tissue + [above]
    across_x = [edge_weight(planes[i], planes[i + 1]) for i in range(size_x + 1)]
    row_index = lax.broadcasted_iota(jnp.int32, (size_y, size_z), 0)
    lane_index = lax.broadcasted_iota(jnp.int32, (size_y, size_z), 1)
    for x in range(size_x):
        y_row = size_x * sensors + x
        shifted = own[x]
        y_before = jnp.where(
            row_index == 0,
            masked(y_low[y_row : y_row + 1, :], flags[1][0]),
            pltpu.roll(shifted, 1, 0),
        )
        y_after = jnp.where(
            row_index == size_y - 1,
            masked(y_high[y_row : y_row + 1, :], flags[1][1]),
            pltpu.roll(shifted, size_y - 1, 0),
        )
        z_before = jnp.where(
            lane_index == 0,
            beyond_end(x, 1, flags[2][0]),
            pltpu.roll(shifted, 1, 1),
        )
        z_after = jnp.where(
            lane_index == size_z - 1,
            beyond_end(x, half, flags[2][1]),
            pltpu.roll(shifted, size_z - 1, 1),
        )
        six = [across_x[x], across_x[x + 1]]
        for beside in (y_before, y_after, z_before, z_after):
            six.append(edge_weight(own_tissue[x], tissue(beside, table_ref)))
        for k, weight in enumerate(six):
            weight_ref[k, x] = weight
        weight_ref[6, x] = mass_term + (six[0] + six[1]) + (six[2] + six[3]) + (six[4] + six[5])
        weight_ref[7, x] = 0.5 * own_tissue[x][0]


def around(dims, rows_ref, halo_refs, z_ref, r, flags=None):
    sensors, size_x, size_y, size_z = dims
    (x_low, x_high), (y_low, y_high) = halo_refs
    x, y = divmod(r, size_y)
    z_low = z_ref[0:sensors, 2 * r + 1 : 2 * r + 2]
    high_lane = size_z // 2 + 2 * r
    z_high = z_ref[0:sensors, high_lane : high_lane + 1]

    def keep(value, dim, end):
        return value if flags is None else jnp.where(flags[dim][end], value, 0.0)

    def row(index):
        return rows_ref[index * sensors : (index + 1) * sensors, :]

    def part(ref, index):
        return ref[index * sensors : (index + 1) * sensors, :]

    centre = row(r)
    x_before = row(r - size_y) if x > 0 else keep(part(x_low, y), 0, 0)
    x_after = row(r + size_y) if x < size_x - 1 else keep(part(x_high, y), 0, 1)
    y_before = row(r - 1) if y > 0 else keep(part(y_low, x), 1, 0)
    y_after = row(r + 1) if y < size_y - 1 else keep(part(y_high, x), 1, 1)
    lane_index = lax.broadcasted_iota(jnp.int32, centre.shape, 1)
    z_before = jnp.where(
        lane_index == 0, keep(z_low, 2, 0), pltpu.roll(centre, 1, 1)
    )
    z_after = jnp.where(
        lane_index == size_z - 1,
        keep(z_high, 2, 1),
        pltpu.roll(centre, size_z - 1, 1),
    )
    return centre, (x_before, x_after, y_before, y_after, z_before, z_after)


def combine(weight_ref, x, y, centre, beside):
    total = weight_ref[6, x, y : y + 1, :] * centre
    for k, value in enumerate(beside):
        total = total - weight_ref[k, x, y : y + 1, :] * value
    return total


def apply_kernel(dims, counts, rows_ref, shifted_ref, table_ref, *refs):
    sensors, size_x, size_y, size_z = dims
    message_refs, refs = refs[: sum(counts)], refs[sum(counts) :]
    weight_ref, end_ref, applied_ref, z_ref = refs[:4]
    face_refs = split_refs(refs[4 : 4 + sum(counts[:2])], counts[:2])
    halo_refs = sort_halos(message_refs, refs[4 + sum(counts[:2]) :], counts)
    z_ref[...] = sort_ends(message_refs[sum(counts[:2]) :])
    weights(dims, shifted_ref, table_ref, halo_refs, z_ref, weight_ref)
    for r in range(size_x * size_y):
        x, y = divmod(r, size_y)
        centre, beside = around(dims, rows_ref, halo_refs, z_ref, r)
        applied_ref[r * sensors : (r + 1) * sensors, :] = combine(weight_ref, x, y, centre, beside)
    write_faces(dims, applied_ref, face_refs, beyond=z_ref[...])
    lines = [(weight_ref[4, x], weight_ref[5, x]) for x in range(size_x)]
    outward = pack_lines(dims, lines, 1, 1)
    end_ref[...] = outward[0:1, :] * pack_rows(dims, applied_ref, 1, 1)


def halves(value):
    high = value.astype(jnp.bfloat16)
    return high, (value - high.astype(jnp.float32)).astype(jnp.bfloat16)


def local_twice(dims, rows_ref, weight_ref, r):
    sensors, size_x, size_y, size_z = dims
    x, y = divmod(r, size_y)

    def row(index):
        return rows_ref[index * sensors : (index + 1) * sensors, :]

    def weight(k):
        return weight_ref[k, x, y : y + 1, :]

    centre = row(r)
    lane_index = lax.broadcasted_iota(jnp.int32, centre.shape, 1)
    total = weight(6) * centre
    if x > 0:
        total = total - weight(0) * row(r - size_y)
    if x < size_x - 1:
        total = total - weight(1) * row(r + size_y)
    if y > 0:
        total = total - weight(2) * row(r - 1)
    if y < size_y - 1:
        total = total - weight(3) * row(r + 1)
    before = jnp.where(lane_index == 0, 0.0, pltpu.roll(centre, 1, 1))
    after = jnp.where(lane_index == size_z - 1, 0.0, pltpu.roll(centre, size_z - 1, 1))
    return total - weight(4) * before - weight(5) * after


def select_columns(dims, rows_ref, weight_ref, halo_refs, z_ref, chosen_ref, parts_ref):
    sensors, size_x, size_y, size_z = dims
    flags = neighbour_flags()
    width = 3 * sensors
    for r in range(size_x * size_y):
        x, y = divmod(r, size_y)
        span = slice(r * size_z, (r + 1) * size_z)
        scale = weight_ref[7, x, y : y + 1, :]
        _, beside = around(dims, rows_ref, halo_refs, z_ref, r, flags)
        for c in range(3):
            high, low = halves(scale * (beside[2 * c + 1] - beside[2 * c]))
            parts_ref[c * sensors : (c + 1) * sensors, span] = high
            parts_ref[width + c * sensors : width + (c + 1) * sensors, span] = low
    found = lax.dot_general(
        chosen_ref[...], parts_ref[...], last_with_last, preferred_element_type=jnp.float32
    )
    return found[:, :width] + found[:, width:]


def source_kernel(dims, counts, rows_ref, applied_ref, weight_ref, chosen_ref, z_ref, *refs):
    sensors, size_x, size_y, size_z = dims
    messages = sum(counts[:2])
    column_ref, sum_ref, parts_ref = refs[messages : messages + 3]
    halo_refs = sort_halos(refs[:messages], refs[messages + 3 :], counts)
    sums = [jnp.zeros((sensors, size_z), jnp.float32) for _ in range(4)]
    for r in range(size_x * size_y):
        source = rows_ref[r * sensors : (r + 1) * sensors, :]
        applied = applied_ref[r * sensors : (r + 1) * sensors, :]
        twice = local_twice(dims, applied_ref, weight_ref, r)
        for k, product in enumerate(
            (source * source, source * applied, applied * applied, applied * twice)
        ):
            sums[k] = sums[k] + product
    for k in range(4):
        sum_ref[k * sensors : (k + 1) * sensors, :] = sums[k]
    column_ref[...] = select_columns(
        dims, rows_ref, weight_ref, halo_refs, z_ref, chosen_ref, parts_ref
    )


def packed_beside(dims, beyond, own, along_x, along_y):
    sensors, size_x, size_y, size_z = dims
    half = size_z // 2
    lane_index = lax.broadcasted_iota(jnp.int32, beyond.shape, 1)
    in_half = lane_index % half
    row = in_half // 2 % size_y

    def moved(value, lanes):
        return pltpu.roll(value, lanes % size_z, 1)

    def either(condition, value, lanes, other, back):
        return jnp.where(condition, moved(value, lanes), moved(other, back))

    step, wrap = 2 * size_y, 2 * size_y * (size_x - 1)
    return (
        either(in_half >= step, beyond, step, along_x[0], -wrap),
        either(in_half < wrap, beyond, -step, along_x[1], wrap),
        either(row > 0, beyond, 2, along_y[0], -2 * (size_y - 1)),
        either(row < size_y - 1, beyond, -2, along_y[1], 2 * (size_y - 1)),
        either(lane_index < half, beyond, 1, beyond, -1),
        either(lane_index < half, own, 1, own, -1),
    )


def moment_kernel(
    dims, counts, applied_ref, weight_ref, sum_ref, end_ref, own_ref, z_ref, table_ref, *refs
):
    sensors, size_x, size_y, size_z = dims
    messages = sum(counts[:2])
    moment_ref, plane_ref = refs[messages : messages + 2]
    halo_refs = sort_halos(refs[:messages], refs[messages + 2 :], counts)
    (x_low, x_high), (y_low, y_high) = halo_refs
    flags = neighbour_flags()

    def forwarded(pair, dim, first, last):
        start = (size_y, size_x)[dim] * sensors
        return [
            jnp.where(flags[dim][end], ref[start + first : start + last, :], 0.0)
            for end, ref in enumerate(pair)
        ]

    def of_lines(first, last):
        return packed_beside(
            dims,
            z_ref[first:last, :],
            own_ref[first:last, :],
            forwarded(halo_refs[0], 0, first, last),
            forwarded(halo_refs[1], 1, first, last),
        )

    middle = tissue(z_ref[sensors:, :], table_ref)
    six = [
        edge_weight(middle, tissue(label, table_ref))
        for label in of_lines(sensors, z_ref.shape[0])
    ]
    total = mass_term + (six[0] + six[1]) + (six[2] + six[3]) + (six[4] + six[5])
    plane = total[0:1, :] * z_ref[0:sensors, :]
    for weight, value in zip(six, of_lines(0, sensors)):
        plane = plane - weight[0:1, :] * value
    plane_ref[...] = plane

    def part(ref, index):
        return ref[index * sensors : (index + 1) * sensors, :]

    def crossing(k, r, beside):
        x, y = divmod(r, size_y)
        return weight_ref[k, x, y : y + 1, :] * part(applied_ref, r) * beside

    outward = jnp.zeros((sensors, size_z), jnp.float32)
    for y in range(size_y):
        outward = outward + crossing(0, y, part(x_low, y))
        outward = outward + crossing(1, (size_x - 1) * size_y + y, part(x_high, y))
    for x in range(size_x):
        outward = outward + crossing(2, x * size_y, part(y_low, x))
        outward = outward + crossing(3, x * size_y + size_y - 1, part(y_high, x))
    outward = outward + end_ref[...] * plane
    last = part(sum_ref, 3) - outward
    moment_ref[...] = lax.dot_general(
        jnp.ones((8, size_z), jnp.float32),
        jnp.concatenate([sum_ref[0 : 3 * sensors, :], last], axis=0),
        last_with_last,
        precision=lax.Precision.HIGHEST,
        preferred_element_type=jnp.float32,
    )


def payload_rows(sensors, slots_each):
    whole, rest = divmod(6 * sensors, lane_tile)
    fold = lane_tile // rest if rest else 0
    assert not fold or (fold * rest == lane_tile and slots_each % fold == 0)
    rows = whole * slots_each + (slots_each // fold if fold else 0)
    return whole, rest, fold, rows, -(-4 * sensors // lane_tile)


def applied_kernel(
    dims, counts, slots_each, applied_ref, weight_ref, chosen_ref, source_column_ref, z_ref, *refs
):
    sensors, messages = dims[0], sum(counts[:2])
    column_ref, parts_ref = refs[messages : messages + 2]
    halo_refs = sort_halos(refs[:messages], refs[messages + 2 :], counts)
    applied_columns = select_columns(
        dims, applied_ref, weight_ref, halo_refs, z_ref, chosen_ref, parts_ref
    )
    columns = jnp.concatenate([source_column_ref[...], applied_columns], axis=1)
    whole, rest, fold, rows, moment_rows = payload_rows(sensors, slots_each)
    for owner in range(columns.shape[0] // slots_each):
        mine = slice(owner * slots_each, (owner + 1) * slots_each)
        at = owner * (rows + moment_rows)
        for tile in range(whole):
            column_ref[at : at + slots_each, :] = columns[mine, tile * lane_tile : (tile + 1) * lane_tile]
            at += slots_each
        if fold:
            part = slots_each // fold
            others = columns[mine, whole * lane_tile :]
            column_ref[at : at + part, :] = jnp.concatenate(
                [others[k * part : (k + 1) * part, :] for k in range(fold)], axis=1
            )
            at += part
        column_ref[at : at + moment_rows, :] = jnp.zeros((moment_rows, lane_tile), jnp.float32)


def owner_kernel(sensors, slots_each, received_ref, chosen_ref, data_ref, projection_ref, gram_ref):
    whole, rest, fold, rows, moment_rows = payload_rows(sensors, slots_each)
    each = rows + moment_rows
    sources = received_ref.shape[0] // each
    slots = sources * slots_each

    def collected(start, count):
        return jnp.concatenate(
            [received_ref[k * each + start : k * each + start + count, :] for k in range(sources)],
            axis=0,
        )

    gathered = jnp.zeros((moment_rows, lane_tile), jnp.float32)
    for k in range(sources):
        gathered = gathered + received_ref[k * each + rows : (k + 1) * each, :]
    moments = []
    sensor_index = lax.broadcasted_iota(jnp.int32, (sensors, lane_tile), 0)
    lane_index = lax.broadcasted_iota(jnp.int32, (sensors, lane_tile), 1)
    for k in range(4):
        total = jnp.zeros((sensors, 1), jnp.float32)
        for row in range(moment_rows):
            here = lane_index + row * lane_tile == sensor_index + k * sensors
            picked = jnp.where(here, gathered[row : row + 1, :], 0.0)
            total = total + jnp.sum(picked, axis=1, keepdims=True)
        moments.append(total)
    moment_zero, moment_one, moment_two, moment_three = moments
    first_step = moment_zero / moment_one
    residue = first_step * first_step * moment_two - moment_zero
    growth = 1.0 + residue / moment_zero
    curvature = (
        growth * growth * moment_one
        - 2.0 * growth * first_step * moment_two
        + first_step * first_step * moment_three
    )
    second_step = residue / curvature
    source_coef = first_step + second_step * growth
    applied_coef = second_step * first_step
    contract = (((0,), (0,)), ((), ()))

    def selected(values, first):
        chosen = chosen_ref[first : first + values.shape[0], :]
        high, low = halves(values)
        return lax.dot_general(
            high, chosen, contract, preferred_element_type=jnp.float32
        ) + lax.dot_general(low, chosen, contract, preferred_element_type=jnp.float32)

    owned = [
        selected(collected(tile * slots_each, slots_each), 0) for tile in range(whole)
    ]
    if fold:
        folded = collected(whole * slots_each, slots_each // fold)
        others = jnp.zeros((rest, chosen_ref.shape[1]), jnp.float32)
        for k in range(fold):
            found = selected(folded, slots + k * (slots // fold))
            others = others + found[k * rest : (k + 1) * rest, :]
        owned.append(others)
    owned = jnp.concatenate(owned, axis=0)
    lead = []
    for c in range(3):
        source_part = owned[c * sensors : (c + 1) * sensors, :]
        applied_part = owned[(3 + c) * sensors : (4 + c) * sensors, :]
        lead.append(source_coef * source_part - applied_coef * applied_part)
        projection_ref[c] = lax.dot_general(
            data_ref[...],
            lead[c],
            contract,
            precision=lax.Precision.HIGHEST,
            preferred_element_type=jnp.float32,
        )
    for k, (first, second) in enumerate(entry_pairs):
        gram_ref[k : k + 1, :] = jnp.sum(lead[first] * lead[second], axis=0, keepdims=True)


def call(body, **arguments):
    return pl.pallas_call(
        body, compiler_params=pltpu.CompilerParams(vmem_limit_bytes=vmem_grant), **arguments
    )


def in_hbm(count):
    return [pl.BlockSpec(memory_space=pltpu.HBM)] * count


def held_in_hbm(*arrays):
    return [pltpu.with_memory_space_constraint(a, pltpu.HBM) for a in arrays]


def in_vmem(count):
    return [pl.BlockSpec(memory_space=pltpu.VMEM)] * count


def face_shapes(dims, counts, x_rows, y_rows):
    sensors, size_x, size_y, size_z = dims
    rows = (size_y * sensors + x_rows, size_x * sensors + y_rows)
    return [
        jax.ShapeDtypeStruct((row, size_z), jnp.float32)
        for row, count in zip(rows, counts)
        for _ in range(count)
    ]


def per_device(source_term, labels, conductivity_table, send_map, owner_slots, sensor_data):
    dims = source_term.shape
    sensors, size_x, size_y, size_z = dims
    rows_count = size_x * size_y
    counts = face_counts()
    messages = sum(counts[:2])
    owners = lax.axis_size("gx") * lax.axis_size("gy")
    slots = send_map.size
    slots_each = slots // owners
    _, _, fold, payload, moment_rows = payload_rows(sensors, slots_each)
    times = sensor_data.shape[1]
    positions = owner_slots.shape[0]

    voxels = rows_count * size_z

    def array(shape, dtype=jnp.float32):
        return jax.ShapeDtypeStruct(shape, dtype)

    parts = [pltpu.VMEM((6 * sensors, voxels), jnp.bfloat16)]
    field_shape = array((rows_count * sensors, size_z))
    ends_shape = array((sensors + 8, size_z))
    levels = conductivity_table.shape[0]
    small = (
        send_map.reshape(1, slots),
        owner_slots.reshape(1, positions),
        sensor_data,
        conductivity_table,
    )
    packed = call(
        functools.partial(pack_kernel, dims, counts),
        out_shape=[field_shape, array(labels.shape), array((levels, size_y, size_z))]
        + [array(value.shape, value.dtype) for value in small[:3]]
        + [ends_shape]
        + face_shapes(dims, counts, size_y, 8 * -(-size_x // 8)),
        in_specs=in_hbm(6),
        out_specs=in_vmem(7 + messages),
        scratch_shapes=[
            pltpu.VMEM((size_x, sensors, size_y, size_z), jnp.float32),
            pltpu.VMEM((size_x, size_y, size_z), jnp.int32),
            pltpu.SMEM((levels,), jnp.float32),
            pltpu.SemaphoreType.DMA((size_x + 5,)),
        ],
        name="pack",
    )(*held_in_hbm(source_term, labels, *small))
    rows, shifted, table, voxel, owned, data, own_ends, *faces = packed
    source_halos = exchange_all([*split_refs(faces, counts[:2]), [own_ends] * counts[2]])
    chosen, owned_chosen, table = call(
        functools.partial(prepare_kernel, size_z, (slots_each, fold)),
        out_shape=[
            array((slots, voxels), jnp.bfloat16),
            array((slots * (2 if fold else 1), positions), jnp.bfloat16),
            array(table.shape),
        ],
        in_specs=in_vmem(3),
        out_specs=in_vmem(3),
        name="prepare",
    )(voxel, owned, table)

    result = call(
        functools.partial(apply_kernel, dims, counts),
        out_shape=[array((8, size_x, size_y, size_z)), array((sensors, size_z)), field_shape]
        + [ends_shape]
        + face_shapes(dims, counts, sensors + 8, sensors + 8),
        in_specs=in_vmem(3 + messages + counts[2]),
        out_specs=in_vmem(4 + messages),
        scratch_shapes=held_halos(source_halos, counts),
        name="apply",
    )(rows, shifted, table, *source_halos)
    weight, ends, applied, beyond, *faces = result
    applied_halos = exchange_all(split_refs(faces, counts[:2]))

    source_columns, sums = call(
        functools.partial(source_kernel, dims, counts),
        out_shape=[array((slots, 3 * sensors)), array((4 * sensors, size_z))],
        in_specs=in_vmem(5 + messages),
        out_specs=in_vmem(2),
        scratch_shapes=parts + held_halos(source_halos, counts),
        name="source_columns",
    )(rows, applied, weight, chosen, beyond, *source_halos[:messages])
    moment, plane = call(
        functools.partial(moment_kernel, dims, counts),
        out_shape=[array((8, 4 * sensors)), array((sensors, size_z))],
        in_specs=in_vmem(7 + messages),
        out_specs=in_vmem(2),
        scratch_shapes=held_halos(applied_halos, counts),
        name="moments",
    )(applied, weight, sums, ends, own_ends, beyond, table, *applied_halos)
    moment = sum_over(moment, "gz")

    each = payload + moment_rows
    columns = call(
        functools.partial(applied_kernel, dims, counts, slots_each),
        out_shape=array((owners * each, lane_tile)),
        in_specs=in_vmem(5 + messages),
        out_specs=in_vmem(1)[0],
        scratch_shapes=parts + held_halos(applied_halos, counts),
        name="applied_columns",
    )(applied, weight, chosen, source_columns, plane, *applied_halos)
    place = lax.broadcasted_iota(jnp.int32, columns.shape, 0) % each
    stamp = jnp.pad(moment[0], (0, moment_rows * lane_tile - 4 * sensors)).reshape(-1, lane_tile)
    for row in range(moment_rows):
        columns = jnp.where(place == payload + row, stamp[row : row + 1], columns)
    received = lax.all_to_all(
        columns.reshape(owners, 1, each * lane_tile), ("gx", "gy"), 0, 0, tiled=True
    ).reshape(columns.shape)
    return call(
        functools.partial(owner_kernel, sensors, slots_each),
        out_shape=[array((3, times, positions)), array((6, positions))],
        in_specs=in_vmem(3),
        out_specs=in_vmem(2),
        name="owner",
    )(received, owned_chosen, data)


def solution(mesh):
    in_specs = (
        P(None, "gx", "gy", "gz"),
        P("gx", "gy", "gz"),
        P(),
        P("gx", "gy", "gz", None),
        P(("gx", "gy", "gz")),
        P(),
    )
    out_specs = (P(None, None, ("gx", "gy", "gz")), P(None, ("gx", "gy", "gz")))
    step = jax.shard_map(
        per_device, mesh=mesh, in_specs=in_specs, out_specs=out_specs, check_vma=False
    )
    return lambda *arguments: tuple(step(*arguments))
```

```python
import functools

import jax
import jax.numpy as jnp
from jax import lax
from jax.experimental import pallas as pl
from jax.experimental.pallas import tpu as pltpu
from jax.sharding import PartitionSpec as P

mass_term = 0.25
lane_tile = 128
axes = ("gx", "gy", "gz")
vmem_grant = 16 << 20
last_with_last = (((1,), (1,)), ((), ()))
entry_pairs = ((0, 0), (1, 1), (2, 2), (0, 1), (0, 2), (1, 2))


def swap(value, axis, odd):
    count, beside = lax.axis_size(axis), lax.axis_size("gz")
    partner = {}
    for first in range(odd, count - 1, 2):
        partner[first], partner[first + 1] = first + 1, first
    alone = [i for i in range(count) if i not in partner]
    if alone and axis != "gz" and beside % 2 == 0:
        table = [
            (i * beside + k, partner[i] * beside + k if i in partner else i * beside + (k ^ 1))
            for i in range(count)
            for k in range(beside)
        ]
        return lax.ppermute(value, (axis, "gz"), table)
    for source, target in zip(alone, alone[::-1]):
        partner[source] = target
    return lax.ppermute(value, axis, sorted(partner.items()))


def sum_over(value, axis):
    count = lax.axis_size(axis)
    steps = [count - 1, *range(1, count - 1)][: count - 1]
    if count & (count - 1) == 0:
        tables = [[(i, i ^ d) for i in range(count)] for d in steps]
    else:
        tables = [[(i, (i + d) % count) for i in range(count)] for d in steps]
    return value + sum(lax.ppermute(value, axis, table) for table in tables)


def face_counts():
    return [1 if lax.axis_size(axis) <= 2 else 2 for axis in axes]


def exchange_all(groups):
    halos = []
    for axis, group in zip(axes, groups):
        if lax.axis_size(axis) > 1:
            group = [swap(face, axis, odd) for odd, face in enumerate(group)]
        halos.extend(group)
    return halos


def sort_halos(halo_refs, held_refs, counts):
    sorted_refs, held_refs = [], list(held_refs)
    for axis, group in zip(axes, split_refs(halo_refs, counts[:2])):
        if len(group) == 1:
            sorted_refs.append((group[0], group[0]))
            continue
        even = lax.axis_index(axis) % 2 == 0
        below, above = held_refs.pop(0), held_refs.pop(0)
        first, second = group[0][...], group[1][...]
        below[...] = jnp.where(even, second, first)
        above[...] = jnp.where(even, first, second)
        sorted_refs.append((below, above))
    return sorted_refs


def sort_ends(z_refs):
    below = above = z_refs[0][...]
    if len(z_refs) == 2:
        even = lax.axis_index("gz") % 2 == 0
        below, above = (
            jnp.where(even, z_refs[1 - k][...], z_refs[k][...]) for k in range(2)
        )
    half = below.shape[1] // 2
    lane_index = lax.broadcasted_iota(jnp.int32, below.shape, 1)
    return pltpu.roll(jnp.where(lane_index < half, above, below), half, 1)


def held_halos(faces, counts):
    return [
        pltpu.VMEM(face.shape, face.dtype)
        for group in split_refs(faces, counts[:2])
        for face in (group if len(group) == 2 else [])
    ]


def lanes_equal(shape, value):
    return lax.broadcasted_iota(jnp.int32, shape, len(shape) - 1) == value


def neighbour_flags():
    flags = []
    for axis in axes:
        index = lax.axis_index(axis)
        flags.append((index > 0, index < lax.axis_size(axis) - 1))
    return flags


def write_faces(dims, rows_ref, face_refs, labels=None, beyond=None):
    sensors, size_x, size_y, size_z = dims
    x_refs, y_refs = face_refs

    def field(r):
        return rows_ref[pl.ds(pl.multiple_of(r * sensors, sensors), sensors), :]

    def high_end(axis, number):
        return lax.axis_index(axis) % 2 == number

    for number, ref in enumerate(x_refs):
        high = high_end("gx", number)
        x = jnp.where(high, size_x - 1, 0)
        for y in range(size_y):
            ref[y * sensors : (y + 1) * sensors, :] = field(x * size_y + y)
        if labels is not None:
            ref[size_y * sensors :, :] = jnp.where(high, labels[-1], labels[0])
        else:
            ref[size_y * sensors :, :] = beyond

    for number, ref in enumerate(y_refs):
        high = high_end("gy", number)
        y = jnp.where(high, size_y - 1, 0)
        for x in range(size_x):
            ref[x * sensors : (x + 1) * sensors, :] = field(x * size_y + y)
            if labels is not None:
                row = size_x * sensors + x
                ref[row : row + 1, :] = jnp.where(high, labels[x][size_y - 1 :, :], labels[x][0:1, :])
        if labels is None:
            ref[size_x * sensors :, :] = beyond


def put_lanes(packed, row, source, target, count):
    lanes = packed.shape[1]
    moved = pltpu.roll(row, (target - source) % lanes, 1)
    lane_index = lax.broadcasted_iota(jnp.int32, packed.shape, 1)
    return jnp.where((lane_index >= target) & (lane_index < target + count), moved, packed)


def pack_lines(dims, values, depth, low_shift):
    size_x, size_y, size_z = dims[1:]
    half = size_z // 2
    packed = jnp.zeros((size_y, size_z), jnp.float32)
    row_index = lax.broadcasted_iota(jnp.int32, packed.shape, 0)
    for x in range(size_x):
        line = 2 * (x * size_y + row_index)
        for p in range(depth):
            low, high = values[x]
            end = size_z - depth + p
            packed = jnp.where(lanes_equal(packed.shape, line + low_shift + p), low[:, p : p + 1], packed)
            packed = jnp.where(lanes_equal(packed.shape, line + half + p), high[:, end : end + 1], packed)
    return jnp.broadcast_to(jnp.sum(packed, axis=0, keepdims=True), (8, size_z))


def pack_rows(dims, rows_ref, depth, low_shift):
    sensors, size_x, size_y, size_z = dims
    half = size_z // 2
    assert 2 * size_x * size_y <= half
    packed = jnp.zeros((sensors, size_z), jnp.float32)
    for r in range(size_x * size_y):
        row = rows_ref[r * sensors : (r + 1) * sensors, :]
        packed = put_lanes(packed, row, 0, 2 * r + low_shift, depth)
        packed = put_lanes(packed, row, size_z - depth, half + 2 * r, depth)
    return packed


def split_refs(refs, counts):
    groups, start = [], 0
    for count in counts:
        groups.append(refs[start : start + count])
        start += count
    return groups


def pack_kernel(dims, counts, source_ref, label_ref, *refs):
    sensors, size_x, size_y, size_z = dims
    small_hbm, refs = refs[:4], refs[4:]
    (rows_ref, shifted_ref, table_ref), small_refs = refs[:3], refs[3:6]
    own_ref, refs = refs[6], refs[7:]
    face_refs = split_refs(refs[: sum(counts[:2])], counts[:2])
    staged_ref, label_vmem, level_ref, semaphores = refs[sum(counts[:2]) :]
    copies = [
        pltpu.make_async_copy(source_ref.at[:, x], staged_ref.at[x], semaphores.at[x])
        for x in range(size_x)
    ]
    moves = [(label_ref, label_vmem), *zip(small_hbm, (*small_refs, level_ref))]
    for k, move in enumerate(moves):
        copies.append(pltpu.make_async_copy(*move, semaphores.at[size_x + k]))
    for copy in copies[size_x:] + copies[:size_x]:
        copy.start()
    for copy in copies[size_x:]:
        copy.wait()
    for level in range(level_ref.shape[0]):
        table_ref[level] = jnp.full(table_ref.shape[1:], level_ref[level], jnp.float32)
    shifted = [(label_vmem[x] + 1).astype(jnp.float32) for x in range(size_x)]
    for x in range(size_x):
        shifted_ref[x] = shifted[x]
    flat = staged_ref.reshape(size_x, sensors * size_y, size_z)
    for x in range(size_x):
        copies[x].wait()
        for y in range(size_y):
            r = x * size_y + y
            rows_ref[r * sensors : (r + 1) * sensors, :] = flat[x, pl.ds(y, sensors, stride=size_y), :]
    write_faces(dims, rows_ref, face_refs, labels=shifted)
    own_ref[0:sensors, :] = pack_rows(dims, rows_ref, 2, 0)
    own_ref[sensors:, :] = pack_lines(dims, [(plane, plane) for plane in shifted], 2, 0)


def prepare_kernel(
    size_z, folding, voxel_ref, owned_ref, level_ref, chosen_ref, owned_chosen_ref, table_ref
):
    table_ref[...] = level_ref[...]
    slots, voxels = chosen_ref.shape
    square = (slots, slots)
    diagonal = lanes_equal(square, lax.broadcasted_iota(jnp.int32, square, 0))
    voxel = jnp.where(diagonal, voxel_ref[...].astype(jnp.float32), 0.0)
    voxel = jnp.sum(voxel, axis=1, keepdims=True).astype(jnp.int32)
    voxel = jnp.broadcast_to(voxel, (slots, size_z))
    row = voxel // size_z
    lane_index = lax.broadcasted_iota(jnp.int32, (slots, size_z), 1)
    lane = one_hot(lane_index == voxel - row * size_z)
    row = row.astype(jnp.float32).astype(jnp.bfloat16)
    none = jnp.zeros_like(lane)
    for r in range(voxels // size_z):
        chosen_ref[:, r * size_z : (r + 1) * size_z] = jnp.where(row == r, lane, none)
    row_index = lax.broadcasted_iota(jnp.int32, (slots, owned_ref.shape[1]), 0)
    owned_chosen_ref[0:slots, :] = one_hot(row_index == owned_ref[...])
    slots_each, fold = folding
    if fold:
        part = slots_each // fold
        row_index = lax.broadcasted_iota(jnp.int32, (slots // fold, owned_ref.shape[1]), 0)
        slot_index = row_index // part * slots_each + row_index % part
        for k in range(fold):
            first = slots + k * (slots // fold)
            owned_chosen_ref[first : first + slots // fold, :] = one_hot(
                slot_index + k * part == owned_ref[...]
            )


def one_hot(condition):
    return condition.astype(jnp.float32).astype(jnp.bfloat16)


def tissue(shifted, table_ref):
    conductivity = jnp.zeros_like(shifted)
    for level in range(table_ref.shape[0]):
        value = table_ref[level] if shifted.shape == table_ref.shape[1:] else table_ref[level, 0:1, 0:1]
        conductivity = jnp.where(shifted == level + 1, value, conductivity)
    return conductivity, (shifted > 0).astype(jnp.float32)


def edge_weight(first, second):
    return 0.5 * (first[0] + second[0]) * first[1] * second[1]


def weights(dims, shifted_ref, table_ref, halo_refs, z_ref, weight_ref):
    sensors, size_x, size_y, size_z = dims
    flags = neighbour_flags()
    (x_low, x_high), (y_low, y_high) = halo_refs
    beyond = z_ref[sensors : sensors + 1, :]
    half = size_z // 2

    def beyond_end(x, first, flag):
        line = 2 * (x * size_y + row_index) + first
        picked = jnp.where(lanes_equal(row_index.shape, line), beyond, 0.0)
        return masked(jnp.sum(picked, axis=1, keepdims=True), flag)

    def masked(value, flag):
        return jnp.where(flag, value, 0.0)

    own = [shifted_ref[x] for x in range(size_x)]
    own_tissue = [tissue(plane, table_ref) for plane in own]
    x_rows = slice(size_y * sensors, size_y * (sensors + 1))
    below = tissue(masked(x_low[x_rows, :], flags[0][0]), table_ref)
    above = tissue(masked(x_high[x_rows, :], flags[0][1]), table_ref)
    planes = [below] + own_tissue + [above]
    across_x = [edge_weight(planes[i], planes[i + 1]) for i in range(size_x + 1)]
    row_index = lax.broadcasted_iota(jnp.int32, (size_y, size_z), 0)
    lane_index = lax.broadcasted_iota(jnp.int32, (size_y, size_z), 1)
    for x in range(size_x):
        y_row = size_x * sensors + x
        shifted = own[x]
        y_before = jnp.where(
            row_index == 0,
            masked(y_low[y_row : y_row + 1, :], flags[1][0]),
            pltpu.roll(shifted, 1, 0),
        )
        y_after = jnp.where(
            row_index == size_y - 1,
            masked(y_high[y_row : y_row + 1, :], flags[1][1]),
            pltpu.roll(shifted, size_y - 1, 0),
        )
        z_before = jnp.where(
            lane_index == 0,
            beyond_end(x, 1, flags[2][0]),
            pltpu.roll(shifted, 1, 1),
        )
        z_after = jnp.where(
            lane_index == size_z - 1,
            beyond_end(x, half, flags[2][1]),
            pltpu.roll(shifted, size_z - 1, 1),
        )
        six = [across_x[x], across_x[x + 1]]
        for beside in (y_before, y_after, z_before, z_after):
            six.append(edge_weight(own_tissue[x], tissue(beside, table_ref)))
        for k, weight in enumerate(six):
            weight_ref[k, x] = weight
        weight_ref[6, x] = mass_term + (six[0] + six[1]) + (six[2] + six[3]) + (six[4] + six[5])
        weight_ref[7, x] = 0.5 * own_tissue[x][0]


def around(dims, rows_ref, halo_refs, z_ref, r, flags=None):
    sensors, size_x, size_y, size_z = dims
    (x_low, x_high), (y_low, y_high) = halo_refs
    x, y = divmod(r, size_y)
    z_low = z_ref[0:sensors, 2 * r + 1 : 2 * r + 2]
    high_lane = size_z // 2 + 2 * r
    z_high = z_ref[0:sensors, high_lane : high_lane + 1]

    def keep(value, dim, end):
        return value if flags is None else jnp.where(flags[dim][end], value, 0.0)

    def row(index):
        return rows_ref[index * sensors : (index + 1) * sensors, :]

    def part(ref, index):
        return ref[index * sensors : (index + 1) * sensors, :]

    centre = row(r)
    x_before = row(r - size_y) if x > 0 else keep(part(x_low, y), 0, 0)
    x_after = row(r + size_y) if x < size_x - 1 else keep(part(x_high, y), 0, 1)
    y_before = row(r - 1) if y > 0 else keep(part(y_low, x), 1, 0)
    y_after = row(r + 1) if y < size_y - 1 else keep(part(y_high, x), 1, 1)
    lane_index = lax.broadcasted_iota(jnp.int32, centre.shape, 1)
    z_before = jnp.where(
        lane_index == 0, keep(z_low, 2, 0), pltpu.roll(centre, 1, 1)
    )
    z_after = jnp.where(
        lane_index == size_z - 1,
        keep(z_high, 2, 1),
        pltpu.roll(centre, size_z - 1, 1),
    )
    return centre, (x_before, x_after, y_before, y_after, z_before, z_after)


def combine(weight_ref, x, y, centre, beside):
    total = weight_ref[6, x, y : y + 1, :] * centre
    for k, value in enumerate(beside):
        total = total - weight_ref[k, x, y : y + 1, :] * value
    return total


def apply_kernel(dims, counts, rows_ref, shifted_ref, table_ref, *refs):
    sensors, size_x, size_y, size_z = dims
    message_refs, refs = refs[: sum(counts)], refs[sum(counts) :]
    weight_ref, end_ref, applied_ref, z_ref = refs[:4]
    face_refs = split_refs(refs[4 : 4 + sum(counts[:2])], counts[:2])
    halo_refs = sort_halos(message_refs, refs[4 + sum(counts[:2]) :], counts)
    z_ref[...] = sort_ends(message_refs[sum(counts[:2]) :])
    weights(dims, shifted_ref, table_ref, halo_refs, z_ref, weight_ref)
    for r in range(size_x * size_y):
        x, y = divmod(r, size_y)
        centre, beside = around(dims, rows_ref, halo_refs, z_ref, r)
        applied_ref[r * sensors : (r + 1) * sensors, :] = combine(weight_ref, x, y, centre, beside)
    write_faces(dims, applied_ref, face_refs, beyond=z_ref[...])
    lines = [(weight_ref[4, x], weight_ref[5, x]) for x in range(size_x)]
    outward = pack_lines(dims, lines, 1, 1)
    end_ref[...] = outward[0:1, :] * pack_rows(dims, applied_ref, 1, 1)


def halves(value):
    high = value.astype(jnp.bfloat16)
    return high, (value - high.astype(jnp.float32)).astype(jnp.bfloat16)


def local_twice(dims, rows_ref, weight_ref, r):
    sensors, size_x, size_y, size_z = dims
    x, y = divmod(r, size_y)

    def row(index):
        return rows_ref[index * sensors : (index + 1) * sensors, :]

    def weight(k):
        return weight_ref[k, x, y : y + 1, :]

    centre = row(r)
    lane_index = lax.broadcasted_iota(jnp.int32, centre.shape, 1)
    total = weight(6) * centre
    if x > 0:
        total = total - weight(0) * row(r - size_y)
    if x < size_x - 1:
        total = total - weight(1) * row(r + size_y)
    if y > 0:
        total = total - weight(2) * row(r - 1)
    if y < size_y - 1:
        total = total - weight(3) * row(r + 1)
    before = jnp.where(lane_index == 0, 0.0, pltpu.roll(centre, 1, 1))
    after = jnp.where(lane_index == size_z - 1, 0.0, pltpu.roll(centre, size_z - 1, 1))
    return total - weight(4) * before - weight(5) * after


def select_columns(dims, rows_ref, weight_ref, halo_refs, z_ref, chosen_ref, parts_ref):
    sensors, size_x, size_y, size_z = dims
    flags = neighbour_flags()
    width = 3 * sensors
    for r in range(size_x * size_y):
        x, y = divmod(r, size_y)
        span = slice(r * size_z, (r + 1) * size_z)
        scale = weight_ref[7, x, y : y + 1, :]
        _, beside = around(dims, rows_ref, halo_refs, z_ref, r, flags)
        for c in range(3):
            high, low = halves(scale * (beside[2 * c + 1] - beside[2 * c]))
            parts_ref[c * sensors : (c + 1) * sensors, span] = high
            parts_ref[width + c * sensors : width + (c + 1) * sensors, span] = low
    found = lax.dot_general(
        chosen_ref[...], parts_ref[...], last_with_last, preferred_element_type=jnp.float32
    )
    return found[:, :width] + found[:, width:]


def source_kernel(dims, counts, rows_ref, applied_ref, weight_ref, chosen_ref, z_ref, *refs):
    sensors, size_x, size_y, size_z = dims
    messages = sum(counts[:2])
    column_ref, sum_ref, parts_ref = refs[messages : messages + 3]
    halo_refs = sort_halos(refs[:messages], refs[messages + 3 :], counts)
    sums = [jnp.zeros((sensors, size_z), jnp.float32) for _ in range(4)]
    for r in range(size_x * size_y):
        source = rows_ref[r * sensors : (r + 1) * sensors, :]
        applied = applied_ref[r * sensors : (r + 1) * sensors, :]
        twice = local_twice(dims, applied_ref, weight_ref, r)
        for k, product in enumerate(
            (source * source, source * applied, applied * applied, applied * twice)
        ):
            sums[k] = sums[k] + product
    for k in range(4):
        sum_ref[k * sensors : (k + 1) * sensors, :] = sums[k]
    column_ref[...] = select_columns(
        dims, rows_ref, weight_ref, halo_refs, z_ref, chosen_ref, parts_ref
    )


def packed_beside(dims, beyond, own, along_x, along_y):
    sensors, size_x, size_y, size_z = dims
    half = size_z // 2
    lane_index = lax.broadcasted_iota(jnp.int32, beyond.shape, 1)
    in_half = lane_index % half
    row = in_half // 2 % size_y

    def moved(value, lanes):
        return pltpu.roll(value, lanes % size_z, 1)

    def either(condition, value, lanes, other, back):
        return jnp.where(condition, moved(value, lanes), moved(other, back))

    step, wrap = 2 * size_y, 2 * size_y * (size_x - 1)
    return (
        either(in_half >= step, beyond, step, along_x[0], -wrap),
        either(in_half < wrap, beyond, -step, along_x[1], wrap),
        either(row > 0, beyond, 2, along_y[0], -2 * (size_y - 1)),
        either(row < size_y - 1, beyond, -2, along_y[1], 2 * (size_y - 1)),
        either(lane_index < half, beyond, 1, beyond, -1),
        either(lane_index < half, own, 1, own, -1),
    )


def moment_kernel(
    dims, counts, applied_ref, weight_ref, sum_ref, end_ref, own_ref, z_ref, table_ref, *refs
):
    sensors, size_x, size_y, size_z = dims
    messages = sum(counts[:2])
    moment_ref, plane_ref = refs[messages : messages + 2]
    halo_refs = sort_halos(refs[:messages], refs[messages + 2 :], counts)
    (x_low, x_high), (y_low, y_high) = halo_refs
    flags = neighbour_flags()

    def forwarded(pair, dim, first, last):
        start = (size_y, size_x)[dim] * sensors
        return [
            jnp.where(flags[dim][end], ref[start + first : start + last, :], 0.0)
            for end, ref in enumerate(pair)
        ]

    def of_lines(first, last):
        return packed_beside(
            dims,
            z_ref[first:last, :],
            own_ref[first:last, :],
            forwarded(halo_refs[0], 0, first, last),
            forwarded(halo_refs[1], 1, first, last),
        )

    middle = tissue(z_ref[sensors:, :], table_ref)
    six = [
        edge_weight(middle, tissue(label, table_ref))
        for label in of_lines(sensors, z_ref.shape[0])
    ]
    total = mass_term + (six[0] + six[1]) + (six[2] + six[3]) + (six[4] + six[5])
    plane = total[0:1, :] * z_ref[0:sensors, :]
    for weight, value in zip(six, of_lines(0, sensors)):
        plane = plane - weight[0:1, :] * value
    plane_ref[...] = plane

    def part(ref, index):
        return ref[index * sensors : (index + 1) * sensors, :]

    def crossing(k, r, beside):
        x, y = divmod(r, size_y)
        return weight_ref[k, x, y : y + 1, :] * part(applied_ref, r) * beside

    outward = jnp.zeros((sensors, size_z), jnp.float32)
    for y in range(size_y):
        outward = outward + crossing(0, y, part(x_low, y))
        outward = outward + crossing(1, (size_x - 1) * size_y + y, part(x_high, y))
    for x in range(size_x):
        outward = outward + crossing(2, x * size_y, part(y_low, x))
        outward = outward + crossing(3, x * size_y + size_y - 1, part(y_high, x))
    outward = outward + end_ref[...] * plane
    last = part(sum_ref, 3) - outward
    moment_ref[...] = lax.dot_general(
        jnp.ones((8, size_z), jnp.float32),
        jnp.concatenate([sum_ref[0 : 3 * sensors, :], last], axis=0),
        last_with_last,
        precision=lax.Precision.HIGHEST,
        preferred_element_type=jnp.float32,
    )


def payload_rows(sensors, slots_each):
    whole, rest = divmod(6 * sensors, lane_tile)
    fold = lane_tile // rest if rest else 0
    assert not fold or (fold * rest == lane_tile and slots_each % fold == 0)
    rows = whole * slots_each + (slots_each // fold if fold else 0)
    return whole, rest, fold, rows, -(-4 * sensors // lane_tile)


def applied_kernel(
    dims, counts, slots_each, applied_ref, weight_ref, chosen_ref, source_column_ref, z_ref, *refs
):
    sensors, messages = dims[0], sum(counts[:2])
    column_ref, parts_ref = refs[messages : messages + 2]
    halo_refs = sort_halos(refs[:messages], refs[messages + 2 :], counts)
    applied_columns = select_columns(
        dims, applied_ref, weight_ref, halo_refs, z_ref, chosen_ref, parts_ref
    )
    columns = jnp.concatenate([source_column_ref[...], applied_columns], axis=1)
    whole, rest, fold, rows, moment_rows = payload_rows(sensors, slots_each)
    for owner in range(columns.shape[0] // slots_each):
        mine = slice(owner * slots_each, (owner + 1) * slots_each)
        at = owner * (rows + moment_rows)
        for tile in range(whole):
            column_ref[at : at + slots_each, :] = columns[mine, tile * lane_tile : (tile + 1) * lane_tile]
            at += slots_each
        if fold:
            part = slots_each // fold
            others = columns[mine, whole * lane_tile :]
            column_ref[at : at + part, :] = jnp.concatenate(
                [others[k * part : (k + 1) * part, :] for k in range(fold)], axis=1
            )
            at += part
        column_ref[at : at + moment_rows, :] = jnp.zeros((moment_rows, lane_tile), jnp.float32)


def owner_kernel(sensors, slots_each, received_ref, chosen_ref, data_ref, projection_ref, gram_ref):
    whole, rest, fold, rows, moment_rows = payload_rows(sensors, slots_each)
    each = rows + moment_rows
    sources = received_ref.shape[0] // each
    slots = sources * slots_each

    def collected(start, count):
        return jnp.concatenate(
            [received_ref[k * each + start : k * each + start + count, :] for k in range(sources)],
            axis=0,
        )

    gathered = jnp.zeros((moment_rows, lane_tile), jnp.float32)
    for k in range(sources):
        gathered = gathered + received_ref[k * each + rows : (k + 1) * each, :]
    moments = []
    sensor_index = lax.broadcasted_iota(jnp.int32, (sensors, lane_tile), 0)
    lane_index = lax.broadcasted_iota(jnp.int32, (sensors, lane_tile), 1)
    for k in range(4):
        total = jnp.zeros((sensors, 1), jnp.float32)
        for row in range(moment_rows):
            here = lane_index + row * lane_tile == sensor_index + k * sensors
            picked = jnp.where(here, gathered[row : row + 1, :], 0.0)
            total = total + jnp.sum(picked, axis=1, keepdims=True)
        moments.append(total)
    moment_zero, moment_one, moment_two, moment_three = moments
    first_step = moment_zero / moment_one
    residue = first_step * first_step * moment_two - moment_zero
    growth = 1.0 + residue / moment_zero
    curvature = (
        growth * growth * moment_one
        - 2.0 * growth * first_step * moment_two
        + first_step * first_step * moment_three
    )
    second_step = residue / curvature
    source_coef = first_step + second_step * growth
    applied_coef = second_step * first_step
    contract = (((0,), (0,)), ((), ()))

    def selected(values, first):
        chosen = chosen_ref[first : first + values.shape[0], :]
        high, low = halves(values)
        return lax.dot_general(
            high, chosen, contract, preferred_element_type=jnp.float32
        ) + lax.dot_general(low, chosen, contract, preferred_element_type=jnp.float32)

    owned = [
        selected(collected(tile * slots_each, slots_each), 0) for tile in range(whole)
    ]
    if fold:
        folded = collected(whole * slots_each, slots_each // fold)
        others = jnp.zeros((rest, chosen_ref.shape[1]), jnp.float32)
        for k in range(fold):
            found = selected(folded, slots + k * (slots // fold))
            others = others + found[k * rest : (k + 1) * rest, :]
        owned.append(others)
    owned = jnp.concatenate(owned, axis=0)
    lead = []
    for c in range(3):
        source_part = owned[c * sensors : (c + 1) * sensors, :]
        applied_part = owned[(3 + c) * sensors : (4 + c) * sensors, :]
        lead.append(source_coef * source_part - applied_coef * applied_part)
        projection_ref[c] = lax.dot_general(
            data_ref[...],
            lead[c],
            contract,
            precision=lax.Precision.HIGHEST,
            preferred_element_type=jnp.float32,
        )
    for k, (first, second) in enumerate(entry_pairs):
        gram_ref[k : k + 1, :] = jnp.sum(lead[first] * lead[second], axis=0, keepdims=True)


def call(body, **arguments):
    return pl.pallas_call(
        body, compiler_params=pltpu.CompilerParams(vmem_limit_bytes=vmem_grant), **arguments
    )


def in_hbm(count):
    return [pl.BlockSpec(memory_space=pltpu.HBM)] * count


def held_in_hbm(*arrays):
    return [pltpu.with_memory_space_constraint(a, pltpu.HBM) for a in arrays]


def in_vmem(count):
    return [pl.BlockSpec(memory_space=pltpu.VMEM)] * count


def face_shapes(dims, counts, x_rows, y_rows):
    sensors, size_x, size_y, size_z = dims
    rows = (size_y * sensors + x_rows, size_x * sensors + y_rows)
    return [
        jax.ShapeDtypeStruct((row, size_z), jnp.float32)
        for row, count in zip(rows, counts)
        for _ in range(count)
    ]


def per_device(source_term, labels, conductivity_table, send_map, owner_slots, sensor_data):
    dims = source_term.shape
    sensors, size_x, size_y, size_z = dims
    rows_count = size_x * size_y
    counts = face_counts()
    messages = sum(counts[:2])
    owners = lax.axis_size("gx") * lax.axis_size("gy")
    slots = send_map.size
    slots_each = slots // owners
    _, _, fold, payload, moment_rows = payload_rows(sensors, slots_each)
    times = sensor_data.shape[1]
    positions = owner_slots.shape[0]

    voxels = rows_count * size_z

    def array(shape, dtype=jnp.float32):
        return jax.ShapeDtypeStruct(shape, dtype)

    parts = [pltpu.VMEM((6 * sensors, voxels), jnp.bfloat16)]
    field_shape = array((rows_count * sensors, size_z))
    ends_shape = array((sensors + 8, size_z))
    levels = conductivity_table.shape[0]
    small = (
        send_map.reshape(1, slots),
        owner_slots.reshape(1, positions),
        sensor_data,
        conductivity_table,
    )
    packed = call(
        functools.partial(pack_kernel, dims, counts),
        out_shape=[field_shape, array(labels.shape), array((levels, size_y, size_z))]
        + [array(value.shape, value.dtype) for value in small[:3]]
        + [ends_shape]
        + face_shapes(dims, counts, size_y, 8 * -(-size_x // 8)),
        in_specs=in_hbm(6),
        out_specs=in_vmem(7 + messages),
        scratch_shapes=[
            pltpu.VMEM((size_x, sensors, size_y, size_z), jnp.float32),
            pltpu.VMEM((size_x, size_y, size_z), jnp.int32),
            pltpu.SMEM((levels,), jnp.float32),
            pltpu.SemaphoreType.DMA((size_x + 5,)),
        ],
        name="pack",
    )(*held_in_hbm(source_term, labels, *small))
    rows, shifted, table, voxel, owned, data, own_ends, *faces = packed
    source_halos = exchange_all([*split_refs(faces, counts[:2]), [own_ends] * counts[2]])
    chosen, owned_chosen, table = call(
        functools.partial(prepare_kernel, size_z, (slots_each, fold)),
        out_shape=[
            array((slots, voxels), jnp.bfloat16),
            array((slots * (2 if fold else 1), positions), jnp.bfloat16),
            array(table.shape),
        ],
        in_specs=in_vmem(3),
        out_specs=in_vmem(3),
        name="prepare",
    )(voxel, owned, table)

    result = call(
        functools.partial(apply_kernel, dims, counts),
        out_shape=[array((8, size_x, size_y, size_z)), array((sensors, size_z)), field_shape]
        + [ends_shape]
        + face_shapes(dims, counts, sensors + 8, sensors + 8),
        in_specs=in_vmem(3 + messages + counts[2]),
        out_specs=in_vmem(4 + messages),
        scratch_shapes=held_halos(source_halos, counts),
        name="apply",
    )(rows, shifted, table, *source_halos)
    weight, ends, applied, beyond, *faces = result
    applied_halos = exchange_all(split_refs(faces, counts[:2]))

    source_columns, sums = call(
        functools.partial(source_kernel, dims, counts),
        out_shape=[array((slots, 3 * sensors)), array((4 * sensors, size_z))],
        in_specs=in_vmem(5 + messages),
        out_specs=in_vmem(2),
        scratch_shapes=parts + held_halos(source_halos, counts),
        name="source_columns",
    )(rows, applied, weight, chosen, beyond, *source_halos[:messages])
    moment, plane = call(
        functools.partial(moment_kernel, dims, counts),
        out_shape=[array((8, 4 * sensors)), array((sensors, size_z))],
        in_specs=in_vmem(7 + messages),
        out_specs=in_vmem(2),
        scratch_shapes=held_halos(applied_halos, counts),
        name="moments",
    )(applied, weight, sums, ends, own_ends, beyond, table, *applied_halos)
    moment = sum_over(moment, "gz")

    each = payload + moment_rows
    columns = call(
        functools.partial(applied_kernel, dims, counts, slots_each),
        out_shape=array((owners * each, lane_tile)),
        in_specs=in_vmem(5 + messages),
        out_specs=in_vmem(1)[0],
        scratch_shapes=parts + held_halos(applied_halos, counts),
        name="applied_columns",
    )(applied, weight, chosen, source_columns, plane, *applied_halos)
    place = lax.broadcasted_iota(jnp.int32, columns.shape, 0) % each
    stamp = jnp.pad(moment[0], (0, moment_rows * lane_tile - 4 * sensors)).reshape(-1, lane_tile)
    for row in range(moment_rows):
        columns = jnp.where(place == payload + row, stamp[row : row + 1], columns)
    received = lax.all_to_all(
        columns.reshape(owners, 1, each * lane_tile), ("gx", "gy"), 0, 0, tiled=True
    ).reshape(columns.shape)
    return call(
        functools.partial(owner_kernel, sensors, slots_each),
        out_shape=[array((3, times, positions)), array((6, positions))],
        in_specs=in_vmem(3),
        out_specs=in_vmem(2),
        name="owner",
    )(received, owned_chosen, data)


def solution(mesh):
    in_specs = (
        P(None, "gx", "gy", "gz"),
        P("gx", "gy", "gz"),
        P(),
        P("gx", "gy", "gz", None),
        P(("gx", "gy", "gz")),
        P(),
    )
    out_specs = (P(None, None, ("gx", "gy", "gz")), P(None, ("gx", "gy", "gz")))
    step = jax.shard_map(
        per_device, mesh=mesh, in_specs=in_specs, out_specs=out_specs, check_vma=False
    )
    return lambda *arguments: tuple(step(*arguments))
```

```python
import functools

import jax
import jax.numpy as jnp
from jax import lax
from jax.experimental import pallas as pl
from jax.experimental.pallas import tpu as pltpu
from jax.sharding import PartitionSpec as P

mass_term = 0.25
lane_tile = 128
axes = ("gx", "gy", "gz")
vmem_grant = 16 << 20
last_with_last = (((1,), (1,)), ((), ()))
entry_pairs = ((0, 0), (1, 1), (2, 2), (0, 1), (0, 2), (1, 2))


def swap(value, axis, odd):
    count, beside = lax.axis_size(axis), lax.axis_size("gz")
    partner = {}
    for first in range(odd, count - 1, 2):
        partner[first], partner[first + 1] = first + 1, first
    alone = [i for i in range(count) if i not in partner]
    if alone and axis != "gz" and beside % 2 == 0:
        table = [
            (i * beside + k, partner[i] * beside + k if i in partner else i * beside + (k ^ 1))
            for i in range(count)
            for k in range(beside)
        ]
        return lax.ppermute(value, (axis, "gz"), table)
    for source, target in zip(alone, alone[::-1]):
        partner[source] = target
    return lax.ppermute(value, axis, sorted(partner.items()))


def sum_over(value, axis):
    count = lax.axis_size(axis)
    steps = [count - 1, *range(1, count - 1)][: count - 1]
    if count & (count - 1) == 0:
        tables = [[(i, i ^ d) for i in range(count)] for d in steps]
    else:
        tables = [[(i, (i + d) % count) for i in range(count)] for d in steps]
    return value + sum(lax.ppermute(value, axis, table) for table in tables)


def face_counts():
    return [1 if lax.axis_size(axis) <= 2 else 2 for axis in axes]


def exchange_all(groups):
    halos = []
    for axis, group in zip(axes, groups):
        if lax.axis_size(axis) > 1:
            group = [swap(face, axis, odd) for odd, face in enumerate(group)]
        halos.extend(group)
    return halos


def sort_halos(halo_refs, held_refs, counts):
    sorted_refs, held_refs = [], list(held_refs)
    for axis, group in zip(axes, split_refs(halo_refs, counts[:2])):
        if len(group) == 1:
            sorted_refs.append((group[0], group[0]))
            continue
        even = lax.axis_index(axis) % 2 == 0
        below, above = held_refs.pop(0), held_refs.pop(0)
        first, second = group[0][...], group[1][...]
        below[...] = jnp.where(even, second, first)
        above[...] = jnp.where(even, first, second)
        sorted_refs.append((below, above))
    return sorted_refs


def sort_ends(z_refs):
    below = above = z_refs[0][...]
    if len(z_refs) == 2:
        even = lax.axis_index("gz") % 2 == 0
        below, above = (
            jnp.where(even, z_refs[1 - k][...], z_refs[k][...]) for k in range(2)
        )
    half = below.shape[1] // 2
    lane_index = lax.broadcasted_iota(jnp.int32, below.shape, 1)
    return pltpu.roll(jnp.where(lane_index < half, above, below), half, 1)


def held_halos(faces, counts):
    return [
        pltpu.VMEM(face.shape, face.dtype)
        for group in split_refs(faces, counts[:2])
        for face in (group if len(group) == 2 else [])
    ]


def lanes_equal(shape, value):
    return lax.broadcasted_iota(jnp.int32, shape, len(shape) - 1) == value


def neighbour_flags():
    flags = []
    for axis in axes:
        index = lax.axis_index(axis)
        flags.append((index > 0, index < lax.axis_size(axis) - 1))
    return flags


def high_end(axis, number):
    return lax.axis_index(axis) % 2 == number


def line_of(dims, rows_ref, r):
    sensors = dims[0]
    return rows_ref[pl.ds(pl.multiple_of(r * sensors, sensors), sensors), :]


def write_x(dims, rows_ref, refs, labels=None, beyond=None):
    sensors, size_x, size_y, size_z = dims
    last = rows_ref.shape[0] // (sensors * size_y) - 1
    for number, ref in enumerate(refs):
        high = high_end("gx", number)
        x = jnp.where(high, last, 0)
        for y in range(size_y):
            ref[y * sensors : (y + 1) * sensors, :] = line_of(dims, rows_ref, x * size_y + y)
        behind = beyond if labels is None else jnp.where(high, labels[-1], labels[0])
        ref[size_y * sensors :, :] = behind


def write_y(dims, rows_ref, refs, labels=None, beyond=None):
    sensors, size_x, size_y, size_z = dims
    for number, ref in enumerate(refs):
        high = high_end("gy", number)
        y = jnp.where(high, size_y - 1, 0)
        for x in range(size_x):
            ref[x * sensors : (x + 1) * sensors, :] = line_of(dims, rows_ref, x * size_y + y)
            if labels is not None:
                row = size_x * sensors + x
                ref[row : row + 1, :] = jnp.where(high, labels[x][size_y - 1 :, :], labels[x][0:1, :])
        if labels is None:
            ref[size_x * sensors :, :] = beyond


def put_lanes(packed, row, source, target, count):
    lanes = packed.shape[1]
    moved = pltpu.roll(row, (target - source) % lanes, 1)
    lane_index = lax.broadcasted_iota(jnp.int32, packed.shape, 1)
    return jnp.where((lane_index >= target) & (lane_index < target + count), moved, packed)


def pack_lines(dims, values, depth, low_shift):
    size_x, size_y, size_z = dims[1:]
    half = size_z // 2
    packed = jnp.zeros((size_y, size_z), jnp.float32)
    row_index = lax.broadcasted_iota(jnp.int32, packed.shape, 0)
    for x in range(size_x):
        line = 2 * (x * size_y + row_index)
        for p in range(depth):
            low, high = values[x]
            end = size_z - depth + p
            packed = jnp.where(lanes_equal(packed.shape, line + low_shift + p), low[:, p : p + 1], packed)
            packed = jnp.where(lanes_equal(packed.shape, line + half + p), high[:, end : end + 1], packed)
    return jnp.broadcast_to(jnp.sum(packed, axis=0, keepdims=True), (8, size_z))


def pack_rows(dims, rows_ref, depth, low_shift):
    sensors, size_x, size_y, size_z = dims
    half = size_z // 2
    assert 2 * size_x * size_y <= half
    packed = jnp.zeros((sensors, size_z), jnp.float32)
    for r in range(size_x * size_y):
        row = rows_ref[r * sensors : (r + 1) * sensors, :]
        packed = put_lanes(packed, row, 0, 2 * r + low_shift, depth)
        packed = put_lanes(packed, row, size_z - depth, half + 2 * r, depth)
    return packed


def split_refs(refs, counts):
    groups, start = [], 0
    for count in counts:
        groups.append(refs[start : start + count])
        start += count
    return groups


def pack_kernel(dims, counts, source_ref, label_ref, *refs):
    sensors, size_x, size_y, size_z = dims
    small_hbm, refs = refs[:4], refs[4:]
    (rows_ref, shifted_ref, table_ref), small_refs = refs[:3], refs[3:6]
    own_ref, refs = refs[6], refs[7:]
    face_refs = split_refs(refs[: sum(counts[:2])], counts[:2])
    staged_ref, label_vmem, level_ref, semaphores = refs[sum(counts[:2]) :]
    copies = [
        pltpu.make_async_copy(source_ref.at[:, x], staged_ref.at[x], semaphores.at[x])
        for x in range(size_x)
    ]
    moves = [(label_ref, label_vmem), *zip(small_hbm, (*small_refs, level_ref))]
    for k, move in enumerate(moves):
        copies.append(pltpu.make_async_copy(*move, semaphores.at[size_x + k]))
    for copy in copies[size_x:] + copies[:size_x]:
        copy.start()
    for copy in copies[size_x:]:
        copy.wait()
    for level in range(level_ref.shape[0]):
        table_ref[level] = jnp.full(table_ref.shape[1:], level_ref[level], jnp.float32)
    shifted = [(label_vmem[x] + 1).astype(jnp.float32) for x in range(size_x)]
    for x in range(size_x):
        shifted_ref[x] = shifted[x]
    flat = staged_ref.reshape(size_x, sensors * size_y, size_z)
    for x in range(size_x):
        copies[x].wait()
        for y in range(size_y):
            r = x * size_y + y
            rows_ref[r * sensors : (r + 1) * sensors, :] = flat[x, pl.ds(y, sensors, stride=size_y), :]
    write_x(dims, rows_ref, face_refs[0], labels=shifted)
    write_y(dims, rows_ref, face_refs[1], labels=shifted)
    own_ref[0:sensors, :] = pack_rows(dims, rows_ref, 2, 0)
    own_ref[sensors:, :] = pack_lines(dims, [(plane, plane) for plane in shifted], 2, 0)


def prepare_kernel(
    size_z, folding, voxel_ref, owned_ref, level_ref, chosen_ref, owned_chosen_ref, table_ref
):
    table_ref[...] = level_ref[...]
    slots, voxels = chosen_ref.shape
    square = (slots, slots)
    diagonal = lanes_equal(square, lax.broadcasted_iota(jnp.int32, square, 0))
    voxel = jnp.where(diagonal, voxel_ref[...].astype(jnp.float32), 0.0)
    voxel = jnp.sum(voxel, axis=1, keepdims=True).astype(jnp.int32)
    voxel = jnp.broadcast_to(voxel, (slots, size_z))
    row = voxel // size_z
    lane_index = lax.broadcasted_iota(jnp.int32, (slots, size_z), 1)
    lane = one_hot(lane_index == voxel - row * size_z)
    row = row.astype(jnp.float32).astype(jnp.bfloat16)
    none = jnp.zeros_like(lane)
    for r in range(voxels // size_z):
        chosen_ref[:, r * size_z : (r + 1) * size_z] = jnp.where(row == r, lane, none)
    row_index = lax.broadcasted_iota(jnp.int32, (slots, owned_ref.shape[1]), 0)
    owned_chosen_ref[0:slots, :] = one_hot(row_index == owned_ref[...])
    slots_each, fold = folding
    if fold:
        part = slots_each // fold
        row_index = lax.broadcasted_iota(jnp.int32, (slots // fold, owned_ref.shape[1]), 0)
        slot_index = row_index // part * slots_each + row_index % part
        for k in range(fold):
            first = slots + k * (slots // fold)
            owned_chosen_ref[first : first + slots // fold, :] = one_hot(
                slot_index + k * part == owned_ref[...]
            )


def one_hot(condition):
    return condition.astype(jnp.float32).astype(jnp.bfloat16)


def tissue(shifted, table_ref):
    conductivity = jnp.zeros_like(shifted)
    for level in range(table_ref.shape[0]):
        value = table_ref[level] if shifted.shape == table_ref.shape[1:] else table_ref[level, 0:1, 0:1]
        conductivity = jnp.where(shifted == level + 1, value, conductivity)
    return conductivity, (shifted > 0).astype(jnp.float32)


def edge_weight(first, second):
    return 0.5 * (first[0] + second[0]) * first[1] * second[1]


def weights(dims, shifted_ref, table_ref, halo_refs, z_ref, weight_ref):
    sensors, size_x, size_y, size_z = dims
    flags = neighbour_flags()
    (x_low, x_high), (y_low, y_high) = halo_refs
    beyond = z_ref[sensors : sensors + 1, :]
    half = size_z // 2

    def beyond_end(x, first, flag):
        line = 2 * (x * size_y + row_index) + first
        picked = jnp.where(lanes_equal(row_index.shape, line), beyond, 0.0)
        return masked(jnp.sum(picked, axis=1, keepdims=True), flag)

    def masked(value, flag):
        return jnp.where(flag, value, 0.0)

    own = [shifted_ref[x] for x in range(size_x)]
    own_tissue = [tissue(plane, table_ref) for plane in own]
    x_rows = slice(size_y * sensors, size_y * (sensors + 1))
    below = tissue(masked(x_low[x_rows, :], flags[0][0]), table_ref)
    above = tissue(masked(x_high[x_rows, :], flags[0][1]), table_ref)
    planes = [below] + own_tissue + [above]
    across_x = [edge_weight(planes[i], planes[i + 1]) for i in range(size_x + 1)]
    row_index = lax.broadcasted_iota(jnp.int32, (size_y, size_z), 0)
    lane_index = lax.broadcasted_iota(jnp.int32, (size_y, size_z), 1)
    for x in range(size_x):
        y_row = size_x * sensors + x
        shifted = own[x]
        y_before = jnp.where(
            row_index == 0,
            masked(y_low[y_row : y_row + 1, :], flags[1][0]),
            pltpu.roll(shifted, 1, 0),
        )
        y_after = jnp.where(
            row_index == size_y - 1,
            masked(y_high[y_row : y_row + 1, :], flags[1][1]),
            pltpu.roll(shifted, size_y - 1, 0),
        )
        z_before = jnp.where(
            lane_index == 0,
            beyond_end(x, 1, flags[2][0]),
            pltpu.roll(shifted, 1, 1),
        )
        z_after = jnp.where(
            lane_index == size_z - 1,
            beyond_end(x, half, flags[2][1]),
            pltpu.roll(shifted, size_z - 1, 1),
        )
        six = [across_x[x], across_x[x + 1]]
        for beside in (y_before, y_after, z_before, z_after):
            six.append(edge_weight(own_tissue[x], tissue(beside, table_ref)))
        for k, weight in enumerate(six):
            weight_ref[k, x] = weight
        weight_ref[6, x] = mass_term + (six[0] + six[1]) + (six[2] + six[3]) + (six[4] + six[5])
        weight_ref[7, x] = 0.5 * own_tissue[x][0]


def around(dims, rows_ref, halo_refs, z_ref, r, flags=None):
    sensors, size_x, size_y, size_z = dims
    (x_low, x_high), (y_low, y_high) = halo_refs
    x, y = divmod(r, size_y)
    z_low = z_ref[0:sensors, 2 * r + 1 : 2 * r + 2]
    high_lane = size_z // 2 + 2 * r
    z_high = z_ref[0:sensors, high_lane : high_lane + 1]

    def keep(value, dim, end):
        return value if flags is None else jnp.where(flags[dim][end], value, 0.0)

    def row(index):
        return rows_ref[index * sensors : (index + 1) * sensors, :]

    def part(ref, index):
        return ref[index * sensors : (index + 1) * sensors, :]

    centre = row(r)
    x_before = row(r - size_y) if x > 0 else keep(part(x_low, y), 0, 0)
    x_after = row(r + size_y) if x < size_x - 1 else keep(part(x_high, y), 0, 1)
    y_before = row(r - 1) if y > 0 else keep(part(y_low, x), 1, 0)
    y_after = row(r + 1) if y < size_y - 1 else keep(part(y_high, x), 1, 1)
    lane_index = lax.broadcasted_iota(jnp.int32, centre.shape, 1)
    z_before = jnp.where(
        lane_index == 0, keep(z_low, 2, 0), pltpu.roll(centre, 1, 1)
    )
    z_after = jnp.where(
        lane_index == size_z - 1,
        keep(z_high, 2, 1),
        pltpu.roll(centre, size_z - 1, 1),
    )
    return centre, (x_before, x_after, y_before, y_after, z_before, z_after)


def combine(weight_ref, x, y, centre, beside):
    total = weight_ref[6, x, y : y + 1, :] * centre
    for k, value in enumerate(beside):
        total = total - weight_ref[k, x, y : y + 1, :] * value
    return total


def x_ends(size_x):
    return sorted({0, size_x - 1})


def apply_rows(dims, rows_ref, weight_ref, halo_refs, z_ref, x, target_ref, place):
    sensors, size_y = dims[0], dims[2]
    for y in range(size_y):
        centre, beside = around(dims, rows_ref, halo_refs, z_ref, x * size_y + y)
        first = (place * size_y + y) * sensors
        target_ref[first : first + sensors, :] = combine(weight_ref, x, y, centre, beside)


def apply_ends_kernel(dims, counts, rows_ref, shifted_ref, table_ref, *refs):
    message_refs, refs = refs[: sum(counts)], refs[sum(counts) :]
    weight_ref, z_ref, edge_ref = refs[:3]
    halo_refs = sort_halos(message_refs, refs[3 + counts[0] :], counts)
    z_ref[...] = sort_ends(message_refs[sum(counts[:2]) :])
    weights(dims, shifted_ref, table_ref, halo_refs, z_ref, weight_ref)
    for place, x in enumerate(x_ends(dims[1])):
        apply_rows(dims, rows_ref, weight_ref, halo_refs, z_ref, x, edge_ref, place)
    write_x(dims, edge_ref, refs[3 : 3 + counts[0]], beyond=z_ref[...])


def apply_kernel(dims, counts, rows_ref, weight_ref, z_ref, edge_ref, *refs):
    sensors, size_x, size_y, size_z = dims
    message_refs, refs = refs[: sum(counts[:2])], refs[sum(counts[:2]) :]
    end_ref, applied_ref = refs[:2]
    halo_refs = sort_halos(message_refs, refs[2 + counts[1] :], counts)
    plane = size_y * sensors
    ends = x_ends(size_x)
    for x in range(size_x):
        if x in ends:
            place = ends.index(x)
            applied_ref[x * plane : (x + 1) * plane, :] = edge_ref[place * plane : (place + 1) * plane, :]
        else:
            apply_rows(dims, rows_ref, weight_ref, halo_refs, z_ref, x, applied_ref, x)
    write_y(dims, applied_ref, refs[2 : 2 + counts[1]], beyond=z_ref[...])
    lines = [(weight_ref[4, x], weight_ref[5, x]) for x in range(size_x)]
    outward = pack_lines(dims, lines, 1, 1)
    end_ref[...] = outward[0:1, :] * pack_rows(dims, applied_ref, 1, 1)


def halves(value):
    high = value.astype(jnp.bfloat16)
    return high, (value - high.astype(jnp.float32)).astype(jnp.bfloat16)


def local_twice(dims, rows_ref, weight_ref, r):
    sensors, size_x, size_y, size_z = dims
    x, y = divmod(r, size_y)

    def row(index):
        return rows_ref[index * sensors : (index + 1) * sensors, :]

    def weight(k):
        return weight_ref[k, x, y : y + 1, :]

    centre = row(r)
    lane_index = lax.broadcasted_iota(jnp.int32, centre.shape, 1)
    total = weight(6) * centre
    if x > 0:
        total = total - weight(0) * row(r - size_y)
    if x < size_x - 1:
        total = total - weight(1) * row(r + size_y)
    if y > 0:
        total = total - weight(2) * row(r - 1)
    if y < size_y - 1:
        total = total - weight(3) * row(r + 1)
    before = jnp.where(lane_index == 0, 0.0, pltpu.roll(centre, 1, 1))
    after = jnp.where(lane_index == size_z - 1, 0.0, pltpu.roll(centre, size_z - 1, 1))
    return total - weight(4) * before - weight(5) * after


def select_columns(dims, rows_ref, weight_ref, halo_refs, z_ref, chosen_ref, parts_ref):
    sensors, size_x, size_y, size_z = dims
    flags = neighbour_flags()
    width = 3 * sensors
    for r in range(size_x * size_y):
        x, y = divmod(r, size_y)
        span = slice(r * size_z, (r + 1) * size_z)
        scale = weight_ref[7, x, y : y + 1, :]
        _, beside = around(dims, rows_ref, halo_refs, z_ref, r, flags)
        for c in range(3):
            high, low = halves(scale * (beside[2 * c + 1] - beside[2 * c]))
            parts_ref[c * sensors : (c + 1) * sensors, span] = high
            parts_ref[width + c * sensors : width + (c + 1) * sensors, span] = low
    found = lax.dot_general(
        chosen_ref[...], parts_ref[...], last_with_last, preferred_element_type=jnp.float32
    )
    return found[:, :width] + found[:, width:]


def source_kernel(dims, counts, rows_ref, applied_ref, weight_ref, chosen_ref, z_ref, *refs):
    sensors, size_x, size_y, size_z = dims
    messages = sum(counts[:2])
    column_ref, sum_ref, parts_ref = refs[messages : messages + 3]
    halo_refs = sort_halos(refs[:messages], refs[messages + 3 :], counts)
    sums = [jnp.zeros((sensors, size_z), jnp.float32) for _ in range(4)]
    for r in range(size_x * size_y):
        source = rows_ref[r * sensors : (r + 1) * sensors, :]
        applied = applied_ref[r * sensors : (r + 1) * sensors, :]
        twice = local_twice(dims, applied_ref, weight_ref, r)
        for k, product in enumerate(
            (source * source, source * applied, applied * applied, applied * twice)
        ):
            sums[k] = sums[k] + product
    for k in range(4):
        sum_ref[k * sensors : (k + 1) * sensors, :] = sums[k]
    column_ref[...] = select_columns(
        dims, rows_ref, weight_ref, halo_refs, z_ref, chosen_ref, parts_ref
    )


def packed_beside(dims, beyond, own, along_x, along_y):
    sensors, size_x, size_y, size_z = dims
    half = size_z // 2
    lane_index = lax.broadcasted_iota(jnp.int32, beyond.shape, 1)
    in_half = lane_index % half
    row = in_half // 2 % size_y

    def moved(value, lanes):
        return pltpu.roll(value, lanes % size_z, 1)

    def either(condition, value, lanes, other, back):
        return jnp.where(condition, moved(value, lanes), moved(other, back))

    step, wrap = 2 * size_y, 2 * size_y * (size_x - 1)
    return (
        either(in_half >= step, beyond, step, along_x[0], -wrap),
        either(in_half < wrap, beyond, -step, along_x[1], wrap),
        either(row > 0, beyond, 2, along_y[0], -2 * (size_y - 1)),
        either(row < size_y - 1, beyond, -2, along_y[1], 2 * (size_y - 1)),
        either(lane_index < half, beyond, 1, beyond, -1),
        either(lane_index < half, own, 1, own, -1),
    )


def moment_kernel(
    dims, counts, applied_ref, weight_ref, sum_ref, end_ref, own_ref, z_ref, table_ref, *refs
):
    sensors, size_x, size_y, size_z = dims
    messages = sum(counts[:2])
    moment_ref, plane_ref = refs[messages : messages + 2]
    halo_refs = sort_halos(refs[:messages], refs[messages + 2 :], counts)
    (x_low, x_high), (y_low, y_high) = halo_refs
    flags = neighbour_flags()

    def forwarded(pair, dim, first, last):
        start = (size_y, size_x)[dim] * sensors
        return [
            jnp.where(flags[dim][end], ref[start + first : start + last, :], 0.0)
            for end, ref in enumerate(pair)
        ]

    def of_lines(first, last):
        return packed_beside(
            dims,
            z_ref[first:last, :],
            own_ref[first:last, :],
            forwarded(halo_refs[0], 0, first, last),
            forwarded(halo_refs[1], 1, first, last),
        )

    middle = tissue(z_ref[sensors:, :], table_ref)
    six = [
        edge_weight(middle, tissue(label, table_ref))
        for label in of_lines(sensors, z_ref.shape[0])
    ]
    total = mass_term + (six[0] + six[1]) + (six[2] + six[3]) + (six[4] + six[5])
    plane = total[0:1, :] * z_ref[0:sensors, :]
    for weight, value in zip(six, of_lines(0, sensors)):
        plane = plane - weight[0:1, :] * value
    plane_ref[...] = plane

    def part(ref, index):
        return ref[index * sensors : (index + 1) * sensors, :]

    def crossing(k, r, beside):
        x, y = divmod(r, size_y)
        return weight_ref[k, x, y : y + 1, :] * part(applied_ref, r) * beside

    outward = jnp.zeros((sensors, size_z), jnp.float32)
    for y in range(size_y):
        outward = outward + crossing(0, y, part(x_low, y))
        outward = outward + crossing(1, (size_x - 1) * size_y + y, part(x_high, y))
    for x in range(size_x):
        outward = outward + crossing(2, x * size_y, part(y_low, x))
        outward = outward + crossing(3, x * size_y + size_y - 1, part(y_high, x))
    outward = outward + end_ref[...] * plane
    last = part(sum_ref, 3) - outward
    moment_ref[...] = lax.dot_general(
        jnp.ones((8, size_z), jnp.float32),
        jnp.concatenate([sum_ref[0 : 3 * sensors, :], last], axis=0),
        last_with_last,
        precision=lax.Precision.HIGHEST,
        preferred_element_type=jnp.float32,
    )


def payload_rows(sensors, slots_each):
    whole, rest = divmod(6 * sensors, lane_tile)
    fold = lane_tile // rest if rest else 0
    assert not fold or (fold * rest == lane_tile and slots_each % fold == 0)
    rows = whole * slots_each + (slots_each // fold if fold else 0)
    return whole, rest, fold, rows, -(-4 * sensors // lane_tile)


def applied_kernel(
    dims, counts, slots_each, applied_ref, weight_ref, chosen_ref, source_column_ref, z_ref, *refs
):
    sensors, messages = dims[0], sum(counts[:2])
    column_ref, parts_ref = refs[messages : messages + 2]
    halo_refs = sort_halos(refs[:messages], refs[messages + 2 :], counts)
    applied_columns = select_columns(
        dims, applied_ref, weight_ref, halo_refs, z_ref, chosen_ref, parts_ref
    )
    columns = jnp.concatenate([source_column_ref[...], applied_columns], axis=1)
    whole, rest, fold, rows, moment_rows = payload_rows(sensors, slots_each)
    for owner in range(columns.shape[0] // slots_each):
        mine = slice(owner * slots_each, (owner + 1) * slots_each)
        at = owner * (rows + moment_rows)
        for tile in range(whole):
            column_ref[at : at + slots_each, :] = columns[mine, tile * lane_tile : (tile + 1) * lane_tile]
            at += slots_each
        if fold:
            part = slots_each // fold
            others = columns[mine, whole * lane_tile :]
            column_ref[at : at + part, :] = jnp.concatenate(
                [others[k * part : (k + 1) * part, :] for k in range(fold)], axis=1
            )
            at += part
        column_ref[at : at + moment_rows, :] = jnp.zeros((moment_rows, lane_tile), jnp.float32)


def owner_kernel(sensors, slots_each, received_ref, chosen_ref, data_ref, projection_ref, gram_ref):
    whole, rest, fold, rows, moment_rows = payload_rows(sensors, slots_each)
    each = rows + moment_rows
    sources = received_ref.shape[0] // each
    slots = sources * slots_each

    def collected(start, count):
        return jnp.concatenate(
            [received_ref[k * each + start : k * each + start + count, :] for k in range(sources)],
            axis=0,
        )

    gathered = jnp.zeros((moment_rows, lane_tile), jnp.float32)
    for k in range(sources):
        gathered = gathered + received_ref[k * each + rows : (k + 1) * each, :]
    moments = []
    sensor_index = lax.broadcasted_iota(jnp.int32, (sensors, lane_tile), 0)
    lane_index = lax.broadcasted_iota(jnp.int32, (sensors, lane_tile), 1)
    for k in range(4):
        total = jnp.zeros((sensors, 1), jnp.float32)
        for row in range(moment_rows):
            here = lane_index + row * lane_tile == sensor_index + k * sensors
            picked = jnp.where(here, gathered[row : row + 1, :], 0.0)
            total = total + jnp.sum(picked, axis=1, keepdims=True)
        moments.append(total)
    moment_zero, moment_one, moment_two, moment_three = moments
    first_step = moment_zero / moment_one
    residue = first_step * first_step * moment_two - moment_zero
    growth = 1.0 + residue / moment_zero
    curvature = (
        growth * growth * moment_one
        - 2.0 * growth * first_step * moment_two
        + first_step * first_step * moment_three
    )
    second_step = residue / curvature
    source_coef = first_step + second_step * growth
    applied_coef = second_step * first_step
    contract = (((0,), (0,)), ((), ()))

    def selected(values, first):
        chosen = chosen_ref[first : first + values.shape[0], :]
        high, low = halves(values)
        return lax.dot_general(
            high, chosen, contract, preferred_element_type=jnp.float32
        ) + lax.dot_general(low, chosen, contract, preferred_element_type=jnp.float32)

    owned = [
        selected(collected(tile * slots_each, slots_each), 0) for tile in range(whole)
    ]
    if fold:
        folded = collected(whole * slots_each, slots_each // fold)
        others = jnp.zeros((rest, chosen_ref.shape[1]), jnp.float32)
        for k in range(fold):
            found = selected(folded, slots + k * (slots // fold))
            others = others + found[k * rest : (k + 1) * rest, :]
        owned.append(others)
    owned = jnp.concatenate(owned, axis=0)
    lead = []
    for c in range(3):
        source_part = owned[c * sensors : (c + 1) * sensors, :]
        applied_part = owned[(3 + c) * sensors : (4 + c) * sensors, :]
        lead.append(source_coef * source_part - applied_coef * applied_part)
        projection_ref[c] = lax.dot_general(
            data_ref[...],
            lead[c],
            contract,
            precision=lax.Precision.HIGHEST,
            preferred_element_type=jnp.float32,
        )
    for k, (first, second) in enumerate(entry_pairs):
        gram_ref[k : k + 1, :] = jnp.sum(lead[first] * lead[second], axis=0, keepdims=True)


def call(body, **arguments):
    return pl.pallas_call(
        body, compiler_params=pltpu.CompilerParams(vmem_limit_bytes=vmem_grant), **arguments
    )


def in_hbm(count):
    return [pl.BlockSpec(memory_space=pltpu.HBM)] * count


def held_in_hbm(*arrays):
    return [pltpu.with_memory_space_constraint(a, pltpu.HBM) for a in arrays]


def in_vmem(count):
    return [pl.BlockSpec(memory_space=pltpu.VMEM)] * count


def face_shapes(dims, counts, x_rows, y_rows):
    sensors, size_x, size_y, size_z = dims
    rows = (size_y * sensors + x_rows, size_x * sensors + y_rows)
    return [
        jax.ShapeDtypeStruct((row, size_z), jnp.float32)
        for row, count in zip(rows, counts)
        for _ in range(count)
    ]


def per_device(source_term, labels, conductivity_table, send_map, owner_slots, sensor_data):
    dims = source_term.shape
    sensors, size_x, size_y, size_z = dims
    rows_count = size_x * size_y
    counts = face_counts()
    messages = sum(counts[:2])
    owners = lax.axis_size("gx") * lax.axis_size("gy")
    slots = send_map.size
    slots_each = slots // owners
    _, _, fold, payload, moment_rows = payload_rows(sensors, slots_each)
    times = sensor_data.shape[1]
    positions = owner_slots.shape[0]

    voxels = rows_count * size_z

    def array(shape, dtype=jnp.float32):
        return jax.ShapeDtypeStruct(shape, dtype)

    parts = [pltpu.VMEM((6 * sensors, voxels), jnp.bfloat16)]
    field_shape = array((rows_count * sensors, size_z))
    ends_shape = array((sensors + 8, size_z))
    levels = conductivity_table.shape[0]
    small = (
        send_map.reshape(1, slots),
        owner_slots.reshape(1, positions),
        sensor_data,
        conductivity_table,
    )
    packed = call(
        functools.partial(pack_kernel, dims, counts),
        out_shape=[field_shape, array(labels.shape), array((levels, size_y, size_z))]
        + [array(value.shape, value.dtype) for value in small[:3]]
        + [ends_shape]
        + face_shapes(dims, counts, size_y, 8 * -(-size_x // 8)),
        in_specs=in_hbm(6),
        out_specs=in_vmem(7 + messages),
        scratch_shapes=[
            pltpu.VMEM((size_x, sensors, size_y, size_z), jnp.float32),
            pltpu.VMEM((size_x, size_y, size_z), jnp.int32),
            pltpu.SMEM((levels,), jnp.float32),
            pltpu.SemaphoreType.DMA((size_x + 5,)),
        ],
        name="pack",
    )(*held_in_hbm(source_term, labels, *small))
    rows, shifted, table, voxel, owned, data, own_ends, *faces = packed
    source_halos = exchange_all([*split_refs(faces, counts[:2]), [own_ends] * counts[2]])
    chosen, owned_chosen, table = call(
        functools.partial(prepare_kernel, size_z, (slots_each, fold)),
        out_shape=[
            array((slots, voxels), jnp.bfloat16),
            array((slots * (2 if fold else 1), positions), jnp.bfloat16),
            array(table.shape),
        ],
        in_specs=in_vmem(3),
        out_specs=in_vmem(3),
        name="prepare",
    )(voxel, owned, table)

    face_out = face_shapes(dims, counts, sensors + 8, sensors + 8)
    weight, beyond, edges, *x_faces = call(
        functools.partial(apply_ends_kernel, dims, counts),
        out_shape=[array((8, size_x, size_y, size_z)), ends_shape]
        + [array((len(x_ends(size_x)) * size_y * sensors, size_z))]
        + face_out[: counts[0]],
        in_specs=in_vmem(3 + messages + counts[2]),
        out_specs=in_vmem(3 + counts[0]),
        scratch_shapes=held_halos(source_halos, counts),
        name="apply_ends",
    )(rows, shifted, table, *source_halos)
    ends, applied, *y_faces = call(
        functools.partial(apply_kernel, dims, counts),
        out_shape=[array((sensors, size_z)), field_shape] + face_out[counts[0] :],
        in_specs=in_vmem(4 + messages),
        out_specs=in_vmem(2 + counts[1]),
        scratch_shapes=held_halos(source_halos, counts),
        name="apply",
    )(rows, weight, beyond, edges, *source_halos[:messages])
    applied_halos = exchange_all([x_faces, y_faces])

    source_columns, sums = call(
        functools.partial(source_kernel, dims, counts),
        out_shape=[array((slots, 3 * sensors)), array((4 * sensors, size_z))],
        in_specs=in_vmem(5 + messages),
        out_specs=in_vmem(2),
        scratch_shapes=parts + held_halos(source_halos, counts),
        name="source_columns",
    )(rows, applied, weight, chosen, beyond, *source_halos[:messages])
    moment, plane = call(
        functools.partial(moment_kernel, dims, counts),
        out_shape=[array((8, 4 * sensors)), array((sensors, size_z))],
        in_specs=in_vmem(7 + messages),
        out_specs=in_vmem(2),
        scratch_shapes=held_halos(applied_halos, counts),
        name="moments",
    )(applied, weight, sums, ends, own_ends, beyond, table, *applied_halos)
    moment = sum_over(moment, "gz")

    each = payload + moment_rows
    columns = call(
        functools.partial(applied_kernel, dims, counts, slots_each),
        out_shape=array((owners * each, lane_tile)),
        in_specs=in_vmem(5 + messages),
        out_specs=in_vmem(1)[0],
        scratch_shapes=parts + held_halos(applied_halos, counts),
        name="applied_columns",
    )(applied, weight, chosen, source_columns, plane, *applied_halos)
    place = lax.broadcasted_iota(jnp.int32, columns.shape, 0) % each
    stamp = jnp.pad(moment[0], (0, moment_rows * lane_tile - 4 * sensors)).reshape(-1, lane_tile)
    for row in range(moment_rows):
        columns = jnp.where(place == payload + row, stamp[row : row + 1], columns)
    received = lax.all_to_all(
        columns.reshape(owners, 1, each * lane_tile), ("gx", "gy"), 0, 0, tiled=True
    ).reshape(columns.shape)
    return call(
        functools.partial(owner_kernel, sensors, slots_each),
        out_shape=[array((3, times, positions)), array((6, positions))],
        in_specs=in_vmem(3),
        out_specs=in_vmem(2),
        name="owner",
    )(received, owned_chosen, data)


def solution(mesh):
    in_specs = (
        P(None, "gx", "gy", "gz"),
        P("gx", "gy", "gz"),
        P(),
        P("gx", "gy", "gz", None),
        P(("gx", "gy", "gz")),
        P(),
    )
    out_specs = (P(None, None, ("gx", "gy", "gz")), P(None, ("gx", "gy", "gz")))
    step = jax.shard_map(
        per_device, mesh=mesh, in_specs=in_specs, out_specs=out_specs, check_vma=False
    )
    return lambda *arguments: tuple(step(*arguments))
```

```python
import functools

import jax
import jax.numpy as jnp
from jax import lax
from jax.experimental import pallas as pl
from jax.experimental.pallas import tpu as pltpu
from jax.sharding import PartitionSpec as P

mass_term = 0.25
lane_tile = 128
axes = ("gx", "gy", "gz")
vmem_grant = 16 << 20
last_with_last = (((1,), (1,)), ((), ()))
entry_pairs = ((0, 0), (1, 1), (2, 2), (0, 1), (0, 2), (1, 2))


def swap(value, axis, odd):
    count, beside = lax.axis_size(axis), lax.axis_size("gz")
    partner = {}
    for first in range(odd, count - 1, 2):
        partner[first], partner[first + 1] = first + 1, first
    alone = [i for i in range(count) if i not in partner]
    if alone and axis != "gz" and beside % 2 == 0:
        table = [
            (i * beside + k, partner[i] * beside + k if i in partner else i * beside + (k ^ 1))
            for i in range(count)
            for k in range(beside)
        ]
        return lax.ppermute(value, (axis, "gz"), table)
    for source, target in zip(alone, alone[::-1]):
        partner[source] = target
    return lax.ppermute(value, axis, sorted(partner.items()))


def sum_over(value, axis):
    count = lax.axis_size(axis)
    steps = sorted(range(1, count), key=lambda d: (d != count // 2, d))
    if count & (count - 1) == 0:
        tables = [[(i, i ^ d) for i in range(count)] for d in steps]
    else:
        tables = [[(i, (i + d) % count) for i in range(count)] for d in steps]
    return value + sum(lax.ppermute(value, axis, table) for table in tables)


def face_counts():
    return [1 if lax.axis_size(axis) <= 2 else 2 for axis in axes]


def exchange_all(groups):
    halos = []
    for axis, group in zip(axes, groups):
        if lax.axis_size(axis) > 1:
            group = [swap(face, axis, odd) for odd, face in enumerate(group)]
        halos.extend(group)
    return halos


def sort_halos(halo_refs, held_refs, counts):
    sorted_refs, held_refs = [], list(held_refs)
    for axis, group in zip(axes, split_refs(halo_refs, counts[:2])):
        if len(group) == 1:
            sorted_refs.append((group[0], group[0]))
            continue
        even = lax.axis_index(axis) % 2 == 0
        below, above = held_refs.pop(0), held_refs.pop(0)
        first, second = group[0][...], group[1][...]
        below[...] = jnp.where(even, second, first)
        above[...] = jnp.where(even, first, second)
        sorted_refs.append((below, above))
    return sorted_refs


def sort_ends(z_refs):
    below = above = z_refs[0][...]
    if len(z_refs) == 2:
        even = lax.axis_index("gz") % 2 == 0
        below, above = (
            jnp.where(even, z_refs[1 - k][...], z_refs[k][...]) for k in range(2)
        )
    half = below.shape[1] // 2
    lane_index = lax.broadcasted_iota(jnp.int32, below.shape, 1)
    return pltpu.roll(jnp.where(lane_index < half, above, below), half, 1)


def held_halos(faces, counts):
    return [
        pltpu.VMEM(face.shape, face.dtype)
        for group in split_refs(faces, counts[:2])
        for face in (group if len(group) == 2 else [])
    ]


def lanes_equal(shape, value):
    return lax.broadcasted_iota(jnp.int32, shape, len(shape) - 1) == value


def neighbour_flags():
    flags = []
    for axis in axes:
        index = lax.axis_index(axis)
        flags.append((index > 0, index < lax.axis_size(axis) - 1))
    return flags


def high_end(axis, number):
    return lax.axis_index(axis) % 2 == number


def line_of(dims, rows_ref, r):
    sensors = dims[0]
    return rows_ref[pl.ds(pl.multiple_of(r * sensors, sensors), sensors), :]


def write_x(dims, rows_ref, refs, labels=None, beyond=None):
    sensors, size_x, size_y, size_z = dims
    last = rows_ref.shape[0] // (sensors * size_y) - 1
    for number, ref in enumerate(refs):
        high = high_end("gx", number)
        x = jnp.where(high, last, 0)
        for y in range(size_y):
            ref[y * sensors : (y + 1) * sensors, :] = line_of(dims, rows_ref, x * size_y + y)
        behind = beyond if labels is None else jnp.where(high, labels[-1], labels[0])
        ref[size_y * sensors :, :] = behind


def write_y(dims, rows_ref, refs, labels=None, beyond=None):
    sensors, size_x, size_y, size_z = dims
    for number, ref in enumerate(refs):
        high = high_end("gy", number)
        y = jnp.where(high, size_y - 1, 0)
        for x in range(size_x):
            ref[x * sensors : (x + 1) * sensors, :] = line_of(dims, rows_ref, x * size_y + y)
            if labels is not None:
                row = size_x * sensors + x
                ref[row : row + 1, :] = jnp.where(high, labels[x][size_y - 1 :, :], labels[x][0:1, :])
        if labels is None:
            ref[size_x * sensors :, :] = beyond


def put_lanes(packed, row, source, target, count):
    lanes = packed.shape[1]
    moved = pltpu.roll(row, (target - source) % lanes, 1)
    lane_index = lax.broadcasted_iota(jnp.int32, packed.shape, 1)
    return jnp.where((lane_index >= target) & (lane_index < target + count), moved, packed)


def pack_lines(dims, values, depth, low_shift):
    size_x, size_y, size_z = dims[1:]
    half = size_z // 2
    packed = jnp.zeros((size_y, size_z), jnp.float32)
    row_index = lax.broadcasted_iota(jnp.int32, packed.shape, 0)
    for x in range(size_x):
        line = 2 * (x * size_y + row_index)
        for p in range(depth):
            low, high = values[x]
            end = size_z - depth + p
            packed = jnp.where(lanes_equal(packed.shape, line + low_shift + p), low[:, p : p + 1], packed)
            packed = jnp.where(lanes_equal(packed.shape, line + half + p), high[:, end : end + 1], packed)
    return jnp.broadcast_to(jnp.sum(packed, axis=0, keepdims=True), (8, size_z))


def pack_rows(dims, rows_ref, depth, low_shift):
    sensors, size_x, size_y, size_z = dims
    half = size_z // 2
    assert 2 * size_x * size_y <= half
    packed = jnp.zeros((sensors, size_z), jnp.float32)
    for r in range(size_x * size_y):
        row = rows_ref[r * sensors : (r + 1) * sensors, :]
        packed = put_lanes(packed, row, 0, 2 * r + low_shift, depth)
        packed = put_lanes(packed, row, size_z - depth, half + 2 * r, depth)
    return packed


def split_refs(refs, counts):
    groups, start = [], 0
    for count in counts:
        groups.append(refs[start : start + count])
        start += count
    return groups


def pack_kernel(dims, counts, source_ref, label_ref, *refs):
    sensors, size_x, size_y, size_z = dims
    small_hbm, refs = refs[:4], refs[4:]
    (rows_ref, shifted_ref, table_ref), small_refs = refs[:3], refs[3:6]
    own_ref, refs = refs[6], refs[7:]
    face_refs = split_refs(refs[: sum(counts[:2])], counts[:2])
    staged_ref, label_vmem, level_ref, semaphores = refs[sum(counts[:2]) :]
    copies = [
        pltpu.make_async_copy(source_ref.at[:, x], staged_ref.at[x], semaphores.at[x])
        for x in range(size_x)
    ]
    moves = [(label_ref, label_vmem), *zip(small_hbm, (*small_refs, level_ref))]
    for k, move in enumerate(moves):
        copies.append(pltpu.make_async_copy(*move, semaphores.at[size_x + k]))
    for copy in copies[size_x:] + copies[:size_x]:
        copy.start()
    for copy in copies[size_x:]:
        copy.wait()
    for level in range(level_ref.shape[0]):
        table_ref[level] = jnp.full(table_ref.shape[1:], level_ref[level], jnp.float32)
    shifted = [(label_vmem[x] + 1).astype(jnp.float32) for x in range(size_x)]
    for x in range(size_x):
        shifted_ref[x] = shifted[x]
    flat = staged_ref.reshape(size_x, sensors * size_y, size_z)
    for x in range(size_x):
        copies[x].wait()
        for y in range(size_y):
            r = x * size_y + y
            rows_ref[r * sensors : (r + 1) * sensors, :] = flat[x, pl.ds(y, sensors, stride=size_y), :]
    write_x(dims, rows_ref, face_refs[0], labels=shifted)
    write_y(dims, rows_ref, face_refs[1], labels=shifted)
    own_ref[0:sensors, :] = pack_rows(dims, rows_ref, 2, 0)
    own_ref[sensors:, :] = pack_lines(dims, [(plane, plane) for plane in shifted], 2, 0)


def prepare_kernel(
    size_z, folding, voxel_ref, owned_ref, level_ref, chosen_ref, owned_chosen_ref, table_ref
):
    table_ref[...] = level_ref[...]
    slots, voxels = chosen_ref.shape
    square = (slots, slots)
    diagonal = lanes_equal(square, lax.broadcasted_iota(jnp.int32, square, 0))
    voxel = jnp.where(diagonal, voxel_ref[...].astype(jnp.float32), 0.0)
    voxel = jnp.sum(voxel, axis=1, keepdims=True).astype(jnp.int32)
    voxel = jnp.broadcast_to(voxel, (slots, size_z))
    row = voxel // size_z
    lane_index = lax.broadcasted_iota(jnp.int32, (slots, size_z), 1)
    lane = one_hot(lane_index == voxel - row * size_z)
    row = row.astype(jnp.float32).astype(jnp.bfloat16)
    none = jnp.zeros_like(lane)
    for r in range(voxels // size_z):
        chosen_ref[:, r * size_z : (r + 1) * size_z] = jnp.where(row == r, lane, none)
    row_index = lax.broadcasted_iota(jnp.int32, (slots, owned_ref.shape[1]), 0)
    owned_chosen_ref[0:slots, :] = one_hot(row_index == owned_ref[...])
    slots_each, fold = folding
    if fold:
        part = slots_each // fold
        row_index = lax.broadcasted_iota(jnp.int32, (slots // fold, owned_ref.shape[1]), 0)
        slot_index = row_index // part * slots_each + row_index % part
        for k in range(fold):
            first = slots + k * (slots // fold)
            owned_chosen_ref[first : first + slots // fold, :] = one_hot(
                slot_index + k * part == owned_ref[...]
            )


def one_hot(condition):
    return condition.astype(jnp.float32).astype(jnp.bfloat16)


def tissue(shifted, table_ref):
    conductivity = jnp.zeros_like(shifted)
    for level in range(table_ref.shape[0]):
        value = table_ref[level] if shifted.shape == table_ref.shape[1:] else table_ref[level, 0:1, 0:1]
        conductivity = jnp.where(shifted == level + 1, value, conductivity)
    return conductivity, (shifted > 0).astype(jnp.float32)


def edge_weight(first, second):
    return 0.5 * (first[0] + second[0]) * first[1] * second[1]


def weights(dims, shifted_ref, table_ref, halo_refs, z_ref, weight_ref):
    sensors, size_x, size_y, size_z = dims
    flags = neighbour_flags()
    (x_low, x_high), (y_low, y_high) = halo_refs
    beyond = z_ref[sensors : sensors + 1, :]
    half = size_z // 2

    def beyond_end(x, first, flag):
        line = 2 * (x * size_y + row_index) + first
        picked = jnp.where(lanes_equal(row_index.shape, line), beyond, 0.0)
        return masked(jnp.sum(picked, axis=1, keepdims=True), flag)

    def masked(value, flag):
        return jnp.where(flag, value, 0.0)

    own = [shifted_ref[x] for x in range(size_x)]
    own_tissue = [tissue(plane, table_ref) for plane in own]
    x_rows = slice(size_y * sensors, size_y * (sensors + 1))
    below = tissue(masked(x_low[x_rows, :], flags[0][0]), table_ref)
    above = tissue(masked(x_high[x_rows, :], flags[0][1]), table_ref)
    planes = [below] + own_tissue + [above]
    across_x = [edge_weight(planes[i], planes[i + 1]) for i in range(size_x + 1)]
    row_index = lax.broadcasted_iota(jnp.int32, (size_y, size_z), 0)
    lane_index = lax.broadcasted_iota(jnp.int32, (size_y, size_z), 1)
    for x in range(size_x):
        y_row = size_x * sensors + x
        shifted = own[x]
        y_before = jnp.where(
            row_index == 0,
            masked(y_low[y_row : y_row + 1, :], flags[1][0]),
            pltpu.roll(shifted, 1, 0),
        )
        y_after = jnp.where(
            row_index == size_y - 1,
            masked(y_high[y_row : y_row + 1, :], flags[1][1]),
            pltpu.roll(shifted, size_y - 1, 0),
        )
        z_before = jnp.where(
            lane_index == 0,
            beyond_end(x, 1, flags[2][0]),
            pltpu.roll(shifted, 1, 1),
        )
        z_after = jnp.where(
            lane_index == size_z - 1,
            beyond_end(x, half, flags[2][1]),
            pltpu.roll(shifted, size_z - 1, 1),
        )
        six = [across_x[x], across_x[x + 1]]
        for beside in (y_before, y_after, z_before, z_after):
            six.append(edge_weight(own_tissue[x], tissue(beside, table_ref)))
        for k, weight in enumerate(six):
            weight_ref[k, x] = weight
        weight_ref[6, x] = mass_term + (six[0] + six[1]) + (six[2] + six[3]) + (six[4] + six[5])
        weight_ref[7, x] = 0.5 * own_tissue[x][0]


def around(dims, rows_ref, halo_refs, z_ref, r, flags=None):
    sensors, size_x, size_y, size_z = dims
    (x_low, x_high), (y_low, y_high) = halo_refs
    x, y = divmod(r, size_y)
    z_low = z_ref[0:sensors, 2 * r + 1 : 2 * r + 2]
    high_lane = size_z // 2 + 2 * r
    z_high = z_ref[0:sensors, high_lane : high_lane + 1]

    def keep(value, dim, end):
        return value if flags is None else jnp.where(flags[dim][end], value, 0.0)

    def row(index):
        return rows_ref[index * sensors : (index + 1) * sensors, :]

    def part(ref, index):
        return ref[index * sensors : (index + 1) * sensors, :]

    centre = row(r)
    x_before = row(r - size_y) if x > 0 else keep(part(x_low, y), 0, 0)
    x_after = row(r + size_y) if x < size_x - 1 else keep(part(x_high, y), 0, 1)
    y_before = row(r - 1) if y > 0 else keep(part(y_low, x), 1, 0)
    y_after = row(r + 1) if y < size_y - 1 else keep(part(y_high, x), 1, 1)
    lane_index = lax.broadcasted_iota(jnp.int32, centre.shape, 1)
    z_before = jnp.where(
        lane_index == 0, keep(z_low, 2, 0), pltpu.roll(centre, 1, 1)
    )
    z_after = jnp.where(
        lane_index == size_z - 1,
        keep(z_high, 2, 1),
        pltpu.roll(centre, size_z - 1, 1),
    )
    return centre, (x_before, x_after, y_before, y_after, z_before, z_after)


def combine(weight_ref, x, y, centre, beside):
    total = weight_ref[6, x, y : y + 1, :] * centre
    for k, value in enumerate(beside):
        total = total - weight_ref[k, x, y : y + 1, :] * value
    return total


def x_ends(size_x):
    return sorted({0, size_x - 1})


def apply_rows(dims, rows_ref, weight_ref, halo_refs, z_ref, x, target_ref, place):
    sensors, size_y = dims[0], dims[2]
    for y in range(size_y):
        centre, beside = around(dims, rows_ref, halo_refs, z_ref, x * size_y + y)
        first = (place * size_y + y) * sensors
        target_ref[first : first + sensors, :] = combine(weight_ref, x, y, centre, beside)


def apply_ends_kernel(dims, counts, rows_ref, shifted_ref, table_ref, *refs):
    message_refs, refs = refs[: sum(counts)], refs[sum(counts) :]
    weight_ref, z_ref, edge_ref = refs[:3]
    halo_refs = sort_halos(message_refs, refs[3 + counts[0] :], counts)
    z_ref[...] = sort_ends(message_refs[sum(counts[:2]) :])
    weights(dims, shifted_ref, table_ref, halo_refs, z_ref, weight_ref)
    for place, x in enumerate(x_ends(dims[1])):
        apply_rows(dims, rows_ref, weight_ref, halo_refs, z_ref, x, edge_ref, place)
    write_x(dims, edge_ref, refs[3 : 3 + counts[0]], beyond=z_ref[...])


def apply_kernel(dims, counts, rows_ref, weight_ref, z_ref, edge_ref, *refs):
    sensors, size_x, size_y, size_z = dims
    message_refs, refs = refs[: sum(counts[:2])], refs[sum(counts[:2]) :]
    end_ref, applied_ref = refs[:2]
    halo_refs = sort_halos(message_refs, refs[2 + counts[1] :], counts)
    plane = size_y * sensors
    ends = x_ends(size_x)
    for x in range(size_x):
        if x in ends:
            place = ends.index(x)
            applied_ref[x * plane : (x + 1) * plane, :] = edge_ref[place * plane : (place + 1) * plane, :]
        else:
            apply_rows(dims, rows_ref, weight_ref, halo_refs, z_ref, x, applied_ref, x)
    write_y(dims, applied_ref, refs[2 : 2 + counts[1]], beyond=z_ref[...])
    lines = [(weight_ref[4, x], weight_ref[5, x]) for x in range(size_x)]
    outward = pack_lines(dims, lines, 1, 1)
    end_ref[...] = outward[0:1, :] * pack_rows(dims, applied_ref, 1, 1)


def halves(value):
    high = value.astype(jnp.bfloat16)
    return high, (value - high.astype(jnp.float32)).astype(jnp.bfloat16)


def local_twice(dims, rows_ref, weight_ref, r):
    sensors, size_x, size_y, size_z = dims
    x, y = divmod(r, size_y)

    def row(index):
        return rows_ref[index * sensors : (index + 1) * sensors, :]

    def weight(k):
        return weight_ref[k, x, y : y + 1, :]

    centre = row(r)
    lane_index = lax.broadcasted_iota(jnp.int32, centre.shape, 1)
    total = weight(6) * centre
    if x > 0:
        total = total - weight(0) * row(r - size_y)
    if x < size_x - 1:
        total = total - weight(1) * row(r + size_y)
    if y > 0:
        total = total - weight(2) * row(r - 1)
    if y < size_y - 1:
        total = total - weight(3) * row(r + 1)
    before = jnp.where(lane_index == 0, 0.0, pltpu.roll(centre, 1, 1))
    after = jnp.where(lane_index == size_z - 1, 0.0, pltpu.roll(centre, size_z - 1, 1))
    return total - weight(4) * before - weight(5) * after


def select_columns(dims, rows_ref, weight_ref, halo_refs, z_ref, chosen_ref, parts_ref):
    sensors, size_x, size_y, size_z = dims
    flags = neighbour_flags()
    width = 3 * sensors
    for r in range(size_x * size_y):
        x, y = divmod(r, size_y)
        span = slice(r * size_z, (r + 1) * size_z)
        scale = weight_ref[7, x, y : y + 1, :]
        _, beside = around(dims, rows_ref, halo_refs, z_ref, r, flags)
        for c in range(3):
            high, low = halves(scale * (beside[2 * c + 1] - beside[2 * c]))
            parts_ref[c * sensors : (c + 1) * sensors, span] = high
            parts_ref[width + c * sensors : width + (c + 1) * sensors, span] = low
    found = lax.dot_general(
        chosen_ref[...], parts_ref[...], last_with_last, preferred_element_type=jnp.float32
    )
    return found[:, :width] + found[:, width:]


def source_kernel(dims, counts, rows_ref, applied_ref, weight_ref, chosen_ref, z_ref, *refs):
    sensors, size_x, size_y, size_z = dims
    messages = sum(counts[:2])
    column_ref, sum_ref, parts_ref = refs[messages : messages + 3]
    halo_refs = sort_halos(refs[:messages], refs[messages + 3 :], counts)
    sums = [jnp.zeros((sensors, size_z), jnp.float32) for _ in range(4)]
    for r in range(size_x * size_y):
        source = rows_ref[r * sensors : (r + 1) * sensors, :]
        applied = applied_ref[r * sensors : (r + 1) * sensors, :]
        twice = local_twice(dims, applied_ref, weight_ref, r)
        for k, product in enumerate(
            (source * source, source * applied, applied * applied, applied * twice)
        ):
            sums[k] = sums[k] + product
    for k in range(4):
        sum_ref[k * sensors : (k + 1) * sensors, :] = sums[k]
    column_ref[...] = select_columns(
        dims, rows_ref, weight_ref, halo_refs, z_ref, chosen_ref, parts_ref
    )


def packed_beside(dims, beyond, own, along_x, along_y):
    sensors, size_x, size_y, size_z = dims
    half = size_z // 2
    lane_index = lax.broadcasted_iota(jnp.int32, beyond.shape, 1)
    in_half = lane_index % half
    row = in_half // 2 % size_y

    def moved(value, lanes):
        return pltpu.roll(value, lanes % size_z, 1)

    def either(condition, value, lanes, other, back):
        return jnp.where(condition, moved(value, lanes), moved(other, back))

    step, wrap = 2 * size_y, 2 * size_y * (size_x - 1)
    return (
        either(in_half >= step, beyond, step, along_x[0], -wrap),
        either(in_half < wrap, beyond, -step, along_x[1], wrap),
        either(row > 0, beyond, 2, along_y[0], -2 * (size_y - 1)),
        either(row < size_y - 1, beyond, -2, along_y[1], 2 * (size_y - 1)),
        either(lane_index < half, beyond, 1, beyond, -1),
        either(lane_index < half, own, 1, own, -1),
    )


def moment_kernel(
    dims, counts, applied_ref, weight_ref, sum_ref, end_ref, own_ref, z_ref, table_ref, *refs
):
    sensors, size_x, size_y, size_z = dims
    messages = sum(counts[:2])
    moment_ref, plane_ref = refs[messages : messages + 2]
    halo_refs = sort_halos(refs[:messages], refs[messages + 2 :], counts)
    (x_low, x_high), (y_low, y_high) = halo_refs
    flags = neighbour_flags()

    def forwarded(pair, dim, first, last):
        start = (size_y, size_x)[dim] * sensors
        return [
            jnp.where(flags[dim][end], ref[start + first : start + last, :], 0.0)
            for end, ref in enumerate(pair)
        ]

    def of_lines(first, last):
        return packed_beside(
            dims,
            z_ref[first:last, :],
            own_ref[first:last, :],
            forwarded(halo_refs[0], 0, first, last),
            forwarded(halo_refs[1], 1, first, last),
        )

    middle = tissue(z_ref[sensors:, :], table_ref)
    six = [
        edge_weight(middle, tissue(label, table_ref))
        for label in of_lines(sensors, z_ref.shape[0])
    ]
    total = mass_term + (six[0] + six[1]) + (six[2] + six[3]) + (six[4] + six[5])
    plane = total[0:1, :] * z_ref[0:sensors, :]
    for weight, value in zip(six, of_lines(0, sensors)):
        plane = plane - weight[0:1, :] * value
    plane_ref[...] = plane

    def part(ref, index):
        return ref[index * sensors : (index + 1) * sensors, :]

    def crossing(k, r, beside):
        x, y = divmod(r, size_y)
        return weight_ref[k, x, y : y + 1, :] * part(applied_ref, r) * beside

    outward = jnp.zeros((sensors, size_z), jnp.float32)
    for y in range(size_y):
        outward = outward + crossing(0, y, part(x_low, y))
        outward = outward + crossing(1, (size_x - 1) * size_y + y, part(x_high, y))
    for x in range(size_x):
        outward = outward + crossing(2, x * size_y, part(y_low, x))
        outward = outward + crossing(3, x * size_y + size_y - 1, part(y_high, x))
    outward = outward + end_ref[...] * plane
    last = part(sum_ref, 3) - outward
    moment_ref[...] = lax.dot_general(
        jnp.ones((8, size_z), jnp.float32),
        jnp.concatenate([sum_ref[0 : 3 * sensors, :], last], axis=0),
        last_with_last,
        precision=lax.Precision.HIGHEST,
        preferred_element_type=jnp.float32,
    )


def payload_rows(sensors, slots_each):
    whole, rest = divmod(6 * sensors, lane_tile)
    fold = lane_tile // rest if rest else 0
    assert not fold or (fold * rest == lane_tile and slots_each % fold == 0)
    rows = whole * slots_each + (slots_each // fold if fold else 0)
    return whole, rest, fold, rows, -(-4 * sensors // lane_tile)


def applied_kernel(
    dims, counts, slots_each, applied_ref, weight_ref, chosen_ref, source_column_ref, z_ref, *refs
):
    sensors, messages = dims[0], sum(counts[:2])
    column_ref, parts_ref = refs[messages : messages + 2]
    halo_refs = sort_halos(refs[:messages], refs[messages + 2 :], counts)
    applied_columns = select_columns(
        dims, applied_ref, weight_ref, halo_refs, z_ref, chosen_ref, parts_ref
    )
    columns = jnp.concatenate([source_column_ref[...], applied_columns], axis=1)
    whole, rest, fold, rows, moment_rows = payload_rows(sensors, slots_each)
    for owner in range(columns.shape[0] // slots_each):
        mine = slice(owner * slots_each, (owner + 1) * slots_each)
        at = owner * (rows + moment_rows)
        for tile in range(whole):
            column_ref[at : at + slots_each, :] = columns[mine, tile * lane_tile : (tile + 1) * lane_tile]
            at += slots_each
        if fold:
            part = slots_each // fold
            others = columns[mine, whole * lane_tile :]
            column_ref[at : at + part, :] = jnp.concatenate(
                [others[k * part : (k + 1) * part, :] for k in range(fold)], axis=1
            )
            at += part
        column_ref[at : at + moment_rows, :] = jnp.zeros((moment_rows, lane_tile), jnp.float32)


def owner_kernel(sensors, slots_each, received_ref, chosen_ref, data_ref, projection_ref, gram_ref):
    whole, rest, fold, rows, moment_rows = payload_rows(sensors, slots_each)
    each = rows + moment_rows
    sources = received_ref.shape[0] // each
    slots = sources * slots_each

    def collected(start, count):
        return jnp.concatenate(
            [received_ref[k * each + start : k * each + start + count, :] for k in range(sources)],
            axis=0,
        )

    gathered = jnp.zeros((moment_rows, lane_tile), jnp.float32)
    for k in range(sources):
        gathered = gathered + received_ref[k * each + rows : (k + 1) * each, :]
    moments = []
    sensor_index = lax.broadcasted_iota(jnp.int32, (sensors, lane_tile), 0)
    lane_index = lax.broadcasted_iota(jnp.int32, (sensors, lane_tile), 1)
    for k in range(4):
        total = jnp.zeros((sensors, 1), jnp.float32)
        for row in range(moment_rows):
            here = lane_index + row * lane_tile == sensor_index + k * sensors
            picked = jnp.where(here, gathered[row : row + 1, :], 0.0)
            total = total + jnp.sum(picked, axis=1, keepdims=True)
        moments.append(total)
    moment_zero, moment_one, moment_two, moment_three = moments
    first_step = moment_zero / moment_one
    residue = first_step * first_step * moment_two - moment_zero
    growth = 1.0 + residue / moment_zero
    curvature = (
        growth * growth * moment_one
        - 2.0 * growth * first_step * moment_two
        + first_step * first_step * moment_three
    )
    second_step = residue / curvature
    source_coef = first_step + second_step * growth
    applied_coef = second_step * first_step
    contract = (((0,), (0,)), ((), ()))

    def selected(values, first):
        chosen = chosen_ref[first : first + values.shape[0], :]
        high, low = halves(values)
        return lax.dot_general(
            high, chosen, contract, preferred_element_type=jnp.float32
        ) + lax.dot_general(low, chosen, contract, preferred_element_type=jnp.float32)

    owned = [
        selected(collected(tile * slots_each, slots_each), 0) for tile in range(whole)
    ]
    if fold:
        folded = collected(whole * slots_each, slots_each // fold)
        others = jnp.zeros((rest, chosen_ref.shape[1]), jnp.float32)
        for k in range(fold):
            found = selected(folded, slots + k * (slots // fold))
            others = others + found[k * rest : (k + 1) * rest, :]
        owned.append(others)
    owned = jnp.concatenate(owned, axis=0)
    lead = []
    for c in range(3):
        source_part = owned[c * sensors : (c + 1) * sensors, :]
        applied_part = owned[(3 + c) * sensors : (4 + c) * sensors, :]
        lead.append(source_coef * source_part - applied_coef * applied_part)
        projection_ref[c] = lax.dot_general(
            data_ref[...],
            lead[c],
            contract,
            precision=lax.Precision.HIGHEST,
            preferred_element_type=jnp.float32,
        )
    for k, (first, second) in enumerate(entry_pairs):
        gram_ref[k : k + 1, :] = jnp.sum(lead[first] * lead[second], axis=0, keepdims=True)


def call(body, **arguments):
    return pl.pallas_call(
        body, compiler_params=pltpu.CompilerParams(vmem_limit_bytes=vmem_grant), **arguments
    )


def in_hbm(count):
    return [pl.BlockSpec(memory_space=pltpu.HBM)] * count


def held_in_hbm(*arrays):
    return [pltpu.with_memory_space_constraint(a, pltpu.HBM) for a in arrays]


def in_vmem(count):
    return [pl.BlockSpec(memory_space=pltpu.VMEM)] * count


def face_shapes(dims, counts, x_rows, y_rows):
    sensors, size_x, size_y, size_z = dims
    rows = (size_y * sensors + x_rows, size_x * sensors + y_rows)
    return [
        jax.ShapeDtypeStruct((row, size_z), jnp.float32)
        for row, count in zip(rows, counts)
        for _ in range(count)
    ]


def per_device(source_term, labels, conductivity_table, send_map, owner_slots, sensor_data):
    dims = source_term.shape
    sensors, size_x, size_y, size_z = dims
    rows_count = size_x * size_y
    counts = face_counts()
    messages = sum(counts[:2])
    owners = lax.axis_size("gx") * lax.axis_size("gy")
    slots = send_map.size
    slots_each = slots // owners
    _, _, fold, payload, moment_rows = payload_rows(sensors, slots_each)
    times = sensor_data.shape[1]
    positions = owner_slots.shape[0]

    voxels = rows_count * size_z

    def array(shape, dtype=jnp.float32):
        return jax.ShapeDtypeStruct(shape, dtype)

    parts = [pltpu.VMEM((6 * sensors, voxels), jnp.bfloat16)]
    field_shape = array((rows_count * sensors, size_z))
    ends_shape = array((sensors + 8, size_z))
    levels = conductivity_table.shape[0]
    small = (
        send_map.reshape(1, slots),
        owner_slots.reshape(1, positions),
        sensor_data,
        conductivity_table,
    )
    packed = call(
        functools.partial(pack_kernel, dims, counts),
        out_shape=[field_shape, array(labels.shape), array((levels, size_y, size_z))]
        + [array(value.shape, value.dtype) for value in small[:3]]
        + [ends_shape]
        + face_shapes(dims, counts, size_y, 8 * -(-size_x // 8)),
        in_specs=in_hbm(6),
        out_specs=in_vmem(7 + messages),
        scratch_shapes=[
            pltpu.VMEM((size_x, sensors, size_y, size_z), jnp.float32),
            pltpu.VMEM((size_x, size_y, size_z), jnp.int32),
            pltpu.SMEM((levels,), jnp.float32),
            pltpu.SemaphoreType.DMA((size_x + 5,)),
        ],
        name="pack",
    )(*held_in_hbm(source_term, labels, *small))
    rows, shifted, table, voxel, owned, data, own_ends, *faces = packed
    source_halos = exchange_all([*split_refs(faces, counts[:2]), [own_ends] * counts[2]])
    chosen, owned_chosen, table = call(
        functools.partial(prepare_kernel, size_z, (slots_each, fold)),
        out_shape=[
            array((slots, voxels), jnp.bfloat16),
            array((slots * (2 if fold else 1), positions), jnp.bfloat16),
            array(table.shape),
        ],
        in_specs=in_vmem(3),
        out_specs=in_vmem(3),
        name="prepare",
    )(voxel, owned, table)

    face_out = face_shapes(dims, counts, sensors + 8, sensors + 8)
    weight, beyond, edges, *x_faces = call(
        functools.partial(apply_ends_kernel, dims, counts),
        out_shape=[array((8, size_x, size_y, size_z)), ends_shape]
        + [array((len(x_ends(size_x)) * size_y * sensors, size_z))]
        + face_out[: counts[0]],
        in_specs=in_vmem(3 + messages + counts[2]),
        out_specs=in_vmem(3 + counts[0]),
        scratch_shapes=held_halos(source_halos, counts),
        name="apply_ends",
    )(rows, shifted, table, *source_halos)
    ends, applied, *y_faces = call(
        functools.partial(apply_kernel, dims, counts),
        out_shape=[array((sensors, size_z)), field_shape] + face_out[counts[0] :],
        in_specs=in_vmem(4 + messages),
        out_specs=in_vmem(2 + counts[1]),
        scratch_shapes=held_halos(source_halos, counts),
        name="apply",
    )(rows, weight, beyond, edges, *source_halos[:messages])
    applied_halos = exchange_all([x_faces, y_faces])

    source_columns, sums = call(
        functools.partial(source_kernel, dims, counts),
        out_shape=[array((slots, 3 * sensors)), array((4 * sensors, size_z))],
        in_specs=in_vmem(5 + messages),
        out_specs=in_vmem(2),
        scratch_shapes=parts + held_halos(source_halos, counts),
        name="source_columns",
    )(rows, applied, weight, chosen, beyond, *source_halos[:messages])
    moment, plane = call(
        functools.partial(moment_kernel, dims, counts),
        out_shape=[array((8, 4 * sensors)), array((sensors, size_z))],
        in_specs=in_vmem(7 + messages),
        out_specs=in_vmem(2),
        scratch_shapes=held_halos(applied_halos, counts),
        name="moments",
    )(applied, weight, sums, ends, own_ends, beyond, table, *applied_halos)
    moment = sum_over(moment, "gz")

    each = payload + moment_rows
    columns = call(
        functools.partial(applied_kernel, dims, counts, slots_each),
        out_shape=array((owners * each, lane_tile)),
        in_specs=in_vmem(5 + messages),
        out_specs=in_vmem(1)[0],
        scratch_shapes=parts + held_halos(applied_halos, counts),
        name="applied_columns",
    )(applied, weight, chosen, source_columns, plane, *applied_halos)
    place = lax.broadcasted_iota(jnp.int32, columns.shape, 0) % each
    stamp = jnp.pad(moment[0], (0, moment_rows * lane_tile - 4 * sensors)).reshape(-1, lane_tile)
    for row in range(moment_rows):
        columns = jnp.where(place == payload + row, stamp[row : row + 1], columns)
    received = lax.all_to_all(
        columns.reshape(owners, 1, each * lane_tile), ("gx", "gy"), 0, 0, tiled=True
    ).reshape(columns.shape)
    return call(
        functools.partial(owner_kernel, sensors, slots_each),
        out_shape=[array((3, times, positions)), array((6, positions))],
        in_specs=in_vmem(3),
        out_specs=in_vmem(2),
        name="owner",
    )(received, owned_chosen, data)


def solution(mesh):
    in_specs = (
        P(None, "gx", "gy", "gz"),
        P("gx", "gy", "gz"),
        P(),
        P("gx", "gy", "gz", None),
        P(("gx", "gy", "gz")),
        P(),
    )
    out_specs = (P(None, None, ("gx", "gy", "gz")), P(None, ("gx", "gy", "gz")))
    step = jax.shard_map(
        per_device, mesh=mesh, in_specs=in_specs, out_specs=out_specs, check_vma=False
    )
    return lambda *arguments: tuple(step(*arguments))
```

```python
import functools

import jax
import jax.numpy as jnp
from jax import lax
from jax.experimental import pallas as pl
from jax.experimental.pallas import tpu as pltpu
from jax.sharding import PartitionSpec as P

mass_term = 0.25
lane_tile = 128
axes = ("gx", "gy", "gz")
vmem_grant = 16 << 20
last_with_last = (((1,), (1,)), ((), ()))
entry_pairs = ((0, 0), (1, 1), (2, 2), (0, 1), (0, 2), (1, 2))


def swap(value, axis, odd):
    count, beside = lax.axis_size(axis), lax.axis_size("gz")
    partner = {}
    for first in range(odd, count - 1, 2):
        partner[first], partner[first + 1] = first + 1, first
    alone = [i for i in range(count) if i not in partner]
    if alone and axis != "gz" and beside % 2 == 0:
        table = [
            (i * beside + k, partner[i] * beside + k if i in partner else i * beside + (k ^ 1))
            for i in range(count)
            for k in range(beside)
        ]
        return lax.ppermute(value, (axis, "gz"), table)
    for source, target in zip(alone, alone[::-1]):
        partner[source] = target
    return lax.ppermute(value, axis, sorted(partner.items()))


def sum_over(value, axis):
    count = lax.axis_size(axis)
    steps = [count - 1, *range(1, count - 1)][: count - 1]
    if count & (count - 1) == 0:
        tables = [[(i, i ^ d) for i in range(count)] for d in steps]
    else:
        tables = [[(i, (i + d) % count) for i in range(count)] for d in steps]
    return value + sum(lax.ppermute(value, axis, table) for table in tables)


def face_counts():
    return [1 if lax.axis_size(axis) <= 2 else 2 for axis in axes]


def exchange_all(groups):
    halos = []
    for axis, group in zip(axes, groups):
        if lax.axis_size(axis) > 1:
            group = [swap(face, axis, odd) for odd, face in enumerate(group)]
        halos.extend(group)
    return halos


def sort_halos(halo_refs, held_refs, counts):
    sorted_refs, held_refs = [], list(held_refs)
    for axis, group in zip(axes, split_refs(halo_refs, counts[:2])):
        if len(group) == 1:
            sorted_refs.append((group[0], group[0]))
            continue
        even = lax.axis_index(axis) % 2 == 0
        below, above = held_refs.pop(0), held_refs.pop(0)
        first, second = group[0][...], group[1][...]
        below[...] = jnp.where(even, second, first)
        above[...] = jnp.where(even, first, second)
        sorted_refs.append((below, above))
    return sorted_refs


def sort_ends(z_refs):
    below = above = z_refs[0][...]
    if len(z_refs) == 2:
        even = lax.axis_index("gz") % 2 == 0
        below, above = (
            jnp.where(even, z_refs[1 - k][...], z_refs[k][...]) for k in range(2)
        )
    half = below.shape[1] // 2
    lane_index = lax.broadcasted_iota(jnp.int32, below.shape, 1)
    return pltpu.roll(jnp.where(lane_index < half, above, below), half, 1)


def held_halos(faces, counts):
    return [
        pltpu.VMEM(face.shape, face.dtype)
        for group in split_refs(faces, counts[:2])
        for face in (group if len(group) == 2 else [])
    ]


def lanes_equal(shape, value):
    return lax.broadcasted_iota(jnp.int32, shape, len(shape) - 1) == value


def neighbour_flags():
    flags = []
    for axis in axes:
        index = lax.axis_index(axis)
        flags.append((index > 0, index < lax.axis_size(axis) - 1))
    return flags


def write_faces(dims, rows_ref, face_refs, labels=None, beyond=None):
    sensors, size_x, size_y, size_z = dims
    x_refs, y_refs = face_refs

    def field(r):
        return rows_ref[pl.ds(pl.multiple_of(r * sensors, sensors), sensors), :]

    def high_end(axis, number):
        return lax.axis_index(axis) % 2 == number

    for number, ref in enumerate(x_refs):
        high = high_end("gx", number)
        x = jnp.where(high, size_x - 1, 0)
        for y in range(size_y):
            ref[y * sensors : (y + 1) * sensors, :] = field(x * size_y + y)
        if labels is not None:
            ref[size_y * sensors :, :] = jnp.where(high, labels[-1], labels[0])
        else:
            ref[size_y * sensors :, :] = beyond

    for number, ref in enumerate(y_refs):
        high = high_end("gy", number)
        y = jnp.where(high, size_y - 1, 0)
        for x in range(size_x):
            ref[x * sensors : (x + 1) * sensors, :] = field(x * size_y + y)
            if labels is not None:
                row = size_x * sensors + x
                ref[row : row + 1, :] = jnp.where(high, labels[x][size_y - 1 :, :], labels[x][0:1, :])
        if labels is None:
            ref[size_x * sensors :, :] = beyond


def put_lanes(packed, row, source, target, count):
    lanes = packed.shape[1]
    moved = pltpu.roll(row, (target - source) % lanes, 1)
    lane_index = lax.broadcasted_iota(jnp.int32, packed.shape, 1)
    return jnp.where((lane_index >= target) & (lane_index < target + count), moved, packed)


def pack_lines(dims, values, depth, low_shift):
    size_x, size_y, size_z = dims[1:]
    half = size_z // 2
    packed = jnp.zeros((size_y, size_z), jnp.float32)
    row_index = lax.broadcasted_iota(jnp.int32, packed.shape, 0)
    for x in range(size_x):
        line = 2 * (x * size_y + row_index)
        for p in range(depth):
            low, high = values[x]
            end = size_z - depth + p
            packed = jnp.where(lanes_equal(packed.shape, line + low_shift + p), low[:, p : p + 1], packed)
            packed = jnp.where(lanes_equal(packed.shape, line + half + p), high[:, end : end + 1], packed)
    return jnp.broadcast_to(jnp.sum(packed, axis=0, keepdims=True), (8, size_z))


def pack_rows(dims, rows_ref, depth, low_shift):
    sensors, size_x, size_y, size_z = dims
    half = size_z // 2
    assert 2 * size_x * size_y <= half
    packed = jnp.zeros((sensors, size_z), jnp.float32)
    for r in range(size_x * size_y):
        row = rows_ref[r * sensors : (r + 1) * sensors, :]
        packed = put_lanes(packed, row, 0, 2 * r + low_shift, depth)
        packed = put_lanes(packed, row, size_z - depth, half + 2 * r, depth)
    return packed


def split_refs(refs, counts):
    groups, start = [], 0
    for count in counts:
        groups.append(refs[start : start + count])
        start += count
    return groups


def pack_kernel(dims, counts, source_ref, label_ref, *refs):
    sensors, size_x, size_y, size_z = dims
    small_hbm, refs = refs[:4], refs[4:]
    (rows_ref, shifted_ref, table_ref), small_refs = refs[:3], refs[3:6]
    own_ref, refs = refs[6], refs[7:]
    face_refs = split_refs(refs[: sum(counts[:2])], counts[:2])
    staged_ref, label_vmem, level_ref, semaphores = refs[sum(counts[:2]) :]
    copies = [
        pltpu.make_async_copy(source_ref.at[:, x], staged_ref.at[x], semaphores.at[x])
        for x in range(size_x)
    ]
    moves = [(label_ref, label_vmem), *zip(small_hbm, (*small_refs, level_ref))]
    for k, move in enumerate(moves):
        copies.append(pltpu.make_async_copy(*move, semaphores.at[size_x + k]))
    for copy in copies:
        copy.start()
    for copy in copies[size_x:]:
        copy.wait()
    for level in range(level_ref.shape[0]):
        table_ref[level] = jnp.full(table_ref.shape[1:], level_ref[level], jnp.float32)
    shifted = [(label_vmem[x] + 1).astype(jnp.float32) for x in range(size_x)]
    for x in range(size_x):
        shifted_ref[x] = shifted[x]
    flat = staged_ref.reshape(size_x, sensors * size_y, size_z)
    for x in range(size_x):
        copies[x].wait()
        for y in range(size_y):
            r = x * size_y + y
            rows_ref[r * sensors : (r + 1) * sensors, :] = flat[x, pl.ds(y, sensors, stride=size_y), :]
    write_faces(dims, rows_ref, face_refs, labels=shifted)
    own_ref[0:sensors, :] = pack_rows(dims, rows_ref, 2, 0)
    own_ref[sensors:, :] = pack_lines(dims, [(plane, plane) for plane in shifted], 2, 0)


def prepare_kernel(
    size_z, folding, voxel_ref, owned_ref, level_ref, chosen_ref, owned_chosen_ref, table_ref
):
    table_ref[...] = level_ref[...]
    slots, voxels = chosen_ref.shape
    square = (slots, slots)
    diagonal = lanes_equal(square, lax.broadcasted_iota(jnp.int32, square, 0))
    voxel = jnp.where(diagonal, voxel_ref[...].astype(jnp.float32), 0.0)
    voxel = jnp.sum(voxel, axis=1, keepdims=True).astype(jnp.int32)
    voxel = jnp.broadcast_to(voxel, (slots, size_z))
    row = voxel // size_z
    lane_index = lax.broadcasted_iota(jnp.int32, (slots, size_z), 1)
    lane = one_hot(lane_index == voxel - row * size_z)
    row = row.astype(jnp.float32).astype(jnp.bfloat16)
    none = jnp.zeros_like(lane)
    for r in range(voxels // size_z):
        chosen_ref[:, r * size_z : (r + 1) * size_z] = jnp.where(row == r, lane, none)
    row_index = lax.broadcasted_iota(jnp.int32, (slots, owned_ref.shape[1]), 0)
    owned_chosen_ref[0:slots, :] = one_hot(row_index == owned_ref[...])
    slots_each, fold = folding
    if fold:
        part = slots_each // fold
        row_index = lax.broadcasted_iota(jnp.int32, (slots // fold, owned_ref.shape[1]), 0)
        slot_index = row_index // part * slots_each + row_index % part
        for k in range(fold):
            first = slots + k * (slots // fold)
            owned_chosen_ref[first : first + slots // fold, :] = one_hot(
                slot_index + k * part == owned_ref[...]
            )


def one_hot(condition):
    return condition.astype(jnp.float32).astype(jnp.bfloat16)


def tissue(shifted, table_ref):
    conductivity = jnp.zeros_like(shifted)
    for level in range(table_ref.shape[0]):
        value = table_ref[level] if shifted.shape == table_ref.shape[1:] else table_ref[level, 0:1, 0:1]
        conductivity = jnp.where(shifted == level + 1, value, conductivity)
    return conductivity, (shifted > 0).astype(jnp.float32)


def edge_weight(first, second):
    return 0.5 * (first[0] + second[0]) * first[1] * second[1]


def weights(dims, shifted_ref, table_ref, halo_refs, z_ref, weight_ref):
    sensors, size_x, size_y, size_z = dims
    flags = neighbour_flags()
    (x_low, x_high), (y_low, y_high) = halo_refs
    beyond = z_ref[sensors : sensors + 1, :]
    half = size_z // 2

    def beyond_end(x, first, flag):
        line = 2 * (x * size_y + row_index) + first
        picked = jnp.where(lanes_equal(row_index.shape, line), beyond, 0.0)
        return masked(jnp.sum(picked, axis=1, keepdims=True), flag)

    def masked(value, flag):
        return jnp.where(flag, value, 0.0)

    own = [shifted_ref[x] for x in range(size_x)]
    own_tissue = [tissue(plane, table_ref) for plane in own]
    x_rows = slice(size_y * sensors, size_y * (sensors + 1))
    below = tissue(masked(x_low[x_rows, :], flags[0][0]), table_ref)
    above = tissue(masked(x_high[x_rows, :], flags[0][1]), table_ref)
    planes = [below] + own_tissue + [above]
    across_x = [edge_weight(planes[i], planes[i + 1]) for i in range(size_x + 1)]
    row_index = lax.broadcasted_iota(jnp.int32, (size_y, size_z), 0)
    lane_index = lax.broadcasted_iota(jnp.int32, (size_y, size_z), 1)
    for x in range(size_x):
        y_row = size_x * sensors + x
        shifted = own[x]
        y_before = jnp.where(
            row_index == 0,
            masked(y_low[y_row : y_row + 1, :], flags[1][0]),
            pltpu.roll(shifted, 1, 0),
        )
        y_after = jnp.where(
            row_index == size_y - 1,
            masked(y_high[y_row : y_row + 1, :], flags[1][1]),
            pltpu.roll(shifted, size_y - 1, 0),
        )
        z_before = jnp.where(
            lane_index == 0,
            beyond_end(x, 1, flags[2][0]),
            pltpu.roll(shifted, 1, 1),
        )
        z_after = jnp.where(
            lane_index == size_z - 1,
            beyond_end(x, half, flags[2][1]),
            pltpu.roll(shifted, size_z - 1, 1),
        )
        six = [across_x[x], across_x[x + 1]]
        for beside in (y_before, y_after, z_before, z_after):
            six.append(edge_weight(own_tissue[x], tissue(beside, table_ref)))
        for k, weight in enumerate(six):
            weight_ref[k, x] = weight
        weight_ref[6, x] = mass_term + (six[0] + six[1]) + (six[2] + six[3]) + (six[4] + six[5])
        weight_ref[7, x] = 0.5 * own_tissue[x][0]


def around(dims, rows_ref, halo_refs, z_ref, r, flags=None):
    sensors, size_x, size_y, size_z = dims
    (x_low, x_high), (y_low, y_high) = halo_refs
    x, y = divmod(r, size_y)
    z_low = z_ref[0:sensors, 2 * r + 1 : 2 * r + 2]
    high_lane = size_z // 2 + 2 * r
    z_high = z_ref[0:sensors, high_lane : high_lane + 1]

    def keep(value, dim, end):
        return value if flags is None else jnp.where(flags[dim][end], value, 0.0)

    def row(index):
        return rows_ref[index * sensors : (index + 1) * sensors, :]

    def part(ref, index):
        return ref[index * sensors : (index + 1) * sensors, :]

    centre = row(r)
    x_before = row(r - size_y) if x > 0 else keep(part(x_low, y), 0, 0)
    x_after = row(r + size_y) if x < size_x - 1 else keep(part(x_high, y), 0, 1)
    y_before = row(r - 1) if y > 0 else keep(part(y_low, x), 1, 0)
    y_after = row(r + 1) if y < size_y - 1 else keep(part(y_high, x), 1, 1)
    lane_index = lax.broadcasted_iota(jnp.int32, centre.shape, 1)
    z_before = jnp.where(
        lane_index == 0, keep(z_low, 2, 0), pltpu.roll(centre, 1, 1)
    )
    z_after = jnp.where(
        lane_index == size_z - 1,
        keep(z_high, 2, 1),
        pltpu.roll(centre, size_z - 1, 1),
    )
    return centre, (x_before, x_after, y_before, y_after, z_before, z_after)


def combine(weight_ref, x, y, centre, beside):
    total = weight_ref[6, x, y : y + 1, :] * centre
    for k, value in enumerate(beside):
        total = total - weight_ref[k, x, y : y + 1, :] * value
    return total


def apply_kernel(dims, counts, rows_ref, shifted_ref, table_ref, *refs):
    sensors, size_x, size_y, size_z = dims
    message_refs, refs = refs[: sum(counts)], refs[sum(counts) :]
    weight_ref, end_ref, applied_ref, z_ref = refs[:4]
    face_refs = split_refs(refs[4 : 4 + sum(counts[:2])], counts[:2])
    halo_refs = sort_halos(message_refs, refs[4 + sum(counts[:2]) :], counts)
    z_ref[...] = sort_ends(message_refs[sum(counts[:2]) :])
    weights(dims, shifted_ref, table_ref, halo_refs, z_ref, weight_ref)
    for r in range(size_x * size_y):
        x, y = divmod(r, size_y)
        centre, beside = around(dims, rows_ref, halo_refs, z_ref, r)
        applied_ref[r * sensors : (r + 1) * sensors, :] = combine(weight_ref, x, y, centre, beside)
    write_faces(dims, applied_ref, face_refs, beyond=z_ref[...])
    lines = [(weight_ref[4, x], weight_ref[5, x]) for x in range(size_x)]
    outward = pack_lines(dims, lines, 1, 1)
    end_ref[...] = outward[0:1, :] * pack_rows(dims, applied_ref, 1, 1)


def halves(value):
    high = value.astype(jnp.bfloat16)
    return high, (value - high.astype(jnp.float32)).astype(jnp.bfloat16)


def local_twice(dims, rows_ref, weight_ref, r):
    sensors, size_x, size_y, size_z = dims
    x, y = divmod(r, size_y)

    def row(index):
        return rows_ref[index * sensors : (index + 1) * sensors, :]

    def weight(k):
        return weight_ref[k, x, y : y + 1, :]

    centre = row(r)
    lane_index = lax.broadcasted_iota(jnp.int32, centre.shape, 1)
    total = weight(6) * centre
    if x > 0:
        total = total - weight(0) * row(r - size_y)
    if x < size_x - 1:
        total = total - weight(1) * row(r + size_y)
    if y > 0:
        total = total - weight(2) * row(r - 1)
    if y < size_y - 1:
        total = total - weight(3) * row(r + 1)
    before = jnp.where(lane_index == 0, 0.0, pltpu.roll(centre, 1, 1))
    after = jnp.where(lane_index == size_z - 1, 0.0, pltpu.roll(centre, size_z - 1, 1))
    return total - weight(4) * before - weight(5) * after


def select_columns(dims, rows_ref, weight_ref, halo_refs, z_ref, chosen_ref, parts_ref):
    sensors, size_x, size_y, size_z = dims
    flags = neighbour_flags()
    width = 3 * sensors
    for r in range(size_x * size_y):
        x, y = divmod(r, size_y)
        span = slice(r * size_z, (r + 1) * size_z)
        scale = weight_ref[7, x, y : y + 1, :]
        _, beside = around(dims, rows_ref, halo_refs, z_ref, r, flags)
        for c in range(3):
            high, low = halves(scale * (beside[2 * c + 1] - beside[2 * c]))
            parts_ref[c * sensors : (c + 1) * sensors, span] = high
            parts_ref[width + c * sensors : width + (c + 1) * sensors, span] = low
    found = lax.dot_general(
        chosen_ref[...], parts_ref[...], last_with_last, preferred_element_type=jnp.float32
    )
    return found[:, :width] + found[:, width:]


def source_kernel(dims, counts, rows_ref, applied_ref, weight_ref, chosen_ref, z_ref, *refs):
    sensors, size_x, size_y, size_z = dims
    messages = sum(counts[:2])
    column_ref, sum_ref, parts_ref = refs[messages : messages + 3]
    halo_refs = sort_halos(refs[:messages], refs[messages + 3 :], counts)
    sums = [jnp.zeros((sensors, size_z), jnp.float32) for _ in range(4)]
    for r in range(size_x * size_y):
        source = rows_ref[r * sensors : (r + 1) * sensors, :]
        applied = applied_ref[r * sensors : (r + 1) * sensors, :]
        twice = local_twice(dims, applied_ref, weight_ref, r)
        for k, product in enumerate(
            (source * source, source * applied, applied * applied, applied * twice)
        ):
            sums[k] = sums[k] + product
    for k in range(4):
        sum_ref[k * sensors : (k + 1) * sensors, :] = sums[k]
    column_ref[...] = select_columns(
        dims, rows_ref, weight_ref, halo_refs, z_ref, chosen_ref, parts_ref
    )


def packed_beside(dims, beyond, own, along_x, along_y):
    sensors, size_x, size_y, size_z = dims
    half = size_z // 2
    lane_index = lax.broadcasted_iota(jnp.int32, beyond.shape, 1)
    in_half = lane_index % half
    row = in_half // 2 % size_y

    def moved(value, lanes):
        return pltpu.roll(value, lanes % size_z, 1)

    def either(condition, value, lanes, other, back):
        return jnp.where(condition, moved(value, lanes), moved(other, back))

    step, wrap = 2 * size_y, 2 * size_y * (size_x - 1)
    return (
        either(in_half >= step, beyond, step, along_x[0], -wrap),
        either(in_half < wrap, beyond, -step, along_x[1], wrap),
        either(row > 0, beyond, 2, along_y[0], -2 * (size_y - 1)),
        either(row < size_y - 1, beyond, -2, along_y[1], 2 * (size_y - 1)),
        either(lane_index < half, beyond, 1, beyond, -1),
        either(lane_index < half, own, 1, own, -1),
    )


def moment_kernel(
    dims, counts, applied_ref, weight_ref, sum_ref, end_ref, own_ref, z_ref, table_ref, *refs
):
    sensors, size_x, size_y, size_z = dims
    messages = sum(counts[:2])
    moment_ref, plane_ref = refs[messages : messages + 2]
    halo_refs = sort_halos(refs[:messages], refs[messages + 2 :], counts)
    (x_low, x_high), (y_low, y_high) = halo_refs
    flags = neighbour_flags()

    def forwarded(pair, dim, first, last):
        start = (size_y, size_x)[dim] * sensors
        return [
            jnp.where(flags[dim][end], ref[start + first : start + last, :], 0.0)
            for end, ref in enumerate(pair)
        ]

    def of_lines(first, last):
        return packed_beside(
            dims,
            z_ref[first:last, :],
            own_ref[first:last, :],
            forwarded(halo_refs[0], 0, first, last),
            forwarded(halo_refs[1], 1, first, last),
        )

    middle = tissue(z_ref[sensors:, :], table_ref)
    six = [
        edge_weight(middle, tissue(label, table_ref))
        for label in of_lines(sensors, z_ref.shape[0])
    ]
    total = mass_term + (six[0] + six[1]) + (six[2] + six[3]) + (six[4] + six[5])
    plane = total[0:1, :] * z_ref[0:sensors, :]
    for weight, value in zip(six, of_lines(0, sensors)):
        plane = plane - weight[0:1, :] * value
    plane_ref[...] = plane

    def part(ref, index):
        return ref[index * sensors : (index + 1) * sensors, :]

    def crossing(k, r, beside):
        x, y = divmod(r, size_y)
        return weight_ref[k, x, y : y + 1, :] * part(applied_ref, r) * beside

    outward = jnp.zeros((sensors, size_z), jnp.float32)
    for y in range(size_y):
        outward = outward + crossing(0, y, part(x_low, y))
        outward = outward + crossing(1, (size_x - 1) * size_y + y, part(x_high, y))
    for x in range(size_x):
        outward = outward + crossing(2, x * size_y, part(y_low, x))
        outward = outward + crossing(3, x * size_y + size_y - 1, part(y_high, x))
    outward = outward + end_ref[...] * plane
    last = part(sum_ref, 3) - outward
    moment_ref[...] = lax.dot_general(
        jnp.ones((8, size_z), jnp.float32),
        jnp.concatenate([sum_ref[0 : 3 * sensors, :], last], axis=0),
        last_with_last,
        precision=lax.Precision.HIGHEST,
        preferred_element_type=jnp.float32,
    )


def payload_rows(sensors, slots_each):
    whole, rest = divmod(6 * sensors, lane_tile)
    fold = lane_tile // rest if rest else 0
    assert not fold or (fold * rest == lane_tile and slots_each % fold == 0)
    rows = whole * slots_each + (slots_each // fold if fold else 0)
    return whole, rest, fold, rows, -(-4 * sensors // lane_tile)


def applied_kernel(
    dims, counts, slots_each, applied_ref, weight_ref, chosen_ref, source_column_ref, z_ref, *refs
):
    sensors, messages = dims[0], sum(counts[:2])
    column_ref, parts_ref = refs[messages : messages + 2]
    halo_refs = sort_halos(refs[:messages], refs[messages + 2 :], counts)
    applied_columns = select_columns(
        dims, applied_ref, weight_ref, halo_refs, z_ref, chosen_ref, parts_ref
    )
    columns = jnp.concatenate([source_column_ref[...], applied_columns], axis=1)
    whole, rest, fold, rows, moment_rows = payload_rows(sensors, slots_each)
    for owner in range(columns.shape[0] // slots_each):
        mine = slice(owner * slots_each, (owner + 1) * slots_each)
        at = owner * (rows + moment_rows)
        for tile in range(whole):
            column_ref[at : at + slots_each, :] = columns[mine, tile * lane_tile : (tile + 1) * lane_tile]
            at += slots_each
        if fold:
            part = slots_each // fold
            others = columns[mine, whole * lane_tile :]
            column_ref[at : at + part, :] = jnp.concatenate(
                [others[k * part : (k + 1) * part, :] for k in range(fold)], axis=1
            )
            at += part
        column_ref[at : at + moment_rows, :] = jnp.zeros((moment_rows, lane_tile), jnp.float32)


def owner_kernel(
    sensors,
    slots_each,
    received_ref,
    chosen_ref,
    data_ref,
    projection_hbm,
    gram_hbm,
    projection_ref,
    gram_ref,
    semaphores,
):
    whole, rest, fold, rows, moment_rows = payload_rows(sensors, slots_each)
    each = rows + moment_rows
    sources = received_ref.shape[0] // each
    slots = sources * slots_each

    def collected(start, count):
        return jnp.concatenate(
            [received_ref[k * each + start : k * each + start + count, :] for k in range(sources)],
            axis=0,
        )

    gathered = jnp.zeros((moment_rows, lane_tile), jnp.float32)
    for k in range(sources):
        gathered = gathered + received_ref[k * each + rows : (k + 1) * each, :]
    moments = []
    sensor_index = lax.broadcasted_iota(jnp.int32, (sensors, lane_tile), 0)
    lane_index = lax.broadcasted_iota(jnp.int32, (sensors, lane_tile), 1)
    for k in range(4):
        total = jnp.zeros((sensors, 1), jnp.float32)
        for row in range(moment_rows):
            here = lane_index + row * lane_tile == sensor_index + k * sensors
            picked = jnp.where(here, gathered[row : row + 1, :], 0.0)
            total = total + jnp.sum(picked, axis=1, keepdims=True)
        moments.append(total)
    moment_zero, moment_one, moment_two, moment_three = moments
    first_step = moment_zero / moment_one
    residue = first_step * first_step * moment_two - moment_zero
    growth = 1.0 + residue / moment_zero
    curvature = (
        growth * growth * moment_one
        - 2.0 * growth * first_step * moment_two
        + first_step * first_step * moment_three
    )
    second_step = residue / curvature
    source_coef = first_step + second_step * growth
    applied_coef = second_step * first_step
    contract = (((0,), (0,)), ((), ()))

    def selected(values, first):
        chosen = chosen_ref[first : first + values.shape[0], :]
        high, low = halves(values)
        return lax.dot_general(
            high, chosen, contract, preferred_element_type=jnp.float32
        ) + lax.dot_general(low, chosen, contract, preferred_element_type=jnp.float32)

    owned = [
        selected(collected(tile * slots_each, slots_each), 0) for tile in range(whole)
    ]
    if fold:
        folded = collected(whole * slots_each, slots_each // fold)
        others = jnp.zeros((rest, chosen_ref.shape[1]), jnp.float32)
        for k in range(fold):
            found = selected(folded, slots + k * (slots // fold))
            others = others + found[k * rest : (k + 1) * rest, :]
        owned.append(others)
    owned = jnp.concatenate(owned, axis=0)
    lead, copies = [], []
    for c in range(3):
        source_part = owned[c * sensors : (c + 1) * sensors, :]
        applied_part = owned[(3 + c) * sensors : (4 + c) * sensors, :]
        lead.append(source_coef * source_part - applied_coef * applied_part)
        projection_ref[c] = lax.dot_general(
            data_ref[...],
            lead[c],
            contract,
            precision=lax.Precision.HIGHEST,
            preferred_element_type=jnp.float32,
        )
        copies.append(
            pltpu.make_async_copy(projection_ref.at[c], projection_hbm.at[c], semaphores.at[c])
        )
        copies[c].start()
    for k, (first, second) in enumerate(entry_pairs):
        gram_ref[k : k + 1, :] = jnp.sum(lead[first] * lead[second], axis=0, keepdims=True)
    copies.append(pltpu.make_async_copy(gram_ref, gram_hbm, semaphores.at[3]))
    copies[3].start()
    for copy in copies:
        copy.wait()


def call(body, **arguments):
    return pl.pallas_call(
        body, compiler_params=pltpu.CompilerParams(vmem_limit_bytes=vmem_grant), **arguments
    )


def in_hbm(count):
    return [pl.BlockSpec(memory_space=pltpu.HBM)] * count


def held_in_hbm(*arrays):
    return [pltpu.with_memory_space_constraint(a, pltpu.HBM) for a in arrays]


def in_vmem(count):
    return [pl.BlockSpec(memory_space=pltpu.VMEM)] * count


def face_shapes(dims, counts, x_rows, y_rows):
    sensors, size_x, size_y, size_z = dims
    rows = (size_y * sensors + x_rows, size_x * sensors + y_rows)
    return [
        jax.ShapeDtypeStruct((row, size_z), jnp.float32)
        for row, count in zip(rows, counts)
        for _ in range(count)
    ]


def per_device(source_term, labels, conductivity_table, send_map, owner_slots, sensor_data):
    dims = source_term.shape
    sensors, size_x, size_y, size_z = dims
    rows_count = size_x * size_y
    counts = face_counts()
    messages = sum(counts[:2])
    owners = lax.axis_size("gx") * lax.axis_size("gy")
    slots = send_map.size
    slots_each = slots // owners
    _, _, fold, payload, moment_rows = payload_rows(sensors, slots_each)
    times = sensor_data.shape[1]
    positions = owner_slots.shape[0]

    voxels = rows_count * size_z

    def array(shape, dtype=jnp.float32):
        return jax.ShapeDtypeStruct(shape, dtype)

    parts = [pltpu.VMEM((6 * sensors, voxels), jnp.bfloat16)]
    field_shape = array((rows_count * sensors, size_z))
    ends_shape = array((sensors + 8, size_z))
    levels = conductivity_table.shape[0]
    small = (
        send_map.reshape(1, slots),
        owner_slots.reshape(1, positions),
        sensor_data,
        conductivity_table,
    )
    packed = call(
        functools.partial(pack_kernel, dims, counts),
        out_shape=[field_shape, array(labels.shape), array((levels, size_y, size_z))]
        + [array(value.shape, value.dtype) for value in small[:3]]
        + [ends_shape]
        + face_shapes(dims, counts, size_y, 8 * -(-size_x // 8)),
        in_specs=in_hbm(6),
        out_specs=in_vmem(7 + messages),
        scratch_shapes=[
            pltpu.VMEM((size_x, sensors, size_y, size_z), jnp.float32),
            pltpu.VMEM((size_x, size_y, size_z), jnp.int32),
            pltpu.SMEM((levels,), jnp.float32),
            pltpu.SemaphoreType.DMA((size_x + 5,)),
        ],
        name="pack",
    )(*held_in_hbm(source_term, labels, *small))
    rows, shifted, table, voxel, owned, data, own_ends, *faces = packed
    source_halos = exchange_all([*split_refs(faces, counts[:2]), [own_ends] * counts[2]])
    chosen, owned_chosen, table = call(
        functools.partial(prepare_kernel, size_z, (slots_each, fold)),
        out_shape=[
            array((slots, voxels), jnp.bfloat16),
            array((slots * (2 if fold else 1), positions), jnp.bfloat16),
            array(table.shape),
        ],
        in_specs=in_vmem(3),
        out_specs=in_vmem(3),
        name="prepare",
    )(voxel, owned, table)

    result = call(
        functools.partial(apply_kernel, dims, counts),
        out_shape=[array((8, size_x, size_y, size_z)), array((sensors, size_z)), field_shape]
        + [ends_shape]
        + face_shapes(dims, counts, sensors + 8, sensors + 8),
        in_specs=in_vmem(3 + messages + counts[2]),
        out_specs=in_vmem(4 + messages),
        scratch_shapes=held_halos(source_halos, counts),
        name="apply",
    )(rows, shifted, table, *source_halos)
    weight, ends, applied, beyond, *faces = result
    applied_halos = exchange_all(split_refs(faces, counts[:2]))

    source_columns, sums = call(
        functools.partial(source_kernel, dims, counts),
        out_shape=[array((slots, 3 * sensors)), array((4 * sensors, size_z))],
        in_specs=in_vmem(5 + messages),
        out_specs=in_vmem(2),
        scratch_shapes=parts + held_halos(source_halos, counts),
        name="source_columns",
    )(rows, applied, weight, chosen, beyond, *source_halos[:messages])
    moment, plane = call(
        functools.partial(moment_kernel, dims, counts),
        out_shape=[array((8, 4 * sensors)), array((sensors, size_z))],
        in_specs=in_vmem(7 + messages),
        out_specs=in_vmem(2),
        scratch_shapes=held_halos(applied_halos, counts),
        name="moments",
    )(applied, weight, sums, ends, own_ends, beyond, table, *applied_halos)
    moment = sum_over(moment, "gz")

    each = payload + moment_rows
    columns = call(
        functools.partial(applied_kernel, dims, counts, slots_each),
        out_shape=array((owners * each, lane_tile)),
        in_specs=in_vmem(5 + messages),
        out_specs=in_vmem(1)[0],
        scratch_shapes=parts + held_halos(applied_halos, counts),
        name="applied_columns",
    )(applied, weight, chosen, source_columns, plane, *applied_halos)
    place = lax.broadcasted_iota(jnp.int32, columns.shape, 0) % each
    stamp = jnp.pad(moment[0], (0, moment_rows * lane_tile - 4 * sensors)).reshape(-1, lane_tile)
    for row in range(moment_rows):
        columns = jnp.where(place == payload + row, stamp[row : row + 1], columns)
    received = lax.all_to_all(
        columns.reshape(owners, 1, each * lane_tile), ("gx", "gy"), 0, 0, tiled=True
    ).reshape(columns.shape)
    return call(
        functools.partial(owner_kernel, sensors, slots_each),
        out_shape=[array((3, times, positions)), array((6, positions))],
        in_specs=in_vmem(3),
        out_specs=in_hbm(2),
        scratch_shapes=[
            pltpu.VMEM((3, times, positions), jnp.float32),
            pltpu.VMEM((6, positions), jnp.float32),
            pltpu.SemaphoreType.DMA((4,)),
        ],
        name="owner",
    )(received, owned_chosen, data)


def solution(mesh):
    in_specs = (
        P(None, "gx", "gy", "gz"),
        P("gx", "gy", "gz"),
        P(),
        P("gx", "gy", "gz", None),
        P(("gx", "gy", "gz")),
        P(),
    )
    out_specs = (P(None, None, ("gx", "gy", "gz")), P(None, ("gx", "gy", "gz")))
    step = jax.shard_map(
        per_device, mesh=mesh, in_specs=in_specs, out_specs=out_specs, check_vma=False
    )
    return lambda *arguments: tuple(step(*arguments))
```
